32 devices in a mesh: gx: 4 (over z), gy: 4 (over y, x), gz: 2 (over core).
Axes of the slice: x: 2, y: 2, z: 4, core: 2. Of those that a mesh axis runs over, the one named last changes fastest.
Arguments:
- forcing: float32 [3, 64, 64, 256], P(None, 'gx', 'gy', 'gz'), may hold values from -6 to 6
- start_field: float32 [3, 64, 64, 256], P(None, 'gx', 'gy', 'gz'), may hold values from -6 to 6
- modulus: float32 [64, 64, 256], P('gx', 'gy', 'gz'), may hold values from 1 to 4
- corners: int32 [32, 3], P(('gx', 'gy', 'gz')), may hold values from 0 to 236, as said below
Outputs:
- displacement: float32 [3, 64, 64, 256], P(None, 'gx', 'gy', 'gz')
- new_modulus: float32 [64, 64, 256], P('gx', 'gy', 'gz')
The draws below stay inside these ranges and needn't reach their ends.
Inputs may be any that keep to these rules, and one draw needn't show every extreme that they name: `corners`: subzone i is handled by device i // 1 in row-major order over (gx, gy, gz). In each dimension its corner lies within lo - 5 to lo + B + 5 - 2 * 10, where lo and B are that device's first voxel and voxel count in that dimension, and the subzone lies inside the grid.
All inputs are finite; a program needn't handle non-finite values.
Results may differ from the reference program's by a relative error of at most 0.0003.
Values sent between devices are 32-bit elements; how exact they have to be, the bound alone decides.
A program may use at most 192 MiB of HBM per device.

```python
import math
import jax
import jax.numpy as jnp
from jax import lax

BX = 16
BY = 16
BZ = 128
SUB_DEV = 1
PC = 10
HALO = 6
FSWEEPS = 4
NX = 64
NY = 64
NZ = 256
NSUB = 32
N_GY = 4
N_GZ = 2


def draw_corners(key, part):
    number = jnp.arange(NSUB, dtype=jnp.int32)
    device = number // SUB_DEV
    brick_x = device // (N_GY * N_GZ)
    brick_y = device // N_GZ % N_GY
    brick_z = device % N_GZ
    lower = jnp.stack([brick_x * BX, brick_y * BY, brick_z * BZ], axis=1)
    counts = jnp.array([BX + 2 * HALO - 1 - 2 * PC, BY + 2 * HALO - 1 - 2 * PC, BZ + 2 * HALO - 1 - 2 * PC], jnp.int32)
    offsets = jax.random.randint(key, (NSUB, 3), jnp.zeros((1, 3), jnp.int32), counts[None, :])
    corner_raw = lower - HALO + 1 + offsets
    upper_limit = jnp.array([NX, NY, NZ], jnp.int32) - 2 * PC
    return jnp.clip(corner_raw, 0, upper_limit[None, :]).astype(jnp.int32)


def block_amplitude(key):
    cell_x = (NX + 3) // 4
    cell_y = (NY + 3) // 4
    cell_z = (NZ + 3) // 4
    exponent = jax.random.uniform(jax.random.fold_in(key, 11), (cell_x, cell_y, cell_z), jnp.float32, -4.0, 0.0)
    amplitude = jnp.exp(exponent)
    amplitude = jnp.repeat(jnp.repeat(jnp.repeat(amplitude, 4, axis=0), 4, axis=1), 4, axis=2)
    return amplitude[:NX, :NY, :NZ]


def modulated_field(key, draw_tag):
    amplitude = block_amplitude(key)
    inner_key = jax.random.fold_in(key, draw_tag)
    samples = jax.random.normal(inner_key, (3, NX, NY, NZ), jnp.float32)
    return jnp.clip(samples * amplitude[None], -6.0, 6.0).astype(jnp.float32)


def draw_forcing(key, part):
    return modulated_field(key, 21)


def draw_start_field(key, part):
    return modulated_field(key, 37)


def shard_levels(stream_key, extent, split, low, largest):
    factor_of, own = 1.0, jax.random.fold_in(stream_key, 6)
    for dim, shards_of in split:
        steps = jnp.exp(jax.random.uniform(jax.random.fold_in(own, dim), (shards_of,), jnp.float32, low / len(split), largest / len(split)))
        factor_of = factor_of * jnp.repeat(steps, extent[dim] // shards_of).reshape([-1 if axis == dim else 1 for axis in range(len(extent))])
    return factor_of


def setup_inputs(seed: int = 0) -> dict:
    arg_keys = jax.random.split(jax.random.key(seed), 5)
    forcing = draw_forcing(jax.random.fold_in(arg_keys[4], 71), 0)
    start_field = draw_start_field(jax.random.fold_in(arg_keys[4], 71), 0)
    modulus = jnp.clip(jnp.exp(math.log(4.0) - 1.3862944 * jax.random.uniform(arg_keys[2], (NX, NY, NZ), jnp.float32) ** shard_levels(arg_keys[2], (NX, NY, NZ), ((0, 4), (1, 4), (2, 2)), -0.2, 0.2)), 1.0, 4.0)
    corners = draw_corners(jax.random.fold_in(arg_keys[4], 71), 0)
    return dict(forcing=forcing, start_field=start_field, modulus=modulus, corners=corners)


MASS_TERM = 0.5
DAMPING = 0.1
EPSILON = 1e-06
DIRECTIONS = ((0, True), (0, False), (1, True), (1, False), (2, True), (2, False))

def neighbor(values, which_axis, upward):
    index_list = [slice(1, -1), slice(1, -1), slice(1, -1)]
    index_list[which_axis] = slice(2, None) if upward else slice(0, -2)
    return values[tuple([slice(None)] * (values.ndim - 3) + index_list)]

def center(values):
    return values[tuple([slice(None)] * (values.ndim - 3) + [slice(1, -1)] * 3)]

def relax_sweep(field_pad, modulus_pad, forcing_mid):
    middle = center(modulus_pad)
    numerator = forcing_mid
    denominator = MASS_TERM
    for which_axis, upward in DIRECTIONS:
        coupling = 0.5 * (middle + neighbor(modulus_pad, which_axis, upward))
        numerator = numerator + coupling * neighbor(field_pad, which_axis, upward)
        denominator = denominator + coupling
    return numerator / denominator

def block_sum(values, coarse):
    return values.reshape(values.shape[0], coarse, 2, coarse, 2, coarse, 2).sum(axis=(2, 4, 6))

def shift_coarse(values, offset):
    padded = jnp.pad(values, 1)
    coarse = values.shape[0]
    begin = (1 - offset[0], 1 - offset[1], 1 - offset[2])
    return lax.slice(padded, begin, (begin[0] + coarse, begin[1] + coarse, begin[2] + coarse))

def zone_update(field_rim, forcing_zone, modulus_rim):
    zone_span = forcing_zone.shape[-1]
    coarse = zone_span // 2
    params = coarse ** 3
    field_mid = center(field_rim)
    modulus_mid = center(modulus_rim)
    applied = MASS_TERM * field_mid
    laplace = jnp.zeros_like(field_mid)
    face_flows = []
    for which_axis, upward in DIRECTIONS:
        field_next = neighbor(field_rim, which_axis, upward)
        modulus_next = neighbor(modulus_rim, which_axis, upward)
        change = field_mid - field_next
        applied = applied + 0.5 * (modulus_mid + modulus_next) * change
        laplace = laplace + change
        face_flows.append(-0.5 * modulus_next * change)
    coarse_resid = block_sum(forcing_zone - applied, coarse)
    diagonal = block_sum(-0.5 * modulus_mid * laplace, coarse)
    position = jnp.arange(coarse)
    columns = {}
    for (which_axis, upward), face_flow in zip(DIRECTIONS, face_flows):
        blocks = face_flow.reshape(3, coarse, 2, coarse, 2, coarse, 2)
        inner_pos = 0 if upward else 1
        same_part = lax.index_in_dim(blocks, inner_pos, 2 + 2 * which_axis, keepdims=True).sum(axis=(2, 4, 6))
        cross_part = lax.index_in_dim(blocks, 1 - inner_pos, 2 + 2 * which_axis, keepdims=True).sum(axis=(2, 4, 6))
        diagonal = diagonal + same_part
        in_range = position < coarse - 1 if upward else position > 0
        shape_list = [1, 1, 1]
        shape_list[which_axis] = coarse
        in_range = in_range.reshape(shape_list)
        step_list = [0, 0, 0]
        step_list[which_axis] = 1 if upward else -1
        columns[tuple(step_list)] = jnp.where(in_range, cross_part, 0.0)
    columns[0, 0, 0] = diagonal
    offset_list = list(columns.keys())
    gradient = jnp.zeros((coarse, coarse, coarse), jnp.float32)
    band_sums = {}
    for offset_one in offset_list:
        gradient = gradient + shift_coarse(jnp.sum(columns[offset_one] * coarse_resid, axis=0), offset_one)
        for offset_two in offset_list:
            band_key = (offset_two[0] - offset_one[0], offset_two[1] - offset_one[1], offset_two[2] - offset_one[2])
            term_value = shift_coarse(jnp.sum(columns[offset_one] * columns[offset_two], axis=0), offset_one)
            if band_key in band_sums:
                band_sums[band_key] = band_sums[band_key] + term_value
            else:
                band_sums[band_key] = term_value
    base_rows = jnp.arange(params, dtype=jnp.int32)
    row_parts = []
    col_parts = []
    value_parts = []
    for band_key, band_value in band_sums.items():
        linear = band_key[0] * coarse * coarse + band_key[1] * coarse + band_key[2]
        target = base_rows + linear
        target = jnp.where((target >= 0) & (target < params), target, params).astype(jnp.int32)
        row_parts.append(base_rows)
        col_parts.append(target)
        value_parts.append(band_value.reshape(params))
    hessian = jnp.zeros((params, params), jnp.float32).at[jnp.concatenate(row_parts), jnp.concatenate(col_parts)].add(jnp.concatenate(value_parts), mode='drop')
    ridge = DAMPING * jnp.sum(band_sums[0, 0, 0]) / params + EPSILON
    hessian = hessian + ridge * jnp.eye(params, dtype=jnp.float32)
    factor = jnp.linalg.cholesky(hessian)
    right_hand = gradient.reshape(params, 1)
    middle_sol = lax.linalg.triangular_solve(factor, right_hand, left_side=True, lower=True)
    solution = lax.linalg.triangular_solve(factor, middle_sol, left_side=True, lower=True, transpose_a=True)
    update = -solution.reshape(coarse, coarse, coarse)
    update = jnp.repeat(jnp.repeat(jnp.repeat(update, 2, axis=0), 2, axis=1), 2, axis=2)
    ramp_curve = jnp.sin(math.pi * (jnp.arange(zone_span, dtype=jnp.float32) + 0.5) / zone_span)
    taper_weight = ramp_curve[:, None, None] * ramp_curve[None, :, None] * ramp_curve[None, None, :]
    return taper_weight * modulus_mid * update

def reference(forcing, start_field, modulus, corners):
    zone_span = 2 * PC
    field = start_field
    modulus_pad = jnp.pad(modulus, 1)
    for sweep_count in range(FSWEEPS):
        field = relax_sweep(jnp.pad(field, ((0, 0), (1, 1), (1, 1), (1, 1))), modulus_pad, forcing)
    field_pad = jnp.pad(field, ((0, 0), (1, 1), (1, 1), (1, 1)))
    anchor = jnp.zeros((), jnp.int32)

    def one_zone(corner):
        corner = corner.astype(jnp.int32)
        field_rim = lax.dynamic_slice(field_pad, (anchor, corner[0], corner[1], corner[2]), (3, zone_span + 2, zone_span + 2, zone_span + 2))
        modulus_rim = lax.dynamic_slice(modulus_pad, (corner[0], corner[1], corner[2]), (zone_span + 2, zone_span + 2, zone_span + 2))
        forcing_zone = lax.dynamic_slice(forcing, (anchor, corner[0], corner[1], corner[2]), (3, zone_span, zone_span, zone_span))
        return zone_update(field_rim, forcing_zone, modulus_rim)
    pieces = lax.map(one_zone, corners)

    def add_piece(number, total):
        corner = corners[number].astype(jnp.int32)
        begin = (corner[0], corner[1], corner[2])
        current = lax.dynamic_slice(total, begin, (zone_span, zone_span, zone_span))
        return lax.dynamic_update_slice(total, current + pieces[number], begin)
    total = lax.fori_loop(0, corners.shape[0], add_piece, jnp.zeros(modulus.shape, jnp.float32))
    return (field, modulus + total)
```

```python
import functools
import math

import jax
import jax.numpy as jnp
from jax import lax
from jax.experimental import pallas as pl
from jax.experimental.pallas import tpu as pltpu
from jax.sharding import PartitionSpec as P

PC = 10
HALO = 6
FSWEEPS = 4


MASS_TERM = 0.5
DAMPING = 0.1
EPSILON = 1e-06
HIGHEST = lax.Precision.HIGHEST
PANEL = 2
F32 = jnp.float32


def dot(a, b, contract):
    return lax.dot_general(
        a, b, ((contract[:1], contract[1:]), ((), ())), precision=HIGHEST, preferred_element_type=F32
    )


def roll(values, shift, axis):
    return pltpu.roll(values, shift % values.shape[axis], axis)


def iota(shape, axis):
    return lax.broadcasted_iota(jnp.int32, shape, axis)


MESH_ID = pl.DeviceIdType.MESH
AXES = ("gx", "gy", "gz")
AROUND = tuple((dx, dy) for dx in (-1, 0, 1) for dy in (-1, 0, 1) if (dx, dy) != (0, 0))
FACES = ((-1, 0, 0), (1, 0, 0), (0, -1, 0), (0, 1, 0), (0, 0, -1), (0, 0, 1))


class Place:
    def __init__(self, counts):
        self.counts = counts
        self.here = [lax.axis_index(name) for name in AXES]

    def exists(self, step):
        inside = None
        for at, count, move in zip(self.here, self.counts, step):
            if move:
                test = at + move < count if move > 0 else at + move >= 0
                inside = test if inside is None else inside & test
        return inside

    def device(self, step):
        return tuple(at + move for at, move in zip(self.here, step))

    def peer(self, turn):
        return self.here[:2] + [lax.rem(self.here[2] + turn, self.counts[2])]

    def greet(self):
        barrier = pltpu.get_barrier_semaphore()
        total = self.counts[2] - 1
        for dx, dy in AROUND:
            step = (dx, dy, 0)

            @pl.when(self.exists(step))
            def _():
                pl.semaphore_signal(
                    barrier, inc=1, device_id=self.device(step), device_id_type=MESH_ID
                )

            total = total + self.exists(step).astype(jnp.int32)
        for turn in range(1, self.counts[2]):
            pl.semaphore_signal(
                barrier, inc=1, device_id=tuple(self.peer(turn)), device_id_type=MESH_ID
            )
        pl.semaphore_wait(barrier, total)


def opposite(step):
    return tuple(-move for move in step)


class Message:
    def __init__(self, place, step, source, target, send, recv):
        self.place, self.step = place, step
        self.copy = pltpu.make_async_remote_copy(
            src_ref=source,
            dst_ref=target,
            send_sem=send,
            recv_sem=recv,
            device_id=place.device(step),
            device_id_type=MESH_ID,
        )

    def start(self):
        pl.when(self.place.exists(self.step))(self.copy.start)

    def sent(self):
        pl.when(self.place.exists(self.step))(self.copy.wait_send)

    def arrived(self):
        pl.when(self.place.exists(opposite(self.step)))(self.copy.wait_recv)


def edge_span(move, size, margin):
    if move > 0:
        return slice(size, size + margin), slice(0, margin)
    if move < 0:
        return slice(margin, 2 * margin), slice(margin + size, 2 * margin + size)
    return slice(margin, margin + size), slice(margin, margin + size)


def spread_messages(place, brick, margins, ref, lanes, send, recv):
    messages = []
    for n, (dx, dy) in enumerate(AROUND):
        from_x, to_x = edge_span(dx, brick[0], margins[0])
        from_y, to_y = edge_span(dy, brick[1], margins[1])
        messages.append(
            Message(
                place,
                (dx, dy, 0),
                ref.at[:, from_x, from_y, lanes],
                ref.at[:, to_x, to_y, lanes],
                send.at[n],
                recv.at[n],
            )
        )
    return messages


def peer_copies(place, ref, lanes, send, recv):
    return [
        pltpu.make_async_remote_copy(
            src_ref=ref.at[:, :, :, lanes],
            dst_ref=ref.at[:, :, :, lanes],
            send_sem=send.at[turn - 1],
            recv_sem=recv.at[turn - 1],
            device_id=tuple(place.peer(turn)),
            device_id_type=MESH_ID,
        )
        for turn in range(1, place.counts[2])
    ]


def clear_outside(place, brick, margins, refs, lanes):
    for dx, dy in AROUND:
        _, to_x = edge_span(-dx, brick[0], margins[0])
        _, to_y = edge_span(-dy, brick[1], margins[1])

        @pl.when(jnp.logical_not(place.exists((dx, dy, 0))))
        def _():
            for ref in refs:
                for k in range(ref.shape[0]):
                    shape = (to_x.stop - to_x.start, to_y.stop - to_y.start, brick[2])
                    ref[k, to_x, to_y, lanes] = jnp.zeros(shape, F32)


def sweep_kernel(counts, brick, margins, forcing, start, modulus, zone_u, zone_w, *scratch):
    fields, rows_in, rows_out, sides = scratch[0:4], scratch[4], scratch[5], scratch[6:10]
    coupling, inverse = scratch[10:12]
    face_send, face_recv, bulk_send, bulk_recv, peer_send, peer_recv = scratch[12:]
    place = Place(counts)
    bx, by, bz = brick
    hx, hy = margins
    lanes = pl.ds(pl.multiple_of(place.here[2] * bz, bz), bz)
    row = iota((by, bz), 0)
    lane = iota((by, bz), 1)

    def stage(x, _):
        for k in range(3):
            u = start[k, x]
            fields[0][k, x + 1] = u
            rows_out[0, 0, k, pl.ds(x, 1), :] = u[:1]
            rows_out[0, 1, k, pl.ds(x, 1), :] = u[by - 1 :]
            zone_w[k, hx + x, hy : hy + by, lanes] = forcing[k, x]
        m = modulus[x]
        fields[0][3, x + 1] = m
        rows_out[0, 0, 3, pl.ds(x, 1), :] = m[:1]
        rows_out[0, 1, 3, pl.ds(x, 1), :] = m[by - 1 :]
        zone_w[3, hx + x, hy : hy + by, lanes] = m
        return 0

    lax.fori_loop(0, bx, stage, 0)

    def faces(sweep):
        channels = 4 if sweep == 0 else 3
        field = fields[sweep]
        messages = []
        for n, step in enumerate(FACES):
            dx, dy, dz = step
            if dx:
                source = field.at[:, bx if dx > 0 else 1]
                target = field.at[:, 0 if dx > 0 else bx + 1]
            elif dy:
                source = rows_out.at[sweep, 1 if dy > 0 else 0, :channels]
                target = rows_in.at[sweep, 0 if dy > 0 else 1, :channels]
            else:
                source = field.at[:, 1 : bx + 1]
                target = sides[sweep].at[0 if dz > 0 else 1]
            at = (sweep, n)
            messages.append(
                Message(place, step, source, target, face_send.at[at], face_recv.at[at])
            )
        return messages

    clear_outside(place, brick, margins, (zone_u, zone_w), lanes)
    for n, (dx, dy, dz) in enumerate(FACES):

        @pl.when(jnp.logical_not(place.exists((dx, dy, dz))))
        def _():
            for sweep in range(FSWEEPS):
                if dx:
                    plane = 0 if dx < 0 else bx + 1
                    for k in range(fields[sweep].shape[0]):
                        fields[sweep][k, plane] = jnp.zeros((by, bz), F32)
                elif dy:
                    for k in range(4):
                        rows_in[sweep, 0 if dy < 0 else 1, k] = jnp.zeros((bx, bz), F32)
                else:
                    for k in range(sides[sweep].shape[1]):
                        blank = jnp.zeros((bx, by, bz), F32)
                        sides[sweep][0 if dz < 0 else 1, k] = blank

    place.greet()
    messages = faces(0)
    pending = list(messages)
    for message in messages:
        message.start()
    bulk = spread_messages(
        place, brick, margins, zone_w, lanes, bulk_send.at[0], bulk_recv.at[0]
    )
    for message in bulk:
        message.start()

    def around(sweep, k, x, u):
        low, high = rows_in[sweep, 0, k, pl.ds(x, 1), :], rows_in[sweep, 1, k, pl.ds(x, 1), :]
        y_up = jnp.where(row == by - 1, jnp.broadcast_to(high, u.shape), roll(u, -1, 0))
        y_down = jnp.where(row == 0, jnp.broadcast_to(low, u.shape), roll(u, 1, 0))
        below, above = sides[sweep][0, k, x], sides[sweep][1, k, x]
        z_up = jnp.where(lane == bz - 1, roll(above, -1, 1), roll(u, -1, 1))
        z_down = jnp.where(lane == 0, roll(below, 1, 1), roll(u, 1, 1))
        field = fields[sweep]
        return field[k, x + 2], field[k, x], y_up, y_down, z_up, z_down

    def couple(x, _):
        m = fields[0][3, x + 1]
        below = MASS_TERM
        for n, other in enumerate(around(0, 3, x, m)):
            face = 0.5 * (m + other)
            coupling[n, x] = face
            below = below + face
        inverse[x] = 1.0 / below
        return 0

    for sweep in range(FSWEEPS):
        for message in messages:
            message.arrived()
        if sweep == 0:
            lax.fori_loop(0, bx, couple, 0)

        def relax(x, _, sweep=sweep):
            weights = [coupling[n, x] for n in range(6)]
            scale = inverse[x]
            for k in range(3):
                u = fields[sweep][k, x + 1]
                total = forcing[k, x]
                for weight, other in zip(weights, around(sweep, k, x, u)):
                    total = total + weight * other
                total = total * scale
                if sweep < FSWEEPS - 1:
                    fields[sweep + 1][k, x + 1] = total
                    rows_out[sweep + 1, 0, k, pl.ds(x, 1), :] = total[:1]
                    rows_out[sweep + 1, 1, k, pl.ds(x, 1), :] = total[by - 1 :]
                else:
                    zone_u[k, hx + x, hy : hy + by, lanes] = total
            return 0

        lax.fori_loop(0, bx, relax, 0)
        if sweep < FSWEEPS - 1:
            messages = faces(sweep + 1)
            pending += messages
            for message in messages:
                message.start()
    last = spread_messages(
        place, brick, margins, zone_u, lanes, bulk_send.at[1], bulk_recv.at[1]
    )
    for message in last:
        message.start()
    for message in bulk:
        message.arrived()
    copies = peer_copies(place, zone_w, lanes, peer_send.at[0], peer_recv.at[0])
    for copy in copies:
        copy.start()
    for message in last:
        message.arrived()
    more = peer_copies(place, zone_u, lanes, peer_send.at[1], peer_recv.at[1])
    for copy in more:
        copy.start()
    for message in pending + bulk + last:
        message.sent()
    for copy in copies + more:
        copy.wait()


def gather_kernel(counts, brick, margins, added, modulus, out, total, from_peer, *scratch):
    from_x, from_y, from_xy, send, recv, peer_send, peer_recv = scratch
    place = Place(counts)
    bx, by, bz = brick
    hx, hy = margins

    def part(turn):
        at = lax.rem(place.here[2] + turn, counts[2])
        return pl.ds(pl.multiple_of(at * bz, bz), bz)

    targets = {}
    for n, (dx, dy) in enumerate(AROUND):
        if dy == 0:
            targets[n] = from_x.at[(dx + 1) // 2]
        elif dx == 0:
            targets[n] = from_y.at[(dy + 1) // 2]
        else:
            targets[n] = from_xy.at[dx + 1 + (dy + 1) // 2]

        @pl.when(jnp.logical_not(place.exists((-dx, -dy, 0))))
        def _():
            targets[n][...] = jnp.zeros(targets[n].shape, F32)

    place.greet()
    copies = [
        pltpu.make_async_remote_copy(
            src_ref=added.at[:, :, part(turn)],
            dst_ref=from_peer.at[turn - 1],
            send_sem=peer_send.at[turn - 1],
            recv_sem=peer_recv.at[turn - 1],
            device_id=tuple(place.peer(turn)),
            device_id_type=MESH_ID,
        )
        for turn in range(1, counts[2])
    ]
    for copy in copies:
        copy.start()
    for copy in copies:
        copy.wait_recv()

    def collect(x, _):
        value = added[x, :, part(0)]
        for turn in range(1, counts[2]):
            value = value + from_peer[turn - 1, x]
        total[x] = value
        return 0

    lax.fori_loop(0, total.shape[0], collect, 0)
    messages = []
    for n, (dx, dy) in enumerate(AROUND):
        _, at_x = edge_span(-dx, bx, hx)
        _, at_y = edge_span(-dy, by, hy)
        messages.append(
            Message(place, (dx, dy, 0), total.at[at_x, at_y], targets[n], send.at[n], recv.at[n])
        )
    for message in messages:
        message.start()

    def centre(x, _):
        out[x] = modulus[x] + total[hx + x, hy : hy + by, :]
        return 0

    lax.fori_loop(0, bx, centre, 0)
    for message in messages:
        message.arrived()
    for n, (dx, dy) in enumerate(AROUND):
        to_x, _ = edge_span(-dx, bx, hx)
        to_y, _ = edge_span(-dy, by, hy)
        out[to_x.start - hx : to_x.stop - hx, to_y.start - hy : to_y.stop - hy, :] += targets[n][...]
    for message in messages:
        message.sent()
    for copy in copies:
        copy.wait_send()


FIELDS = 8


def coarse_fields(zone_u, zone_f, zone_m, temp, fields):
    rows = zone_m.shape[1]
    first_y = iota((rows, 128), 0) % 2 == 1
    first_z = iota((rows, 128), 1) % 2 == 1
    rank = iota((PC, 128), 0)
    lane = iota((PC, 128), 1)
    for x in range(PC):
        for k in range(3):
            sums = [None] * FIELDS

            def put(number, value):
                sums[number] = value if sums[number] is None else sums[number] + value

            for a in range(2):
                at = 2 * x + 1 + a
                u, m = zone_u[k, at], zone_m[at]
                applied = MASS_TERM * u
                laplace = jnp.zeros_like(u)
                for number, (axis, step) in enumerate(
                    ((0, 1), (0, -1), (1, 1), (1, -1), (2, 1), (2, -1))
                ):
                    if axis == 0:
                        u_next, m_next = zone_u[k, at + step], zone_m[at + step]
                    else:
                        u_next, m_next = roll(u, -step, axis - 1), roll(m, -step, axis - 1)
                    change = u - u_next
                    applied = applied + 0.5 * (m + m_next) * change
                    laplace = laplace + change
                    flow = -0.5 * m_next * change
                    if axis == 0:
                        same = (a == 0) == (step == 1)
                        put(0 if same else 1 + number, flow)
                    else:
                        first = first_y if axis == 1 else first_z
                        near = first if step == 1 else ~first
                        put(0, jnp.where(near, flow, 0.0))
                        put(1 + number, jnp.where(near, 0.0, flow))
                put(0, -0.5 * m * laplace)
                put(7, zone_f[k, at] - applied)
            for number in range(FIELDS):
                slot = temp.at[k * FIELDS + number]
                slot[...] = sums[number]
                pair = slot[pl.ds(1, PC, stride=2), :] + slot[pl.ds(2, PC, stride=2), :]
                pair = pair + roll(pair, -1, 1)
                keep = (lane % 2 == 1) & (lane < 2 * PC)
                if number == 1 and x == PC - 1 or number == 2 and x == 0:
                    keep = jnp.zeros_like(keep)
                if number == 3:
                    keep = keep & (rank < PC - 1)
                if number == 4:
                    keep = keep & (rank > 0)
                if number == 5:
                    keep = keep & (lane < 2 * PC - 2)
                if number == 6:
                    keep = keep & (lane > 1)
                fields[k * FIELDS + number, x * PC : (x + 1) * PC, :] = jnp.where(keep, pair, 0.0)


def assemble(fields, strip, mat, side):
    size = fields.shape[1]
    gap = iota((size, 128), 1) - iota((size, 128), 0)
    mat[...] = jnp.zeros_like(mat)
    side[...] = jnp.zeros_like(side)
    for c in range(2):
        for t in range(PC // 2):
            z = t if c == 0 else PC - 1 - t
            for k in range(3):
                def column(number):
                    value = fields[k * FIELDS + number, :, 2 * z + 1 : 2 * z + 2]
                    return jnp.broadcast_to(value, (size, 128))

                part = slice(k * size, (k + 1) * size)
                ahead, behind = (5, 6) if c == 0 else (6, 5)
                strip[part, 0:128] = jnp.where(gap == 0, column(behind), 0.0)
                inner = jnp.where(gap == 0, column(0), 0.0)
                for number, offset in ((1, PC), (2, -PC), (3, 1), (4, -1)):
                    inner = jnp.where(gap == offset, column(number), inner)
                strip[part, 128:256] = inner
                strip[part, 256:384] = jnp.where(gap == 0, column(ahead), 0.0)
                strip[part, 384:512] = column(7)
            product = dot(strip[:, :384], strip[...], (0, 0))
            for i in range(3):
                at = t - 1 + i
                if at < 0:
                    continue
                rows = slice(128 * i, 128 * (i + 1))
                mat[c, at] += product[rows, 128 * i : 128 * (i + 1)]
                for j in range(i + 1, 3):
                    place = slice(128 * (j - i - 1), 128 * (j - i))
                    side[c, at, :, place] += product[rows, 128 * j : 128 * (j + 1)]
                side[c, at, :, 256:384] += product[rows, 384:512]


def inverted(blocks, count):
    row_at = iota(blocks[0].shape, 0)
    lane_at = iota((1, blocks[0].shape[1]), 1)
    shape = blocks[0].shape
    for first in range(0, count, PANEL):
        pivots = range(first, min(first + PANEL, count))
        states = []
        for block in blocks:
            columns = [jnp.broadcast_to(block[:, j : j + 1], shape) for j in pivots]
            states.append([columns, [block[j : j + 1, :] for j in pivots], block])
        for i, j in enumerate(pivots):
            for state in states:
                columns, rows, block = state
                pivot = 1.0 / columns[i][j : j + 1, :]
                row = jnp.where(lane_at == j, pivot, rows[i] * pivot)
                column = jnp.where(row_at == j, -1.0, columns[i])
                for n in range(i + 1, len(columns)):
                    crossing = columns[n][j : j + 1, :] * pivot
                    rows[n] = jnp.where(lane_at == j, 0.0, rows[n])
                    rows[n] = rows[n] - columns[i][pivots[n] : pivots[n] + 1, :] * row
                    columns[n] = jnp.where(row_at == j, 0.0, columns[n]) - column * crossing
                clear = (row_at == j) | (lane_at == j)
                state[2] = jnp.where(clear, 0.0, block) - column * row
        blocks = [state[2] for state in states]
    return blocks


def eliminate(t, chains, size, ridge, mat, side, solved):
    params = PC * PC
    diagonal = (iota((size, 128), 0) == iota((size, 128), 1)) & (iota((size, 128), 0) < params)
    blocks = [mat[c, t, :size, :] + jnp.where(diagonal, ridge, 0.0) for c in chains]
    for c, inverse in zip(chains, inverted(blocks, params)):
        right = side[c, t]
        w = dot(inverse, right, (1, 0))
        solved[c, t] = w
        schur = dot(right[:size, :256], w, (0, 0))
        mat[c, t + 1] -= schur[:128, :128]
        side[c, t + 1, :, 0:128] -= schur[:128, 128:256]
        side[c, t + 1, :, 256:384] -= schur[:128, 256:384]
        mat[c, t + 2] -= schur[128:, 128:256]
        side[c, t + 2, :, 256:384] -= schur[128:, 256:384]


def solve_zone(fields, mat, side, solved, answer):
    size = fields.shape[1]
    squares = jnp.zeros((size, 128), F32)
    for number in range(3 * FIELDS):
        if number % FIELDS < FIELDS - 1:
            squares = squares + fields[number] * fields[number]
    trace = jnp.sum(jnp.sum(squares, axis=0, keepdims=True), axis=1, keepdims=True)
    ridge = DAMPING * trace / PC**3 + EPSILON
    meet = PC // 2 - 1

    def both(t, _):
        eliminate(t, (0, 1), size, ridge, mat, side, solved)
        return 0

    lax.fori_loop(0, meet, both, 0)
    mat[0, meet] += mat[1, meet + 1]
    mat[0, meet + 1] += mat[1, meet]
    side[0, meet, :, 0:128] += side[1, meet, :, 0:128].T
    side[0, meet, :, 256:384] += side[1, meet + 1, :, 256:384]
    side[0, meet + 1, :, 256:384] += side[1, meet, :, 256:384]

    def single(t, _):
        eliminate(t, (0,), size, ridge, mat, side, solved)
        return 0

    lax.fori_loop(meet, meet + 2, single, 0)
    answer[...] = jnp.zeros_like(answer)

    def back(t, c):
        value = solved[c, t, :, 256:384]
        value = value - dot(solved[c, t, :, 0:128], answer[c, t + 1], (1, 0))
        value = value - dot(solved[c, t, :, 128:256], answer[c, t + 2], (1, 0))
        answer[c, t, :size, :] = value

    answer[0, meet + 1, :size, :] = solved[0, meet + 1, :, 256:384]
    value = solved[0, meet, :, 256:384]
    answer[0, meet, :size, :] = value - dot(solved[0, meet, :, 0:128], answer[0, meet + 1], (1, 0))
    answer[1, meet] = answer[0, meet + 1]
    answer[1, meet + 1] = answer[0, meet]
    for t in range(meet - 1, -1, -1):
        for c in range(2):
            back(t, c)


def cut_zone(begin, depth, zone_all_u, zone_all_w, zone_u, zone_f, zone_m):
    count, rows = zone_m.shape[:2]
    whole_rows, whole_lanes = zone_all_u.shape[-2:]
    shift = lax.rem(whole_lanes - begin[2], whole_lanes)
    shift_y = lax.rem(whole_rows - begin[1], whole_rows)
    z = begin[2] + iota((rows, 128), 1)
    inside = (z >= 0) & (z < depth)

    def cut(x, _):
        def take(ref, k):
            plane = pltpu.roll(ref[k, begin[0] + x], shift, 1)[:, :128]
            return jnp.where(inside, pltpu.roll(plane, shift_y, 0)[:rows], 0.0)

        for k in range(3):
            zone_u[k, x] = take(zone_all_u, k)
            zone_f[k, x] = take(zone_all_w, k)
        zone_m[x] = take(zone_all_w, 3)
        return 0

    lax.fori_loop(0, count, cut, 0)


def place_zone(begin, zone_m, answer, spread, temp, added):
    rows = zone_m.shape[1]
    span = 2 * PC
    lane = iota((128, 128), 1)
    update = jnp.zeros((128, 128), F32)
    for z in range(PC):
        value = answer[0, z] if z < PC // 2 else answer[1, PC - 1 - z]
        update = jnp.where((lane == 2 * z + 1) | (lane == 2 * z + 2), -value, update)
    spread[...] = update

    def ramp(position):
        value = jnp.sin(math.pi * (position.astype(F32) - 0.5) / span)
        return jnp.where((position >= 1) & (position <= span), value, 0.0)

    weight = ramp(iota((rows, 128), 0)) * ramp(iota((rows, 128), 1))
    temp[0] = jnp.zeros_like(weight)
    shift = lax.rem(begin[2] + added.shape[2], added.shape[2])
    for x in range(PC):
        part = spread[x * PC : (x + 1) * PC, :]
        temp[0, pl.ds(1, PC, stride=2), :] = part
        temp[0, pl.ds(2, PC, stride=2), :] = part
        value = weight * temp[0]
        for a in range(2):
            at = 2 * x + 1 + a
            plane = value * math.sin(math.pi * (at - 0.5) / span) * zone_m[at]
            plane = jnp.pad(plane, ((0, added.shape[1] - rows), (0, 0)))
            plane = pltpu.roll(plane, begin[1], 0)
            plane = jnp.pad(plane, ((0, 0), (0, added.shape[2] - 128)))
            added[begin[0] + at] += pltpu.roll(plane, shift, 1)


def zone_kernel(counts, brick, margins, corners, zone_all_u, zone_all_w, field_out, added, *scratch):
    zone_u, zone_f, zone_m = scratch[:3]
    temp, fields, strip, mat, side, solved, answer, spread = scratch[3:]
    bx, by, bz = brick
    hx, hy = margins
    here = [lax.axis_index(name) for name in AXES]
    lanes = pl.ds(pl.multiple_of(here[2] * bz, bz), bz)
    for k in range(3):
        field_out[k] = zone_all_u[k, hx : hx + bx, hy : hy + by, lanes]
    added[...] = jnp.zeros_like(added)
    for number in range(corners.shape[0]):
        begin = [
            corners[number, 0] - here[0] * bx + hx - 1,
            corners[number, 1] - here[1] * by + hy - 1,
            corners[number, 2] - 1,
        ]
        cut_zone(begin, counts[2] * bz, zone_all_u, zone_all_w, zone_u, zone_f, zone_m)
        fields[...] = jnp.zeros_like(fields)
        coarse_fields(zone_u, zone_f, zone_m, temp, fields)
        assemble(fields, strip, mat, side)
        solve_zone(fields, mat, side, solved, answer)
        place_zone(begin, zone_m, answer, spread, temp, added)


def body(forcing, start_field, modulus, corners):
    brick = modulus.shape
    bx, by, bz = brick
    counts = [lax.axis_size(name) for name in AXES]
    margins = (HALO, -(-HALO // 8) * 8)
    span = [size + 2 * margin for size, margin in zip(brick, margins)] + [counts[2] * bz]
    whole = pl.BlockSpec(memory_space=pltpu.VMEM)
    dma = pltpu.SemaphoreType.DMA
    peers = max(counts[2] - 1, 1)
    zone_all_u, zone_all_w = pl.pallas_call(
        functools.partial(sweep_kernel, counts, brick, margins),
        out_shape=(
            jax.ShapeDtypeStruct((3, *span), F32),
            jax.ShapeDtypeStruct((4, *span), F32),
        ),
        in_specs=[whole, whole, whole],
        out_specs=(whole, whole),
        scratch_shapes=[
            pltpu.VMEM((4, bx + 2, by, bz), F32),
            *[pltpu.VMEM((3, bx + 2, by, bz), F32)] * (FSWEEPS - 1),
            pltpu.VMEM((FSWEEPS, 2, 4, bx, bz), F32),
            pltpu.VMEM((FSWEEPS, 2, 4, bx, bz), F32),
            pltpu.VMEM((2, 4, bx, by, bz), F32),
            *[pltpu.VMEM((2, 3, bx, by, bz), F32)] * (FSWEEPS - 1),
            pltpu.VMEM((6, bx, by, bz), F32),
            pltpu.VMEM((bx, by, bz), F32),
            dma((FSWEEPS, len(FACES))),
            dma((FSWEEPS, len(FACES))),
            dma((2, len(AROUND))),
            dma((2, len(AROUND))),
            dma((2, peers)),
            dma((2, peers)),
        ],
        compiler_params=pltpu.CompilerParams(
            collective_id=0, has_side_effects=True, vmem_limit_bytes=40 * 1024 * 1024
        ),
        name="sweeps",
    )(forcing, start_field, modulus)
    zone_span = 2 * PC + 2
    zone_rows = -(-zone_span // 8) * 8
    size = -(-PC * PC // 8) * 8
    planes = PC // 2 + 3
    field, added = pl.pallas_call(
        functools.partial(zone_kernel, counts, brick, margins),
        out_shape=(
            jax.ShapeDtypeStruct(forcing.shape, F32),
            jax.ShapeDtypeStruct(tuple(span), F32),
        ),
        in_specs=[pl.BlockSpec(memory_space=pltpu.SMEM), whole, whole],
        out_specs=(whole, whole),
        scratch_shapes=[
            pltpu.VMEM((3, zone_span, zone_rows, 128), F32),
            pltpu.VMEM((3, zone_span, zone_rows, 128), F32),
            pltpu.VMEM((zone_span, zone_rows, 128), F32),
            pltpu.VMEM((3 * FIELDS, zone_rows, 128), F32),
            pltpu.VMEM((3 * FIELDS, size, 128), F32),
            pltpu.VMEM((3 * size, 512), F32),
            pltpu.VMEM((2, planes, 128, 128), F32),
            pltpu.VMEM((2, planes, 128, 384), F32),
            pltpu.VMEM((2, planes, size, 384), F32),
            pltpu.VMEM((2, planes, 128, 128), F32),
            pltpu.VMEM((128, 128), F32),
        ],
        compiler_params=pltpu.CompilerParams(vmem_limit_bytes=40 * 1024 * 1024),
        name="zone",
    )(corners, zone_all_u, zone_all_w)
    updated = pl.pallas_call(
        functools.partial(gather_kernel, counts, brick, margins),
        out_shape=jax.ShapeDtypeStruct(brick, F32),
        in_specs=[whole, whole],
        out_specs=whole,
        scratch_shapes=[
            pltpu.VMEM((span[0], span[1], bz), F32),
            pltpu.VMEM((peers, span[0], span[1], bz), F32),
            pltpu.VMEM((2, margins[0], by, bz), F32),
            pltpu.VMEM((2, bx, margins[1], bz), F32),
            pltpu.VMEM((4, margins[0], margins[1], bz), F32),
            dma((len(AROUND),)),
            dma((len(AROUND),)),
            dma((peers,)),
            dma((peers,)),
        ],
        compiler_params=pltpu.CompilerParams(
            collective_id=1, has_side_effects=True, vmem_limit_bytes=40 * 1024 * 1024
        ),
        name="gather",
    )(added, modulus)
    return (field, updated)


def solution(mesh):
    placed = (
        P(None, "gx", "gy", "gz"),
        P(None, "gx", "gy", "gz"),
        P("gx", "gy", "gz"),
        P(("gx", "gy", "gz"), None),
    )
    return jax.shard_map(
        body,
        mesh=mesh,
        in_specs=placed,
        out_specs=(P(None, "gx", "gy", "gz"), P("gx", "gy", "gz")),
        check_vma=False,
    )
```

```python
import functools
import math

import jax
import jax.numpy as jnp
from jax import lax
from jax.experimental import pallas as pl
from jax.experimental.pallas import tpu as pltpu
from jax.sharding import PartitionSpec as P

PC = 10
HALO = 6
FSWEEPS = 4


MASS_TERM = 0.5
DAMPING = 0.1
EPSILON = 1e-06
HIGHEST = lax.Precision.HIGHEST
F32 = jnp.float32


def dot(a, b, contract):
    return lax.dot_general(
        a, b, ((contract[:1], contract[1:]), ((), ())), precision=HIGHEST, preferred_element_type=F32
    )


def roll(values, shift, axis):
    return pltpu.roll(values, shift % values.shape[axis], axis)


def iota(shape, axis):
    return lax.broadcasted_iota(jnp.int32, shape, axis)


MESH_ID = pl.DeviceIdType.MESH
AXES = ("gx", "gy", "gz")
AROUND = tuple((dx, dy) for dx in (-1, 0, 1) for dy in (-1, 0, 1) if (dx, dy) != (0, 0))
FACES = ((-1, 0, 0), (1, 0, 0), (0, -1, 0), (0, 1, 0), (0, 0, -1), (0, 0, 1))


class Place:
    def __init__(self, counts):
        self.counts = counts
        self.here = [lax.axis_index(name) for name in AXES]

    def exists(self, step):
        inside = None
        for at, count, move in zip(self.here, self.counts, step):
            if move:
                test = at + move < count if move > 0 else at + move >= 0
                inside = test if inside is None else inside & test
        return inside

    def device(self, step):
        return tuple(at + move for at, move in zip(self.here, step))

    def peer(self, turn):
        return self.here[:2] + [lax.rem(self.here[2] + turn, self.counts[2])]

    def greet(self):
        barrier = pltpu.get_barrier_semaphore()
        total = self.counts[2] - 1
        for dx, dy in AROUND:
            step = (dx, dy, 0)

            @pl.when(self.exists(step))
            def _():
                pl.semaphore_signal(
                    barrier, inc=1, device_id=self.device(step), device_id_type=MESH_ID
                )

            total = total + self.exists(step).astype(jnp.int32)
        for turn in range(1, self.counts[2]):
            pl.semaphore_signal(
                barrier, inc=1, device_id=tuple(self.peer(turn)), device_id_type=MESH_ID
            )
        pl.semaphore_wait(barrier, total)


def opposite(step):
    return tuple(-move for move in step)


class Message:
    def __init__(self, place, step, source, target, send, recv):
        self.place, self.step = place, step
        self.copy = pltpu.make_async_remote_copy(
            src_ref=source,
            dst_ref=target,
            send_sem=send,
            recv_sem=recv,
            device_id=place.device(step),
            device_id_type=MESH_ID,
        )

    def start(self):
        pl.when(self.place.exists(self.step))(self.copy.start)

    def sent(self):
        pl.when(self.place.exists(self.step))(self.copy.wait_send)

    def arrived(self):
        pl.when(self.place.exists(opposite(self.step)))(self.copy.wait_recv)


def edge_span(move, size, margin, reach=None):
    reach = margin if reach is None else reach
    if move > 0:
        return slice(margin + size - reach, margin + size), slice(margin - reach, margin)
    if move < 0:
        far = margin + size
        return slice(margin, margin + reach), slice(far, far + reach)
    return slice(margin, margin + size), slice(margin, margin + size)


def spread_messages(place, brick, margins, ref, lanes, send, recv):
    messages = []
    for n, (dx, dy) in enumerate(AROUND):
        from_x, to_x = edge_span(dx, brick[0], margins[0], HALO)
        from_y, to_y = edge_span(dy, brick[1], margins[1], HALO)
        messages.append(
            Message(
                place,
                (dx, dy, 0),
                ref.at[:, from_x, from_y, lanes],
                ref.at[:, to_x, to_y, lanes],
                send.at[n],
                recv.at[n],
            )
        )
    return messages


def peer_copies(place, ref, lanes, send, recv):
    return [
        pltpu.make_async_remote_copy(
            src_ref=ref.at[:, :, :, lanes],
            dst_ref=ref.at[:, :, :, lanes],
            send_sem=send.at[turn - 1],
            recv_sem=recv.at[turn - 1],
            device_id=tuple(place.peer(turn)),
            device_id_type=MESH_ID,
        )
        for turn in range(1, place.counts[2])
    ]


def clear_outside(place, brick, margins, refs, lanes):
    for dx, dy in AROUND:
        _, to_x = edge_span(-dx, brick[0], margins[0])
        _, to_y = edge_span(-dy, brick[1], margins[1])

        @pl.when(jnp.logical_not(place.exists((dx, dy, 0))))
        def _():
            for ref in refs:
                for k in range(ref.shape[0]):
                    shape = (to_x.stop - to_x.start, to_y.stop - to_y.start, brick[2])
                    ref[k, to_x, to_y, lanes] = jnp.zeros(shape, F32)


def sweep_kernel(counts, brick, margins, forcing, start, modulus, zone_u, zone_w, *scratch):
    fields, rows_in, rows_out, sides = scratch[0:4], scratch[4], scratch[5], scratch[6:10]
    coupling, inverse = scratch[10:12]
    face_send, face_recv, bulk_send, bulk_recv, peer_send, peer_recv = scratch[12:]
    place = Place(counts)
    bx, by, bz = brick
    hx, hy = margins
    lanes = pl.ds(pl.multiple_of(place.here[2] * bz, bz), bz)
    row = iota((by, bz), 0)
    lane = iota((by, bz), 1)

    def stage(x, _):
        for k in range(3):
            u = start[k, x]
            fields[0][k, x + 1] = u
            rows_out[0, 0, k, pl.ds(x, 1), :] = u[:1]
            rows_out[0, 1, k, pl.ds(x, 1), :] = u[by - 1 :]
            zone_w[k, hx + x, hy : hy + by, lanes] = forcing[k, x]
        m = modulus[x]
        fields[0][3, x + 1] = m
        rows_out[0, 0, 3, pl.ds(x, 1), :] = m[:1]
        rows_out[0, 1, 3, pl.ds(x, 1), :] = m[by - 1 :]
        zone_w[3, hx + x, hy : hy + by, lanes] = m
        return 0

    lax.fori_loop(0, bx, stage, 0)

    def faces(sweep):
        channels = 4 if sweep == 0 else 3
        field = fields[sweep]
        messages = []
        for n, step in enumerate(FACES):
            dx, dy, dz = step
            if dx:
                source = field.at[:, bx if dx > 0 else 1]
                target = field.at[:, 0 if dx > 0 else bx + 1]
            elif dy:
                source = rows_out.at[sweep, 1 if dy > 0 else 0, :channels]
                target = rows_in.at[sweep, 0 if dy > 0 else 1, :channels]
            else:
                source = field.at[:, 1 : bx + 1]
                target = sides[sweep].at[0 if dz > 0 else 1]
            at = (sweep, n)
            messages.append(
                Message(place, step, source, target, face_send.at[at], face_recv.at[at])
            )
        return messages

    clear_outside(place, brick, margins, (zone_u, zone_w), lanes)
    for n, (dx, dy, dz) in enumerate(FACES):

        @pl.when(jnp.logical_not(place.exists((dx, dy, dz))))
        def _():
            for sweep in range(FSWEEPS):
                if dx:
                    plane = 0 if dx < 0 else bx + 1
                    for k in range(fields[sweep].shape[0]):
                        fields[sweep][k, plane] = jnp.zeros((by, bz), F32)
                elif dy:
                    for k in range(4):
                        rows_in[sweep, 0 if dy < 0 else 1, k] = jnp.zeros((bx, bz), F32)
                else:
                    for k in range(sides[sweep].shape[1]):
                        blank = jnp.zeros((bx, by, bz), F32)
                        sides[sweep][0 if dz < 0 else 1, k] = blank

    place.greet()
    messages = faces(0)
    pending = list(messages)
    for message in messages:
        message.start()
    bulk = spread_messages(
        place, brick, margins, zone_w, lanes, bulk_send.at[0], bulk_recv.at[0]
    )
    for message in bulk:
        message.start()

    def around(sweep, k, x, u):
        low, high = rows_in[sweep, 0, k, pl.ds(x, 1), :], rows_in[sweep, 1, k, pl.ds(x, 1), :]
        y_up = jnp.where(row == by - 1, jnp.broadcast_to(high, u.shape), roll(u, -1, 0))
        y_down = jnp.where(row == 0, jnp.broadcast_to(low, u.shape), roll(u, 1, 0))
        below, above = sides[sweep][0, k, x], sides[sweep][1, k, x]
        z_up = jnp.where(lane == bz - 1, roll(above, -1, 1), roll(u, -1, 1))
        z_down = jnp.where(lane == 0, roll(below, 1, 1), roll(u, 1, 1))
        field = fields[sweep]
        return field[k, x + 2], field[k, x], y_up, y_down, z_up, z_down

    def couple(x, _):
        m = fields[0][3, x + 1]
        below = MASS_TERM
        for n, other in enumerate(around(0, 3, x, m)):
            face = 0.5 * (m + other)
            coupling[n, x] = face
            below = below + face
        inverse[x] = 1.0 / below
        return 0

    for sweep in range(FSWEEPS):
        for message in messages:
            message.arrived()
        if sweep == 0:
            lax.fori_loop(0, bx, couple, 0)

        def relax(x, _, sweep=sweep):
            weights = [coupling[n, x] for n in range(6)]
            scale = inverse[x]
            for k in range(3):
                u = fields[sweep][k, x + 1]
                total = forcing[k, x]
                for weight, other in zip(weights, around(sweep, k, x, u)):
                    total = total + weight * other
                total = total * scale
                if sweep < FSWEEPS - 1:
                    fields[sweep + 1][k, x + 1] = total
                    rows_out[sweep + 1, 0, k, pl.ds(x, 1), :] = total[:1]
                    rows_out[sweep + 1, 1, k, pl.ds(x, 1), :] = total[by - 1 :]
                else:
                    zone_u[k, hx + x, hy : hy + by, lanes] = total
            return 0

        lax.fori_loop(0, bx, relax, 0)
        if sweep < FSWEEPS - 1:
            messages = faces(sweep + 1)
            pending += messages
            for message in messages:
                message.start()
    last = spread_messages(
        place, brick, margins, zone_u, lanes, bulk_send.at[1], bulk_recv.at[1]
    )
    for message in last:
        message.start()
    for message in bulk:
        message.arrived()
    copies = peer_copies(place, zone_w, lanes, peer_send.at[0], peer_recv.at[0])
    for copy in copies:
        copy.start()
    for message in last:
        message.arrived()
    more = peer_copies(place, zone_u, lanes, peer_send.at[1], peer_recv.at[1])
    for copy in more:
        copy.start()
    for message in pending + bulk + last:
        message.sent()
    for copy in copies + more:
        copy.wait()


def gather_kernel(counts, brick, margins, added, modulus, out, total, from_peer, *scratch):
    from_x, from_y, from_xy, send, recv, peer_send, peer_recv = scratch
    place = Place(counts)
    bx, by, bz = brick
    hx, hy = margins

    def part(turn):
        at = lax.rem(place.here[2] + turn, counts[2])
        return pl.ds(pl.multiple_of(at * bz, bz), bz)

    targets = {}
    for n, (dx, dy) in enumerate(AROUND):
        if dy == 0:
            targets[n] = from_x.at[(dx + 1) // 2]
        elif dx == 0:
            targets[n] = from_y.at[(dy + 1) // 2]
        else:
            targets[n] = from_xy.at[dx + 1 + (dy + 1) // 2]

        @pl.when(jnp.logical_not(place.exists((-dx, -dy, 0))))
        def _():
            targets[n][...] = jnp.zeros(targets[n].shape, F32)

    place.greet()
    copies = [
        pltpu.make_async_remote_copy(
            src_ref=added.at[:, :, part(turn)],
            dst_ref=from_peer.at[turn - 1],
            send_sem=peer_send.at[turn - 1],
            recv_sem=peer_recv.at[turn - 1],
            device_id=tuple(place.peer(turn)),
            device_id_type=MESH_ID,
        )
        for turn in range(1, counts[2])
    ]
    for copy in copies:
        copy.start()
    for copy in copies:
        copy.wait_recv()

    def collect(x, _):
        value = added[x, :, part(0)]
        for turn in range(1, counts[2]):
            value = value + from_peer[turn - 1, x]
        total[x] = value
        return 0

    lax.fori_loop(0, total.shape[0], collect, 0)
    messages = []
    for n, (dx, dy) in enumerate(AROUND):
        _, at_x = edge_span(-dx, bx, hx)
        _, at_y = edge_span(-dy, by, hy)
        messages.append(
            Message(place, (dx, dy, 0), total.at[at_x, at_y], targets[n], send.at[n], recv.at[n])
        )
    for message in messages:
        message.start()

    def centre(x, _):
        out[x] = modulus[x] + total[hx + x, hy : hy + by, :]
        return 0

    lax.fori_loop(0, bx, centre, 0)
    for message in messages:
        message.arrived()
    for n, (dx, dy) in enumerate(AROUND):
        to_x, _ = edge_span(-dx, bx, hx)
        to_y, _ = edge_span(-dy, by, hy)
        out[to_x.start - hx : to_x.stop - hx, to_y.start - hy : to_y.stop - hy, :] += targets[n][...]
    for message in messages:
        message.sent()
    for copy in copies:
        copy.wait_send()


FIELDS = 8


def coarse_fields(zone_u, zone_f, zone_m, temp, fields):
    rows = zone_m.shape[1]
    first_y = iota((rows, 128), 0) % 2 == 1
    first_z = iota((rows, 128), 1) % 2 == 1
    rank = iota((PC, 128), 0)
    lane = iota((PC, 128), 1)
    for x in range(PC):
        for k in range(3):
            sums = [None] * FIELDS

            def put(number, value):
                sums[number] = value if sums[number] is None else sums[number] + value

            for a in range(2):
                at = 2 * x + 1 + a
                u, m = zone_u[k, at], zone_m[at]
                applied = MASS_TERM * u
                laplace = jnp.zeros_like(u)
                for number, (axis, step) in enumerate(
                    ((0, 1), (0, -1), (1, 1), (1, -1), (2, 1), (2, -1))
                ):
                    if axis == 0:
                        u_next, m_next = zone_u[k, at + step], zone_m[at + step]
                    else:
                        u_next, m_next = roll(u, -step, axis - 1), roll(m, -step, axis - 1)
                    change = u - u_next
                    applied = applied + 0.5 * (m + m_next) * change
                    laplace = laplace + change
                    flow = -0.5 * m_next * change
                    if axis == 0:
                        same = (a == 0) == (step == 1)
                        put(0 if same else 1 + number, flow)
                    else:
                        first = first_y if axis == 1 else first_z
                        near = first if step == 1 else ~first
                        put(0, jnp.where(near, flow, 0.0))
                        put(1 + number, jnp.where(near, 0.0, flow))
                put(0, -0.5 * m * laplace)
                put(7, zone_f[k, at] - applied)
            for number in range(FIELDS):
                slot = temp.at[k * FIELDS + number]
                slot[...] = sums[number]
                pair = slot[pl.ds(1, PC, stride=2), :] + slot[pl.ds(2, PC, stride=2), :]
                pair = pair + roll(pair, -1, 1)
                keep = (lane % 2 == 1) & (lane < 2 * PC)
                if number == 1 and x == PC - 1 or number == 2 and x == 0:
                    keep = jnp.zeros_like(keep)
                if number == 3:
                    keep = keep & (rank < PC - 1)
                if number == 4:
                    keep = keep & (rank > 0)
                if number == 5:
                    keep = keep & (lane < 2 * PC - 2)
                if number == 6:
                    keep = keep & (lane > 1)
                fields[k * FIELDS + number, x * PC : (x + 1) * PC, :] = jnp.where(keep, pair, 0.0)


PAIRS = ((0, 0, 0), (1, 0, 0), (-1, 0, 0), (0, 1, 0), (0, -1, 0), (0, 0, 1), (0, 0, -1))
BANDS = tuple(
    sorted({tuple(b - a for a, b in zip(one, two)) for one in PAIRS for two in PAIRS})
)
PER_GROUP = 12


def transpose_fields(fields, packed, flat):
    size = fields.shape[1]
    flat[...] = jnp.zeros_like(flat)
    for group in range(2):
        total = None
        for j in range(PER_GROUP):
            shift = 2 * PC * (j // 2) - 1 + j % 2
            part = fields[group * PER_GROUP + j]
            part = roll(part, shift, 1) if shift else part
            total = part if total is None else total + part
        packed[:size, :] = total
        packed[size:, :] = jnp.zeros((128 - size, 128), F32)
        packed[...] = packed[...].T
        for j in range(PER_GROUP):
            first = 2 * PC * (j // 2) + j % 2
            flat[group * PER_GROUP + j, :PC, :] = packed[pl.ds(first, PC, stride=2), :]


def band_sums(flat, packed, bands, slopes):
    columns = [[flat[k * FIELDS + n] for k in range(3)] for n in range(FIELDS)]

    def product(a, b):
        return sum(columns[a][k] * columns[b][k] for k in range(3))

    def moved(value, step):
        x, y, z = step
        value = roll(value, PC * x + y, 1) if x or y else value
        return roll(value, z, 0) if z else value

    totals = {}
    trace = None
    for a in range(len(PAIRS)):
        for b in range(a, len(PAIRS)):
            value = product(a, b)
            if a == b:
                trace = value if trace is None else trace + value
            for one, two in {(a, b), (b, a)}:
                key = tuple(q - p for p, q in zip(PAIRS[one], PAIRS[two]))
                part = moved(value, PAIRS[two])
                totals[key] = part if key not in totals else totals[key] + part
    trace = jnp.sum(jnp.sum(trace, axis=0, keepdims=True), axis=1, keepdims=True)
    ridge = DAMPING * trace / PC**3 + EPSILON
    totals[0, 0, 0] = totals[0, 0, 0] + ridge
    for n, key in enumerate(BANDS):
        bands[n] = totals[key]
    slope = None
    for a in range(len(PAIRS)):
        part = moved(product(a, FIELDS - 1), PAIRS[a])
        slope = part if slope is None else slope + part
    packed[...] = jnp.zeros_like(packed)
    packed[: slope.shape[0], :] = slope
    slopes[...] = packed[...].T


def fill(c, t, z, bands, slopes, mat, side, reach):
    params = PC * PC
    lane = iota((8, 128), 1)
    gap = lane - iota((8, 128), 0)
    column = pltpu.roll(slopes[...], params - z, 1)
    ahead = 1 if c == 0 else -1

    def rows_of(depth):
        found = []
        for n, (x, y, dz) in enumerate(BANDS):
            if dz == depth * ahead:
                row = bands[n, pl.ds(z + depth * ahead, 1), :]
                found.append((PC * x + y, jnp.broadcast_to(row, (8, 128))))
        return found

    parts = [rows_of(depth) for depth in range(reach + 1)]
    for q in range(-(-params // 8)):
        here = slice(8 * q, 8 * q + 8)
        inside = lane < params

        def block(entries):
            value = jnp.zeros((8, 128), F32)
            for offset, row in entries:
                value = jnp.where(gap == 8 * q + offset, row, value)
            return jnp.where(inside, value, 0.0)

        mat[c, t, here, :] = block(parts[0])
        first = block(parts[1]) if reach > 0 else jnp.zeros((8, 128), F32)
        side[c, t, here, 0:128] = jnp.where(lane == params, column[here], first)
        if reach > 1:
            side[c, t, here, 128:256] = block(parts[2])


def assemble(bands, slopes, mat, side):
    meet = PC // 2 - 1
    mat[...] = jnp.zeros_like(mat)
    side[...] = jnp.zeros_like(side)

    def both(t, _):
        fill(0, t, t, bands, slopes, mat, side, 2)
        fill(1, t, PC - 1 - t, bands, slopes, mat, side, 2)
        return 0

    lax.fori_loop(0, meet, both, 0)
    fill(0, meet, meet, bands, slopes, mat, side, 1)
    fill(0, meet + 1, meet + 1, bands, slopes, mat, side, 0)


def factored(blocks, count):
    lane = iota((8, 128), 1)
    sub = iota((8, 128), 0)
    tiles = -(-count // 8)

    def over_lanes(value, at):
        return jnp.broadcast_to(value[:, at : at + 1], value.shape)

    def over_rows(value, at):
        return jnp.broadcast_to(value[at : at + 1, :], value.shape)

    grids = [[block[8 * q : 8 * q + 8] for q in range(tiles)] for block in blocks]
    lower = [[] for _ in blocks]
    scaled = [[] for _ in blocks]
    for p in range(tiles):
        pivots = range(8 * p, min(8 * p + 8, count))
        within = (lane >= pivots[0]) & (lane <= pivots[-1])
        keep = (lane <= pivots[-1]) & (sub < len(pivots))
        for grid, low, high in zip(grids, lower, scaled):
            panel = grid[p]
            unit = jnp.where(lane - 8 * p == sub, 1.0, 0.0)
            low.append(jnp.where(keep, jnp.where(within, unit, panel), 0.0))
            columns = [over_lanes(panel, j) for j in pivots]
            for i, j in enumerate(pivots):
                column = columns[i]
                pivot = 1.0 / over_rows(column, i)
                row = jnp.where(lane == j, pivot, over_rows(panel, i) * pivot)
                for n in range(i + 1, len(pivots)):
                    crossing = over_rows(columns[n], i) * pivot
                    columns[n] = jnp.where(sub == i, crossing, columns[n] - column * crossing)
                cleared = jnp.where(lane == j, 0.0, panel)
                panel = jnp.where(sub == i, row, cleared - column * row)
            high.append(jnp.where(keep, panel, 0.0))
            rows = [over_rows(panel, i) for i in range(len(pivots))]
            for q in range(p + 1, tiles):
                old = grid[q]
                terms = [over_lanes(old, j) * row for j, row in zip(pivots, rows)]
                while len(terms) > 1:
                    pairs = [terms[n] + terms[n + 1] for n in range(0, len(terms) - 1, 2)]
                    terms = pairs + terms[len(terms) - len(terms) % 2 :]
                grid[q] = jnp.where(within, 0.0, old) - terms[0]
    return [
        (jnp.concatenate(low, axis=0), jnp.concatenate(high, axis=0))
        for low, high in zip(lower, scaled)
    ]


def eliminate(t, chains, size, mat, side, lowers, solved, more=True):
    params = PC * PC
    mark = iota((128, 128), 1) == params
    blocks = [mat[c, t, :size, :] for c in chains]
    for c, (low, high) in zip(chains, factored(blocks, params)):
        lowers[c, t, :size, :] = low
        right = side[c, t, :size, :]
        z = dot(high[:, :size], right, (1, 0))
        solved[c, t, :size, :] = z
        if not more:
            continue
        y = dot(low[:, :size], right, (1, 0))
        schur = dot(y, z, (0, 0))
        near, far = schur[:128], schur[128:]
        mat[c, t + 1] -= near[:, :128]
        side[c, t + 1, :, 0:128] -= jnp.where(mark, near[:, :128], near[:, 128:])
        mat[c, t + 2] -= far[:, 128:]
        side[c, t + 2, :, 0:128] -= jnp.where(mark, far[:, :128], 0.0)


def solve_zone(size, mat, side, lowers, solved, spread):
    params = PC * PC
    meet = PC // 2 - 1
    mark = iota((128, 128), 1) == params
    lowers[...] = jnp.zeros_like(lowers)
    solved[...] = jnp.zeros_like(solved)

    def both(t, _):
        eliminate(t, (0, 1), size, mat, side, lowers, solved)
        return 0

    lax.fori_loop(0, meet, both, 0)
    mat[0, meet] += mat[1, meet + 1]
    mat[0, meet + 1] += mat[1, meet]
    turned = side[1, meet, :, 0:128].T
    side[0, meet, :, 0:128] += jnp.where(mark, side[1, meet + 1, :, 0:128], turned)
    side[0, meet + 1, :, 0:128] += jnp.where(mark, side[1, meet, :, 0:128], 0.0)
    eliminate(meet, (0,), size, mat, side, lowers, solved)
    eliminate(meet + 1, (0,), size, mat, side, lowers, solved, more=False)

    flag = iota((8, 128), 1) == params

    def back(c, t, near, far):
        row = jnp.concatenate([jnp.where(flag, -1.0, near), far], axis=1)
        value = dot(row, solved[c, t], (1, 1))
        return -dot(value, lowers[c, t], (1, 0))

    blank = jnp.zeros((8, 128), F32)
    rows = [blank] * PC
    rows[meet + 1] = back(0, meet + 1, blank, blank)
    rows[meet] = back(0, meet, rows[meet + 1], blank)
    for t in range(meet - 1, -1, -1):
        rows[t] = back(0, t, rows[t + 1], rows[t + 2])
        z = PC - 1 - t
        rows[z] = back(1, t, rows[z - 1], rows[z - 2])
    spread[...] = jnp.zeros_like(spread)
    for z in range(PC):
        spread[2 * z + 1 : 2 * z + 3, :] = -rows[z][:2]
    spread[...] = spread[...].T


def place_zone(begin, zone_m, spread, temp, added):
    rows = zone_m.shape[1]
    span = 2 * PC

    def ramp(position):
        value = jnp.sin(math.pi * (position.astype(F32) - 0.5) / span)
        return jnp.where((position >= 1) & (position <= span), value, 0.0)

    weight = ramp(iota((rows, 128), 0)) * ramp(iota((rows, 128), 1))
    temp[0] = jnp.zeros_like(weight)
    shift = lax.rem(begin[2] + added.shape[2], added.shape[2])
    for x in range(PC):
        part = spread[x * PC : (x + 1) * PC, :]
        temp[0, pl.ds(1, PC, stride=2), :] = part
        temp[0, pl.ds(2, PC, stride=2), :] = part
        value = weight * temp[0]
        for a in range(2):
            at = 2 * x + 1 + a
            plane = value * math.sin(math.pi * (at - 0.5) / span) * zone_m[at]
            plane = jnp.pad(plane, ((0, added.shape[1] - rows), (0, 0)))
            plane = pltpu.roll(plane, begin[1], 0)
            plane = jnp.pad(plane, ((0, 0), (0, added.shape[2] - 128)))
            added[begin[0] + at] += pltpu.roll(plane, shift, 1)


def cut_zone(begin, depth, zone_all_u, zone_all_w, zone_u, zone_f, zone_m):
    count, rows = zone_m.shape[:2]
    whole_rows, whole_lanes = zone_all_u.shape[-2:]
    shift = lax.rem(whole_lanes - begin[2], whole_lanes)
    shift_y = lax.rem(whole_rows - begin[1], whole_rows)
    z = begin[2] + iota((rows, 128), 1)
    inside = (z >= 0) & (z < depth)

    def cut(x, _):
        def take(ref, k):
            plane = pltpu.roll(ref[k, begin[0] + x], shift, 1)[:, :128]
            return jnp.where(inside, pltpu.roll(plane, shift_y, 0)[:rows], 0.0)

        for k in range(3):
            zone_u[k, x] = take(zone_all_u, k)
            zone_f[k, x] = take(zone_all_w, k)
        zone_m[x] = take(zone_all_w, 3)
        return 0

    lax.fori_loop(0, count, cut, 0)


def zone_kernel(counts, brick, margins, corners, zone_all_u, zone_all_w, field_out, added, *scratch):
    zone_u, zone_f, zone_m = scratch[:3]
    temp, fields, packed, flat, bands, slopes, mat, side, lowers, solved, spread = scratch[3:]
    bx, by, bz = brick
    hx, hy = margins
    here = [lax.axis_index(name) for name in AXES]
    lanes = pl.ds(pl.multiple_of(here[2] * bz, bz), bz)
    for k in range(3):
        field_out[k] = zone_all_u[k, hx : hx + bx, hy : hy + by, lanes]
    added[...] = jnp.zeros_like(added)
    for number in range(corners.shape[0]):
        begin = [
            corners[number, 0] - here[0] * bx + hx - 1,
            corners[number, 1] - here[1] * by + hy - 1,
            corners[number, 2] - 1,
        ]
        cut_zone(begin, counts[2] * bz, zone_all_u, zone_all_w, zone_u, zone_f, zone_m)
        fields[...] = jnp.zeros_like(fields)
        coarse_fields(zone_u, zone_f, zone_m, temp, fields)
        transpose_fields(fields, packed, flat)
        band_sums(flat, packed, bands, slopes)
        assemble(bands, slopes, mat, side)
        solve_zone(fields.shape[1], mat, side, lowers, solved, spread)
        place_zone(begin, zone_m, spread, temp, added)


def body(forcing, start_field, modulus, corners):
    brick = modulus.shape
    bx, by, bz = brick
    counts = [lax.axis_size(name) for name in AXES]
    margins = (HALO, -(-HALO // 8) * 8)
    span = [size + 2 * margin for size, margin in zip(brick, margins)] + [counts[2] * bz]
    whole = pl.BlockSpec(memory_space=pltpu.VMEM)
    dma = pltpu.SemaphoreType.DMA
    peers = max(counts[2] - 1, 1)
    zone_all_u, zone_all_w = pl.pallas_call(
        functools.partial(sweep_kernel, counts, brick, margins),
        out_shape=(
            jax.ShapeDtypeStruct((3, *span), F32),
            jax.ShapeDtypeStruct((4, *span), F32),
        ),
        in_specs=[whole, whole, whole],
        out_specs=(whole, whole),
        scratch_shapes=[
            pltpu.VMEM((4, bx + 2, by, bz), F32),
            *[pltpu.VMEM((3, bx + 2, by, bz), F32)] * (FSWEEPS - 1),
            pltpu.VMEM((FSWEEPS, 2, 4, bx, bz), F32),
            pltpu.VMEM((FSWEEPS, 2, 4, bx, bz), F32),
            pltpu.VMEM((2, 4, bx, by, bz), F32),
            *[pltpu.VMEM((2, 3, bx, by, bz), F32)] * (FSWEEPS - 1),
            pltpu.VMEM((6, bx, by, bz), F32),
            pltpu.VMEM((bx, by, bz), F32),
            dma((FSWEEPS, len(FACES))),
            dma((FSWEEPS, len(FACES))),
            dma((2, len(AROUND))),
            dma((2, len(AROUND))),
            dma((2, peers)),
            dma((2, peers)),
        ],
        compiler_params=pltpu.CompilerParams(
            collective_id=0, has_side_effects=True, vmem_limit_bytes=40 * 1024 * 1024
        ),
        name="sweeps",
    )(forcing, start_field, modulus)
    zone_span = 2 * PC + 2
    zone_rows = -(-zone_span // 8) * 8
    size = -(-PC * PC // 8) * 8
    planes = PC // 2 + 3
    field, added = pl.pallas_call(
        functools.partial(zone_kernel, counts, brick, margins),
        out_shape=(
            jax.ShapeDtypeStruct(forcing.shape, F32),
            jax.ShapeDtypeStruct(tuple(span), F32),
        ),
        in_specs=[pl.BlockSpec(memory_space=pltpu.SMEM), whole, whole],
        out_specs=(whole, whole),
        scratch_shapes=[
            pltpu.VMEM((3, zone_span, zone_rows, 128), F32),
            pltpu.VMEM((3, zone_span, zone_rows, 128), F32),
            pltpu.VMEM((zone_span, zone_rows, 128), F32),
            pltpu.VMEM((3 * FIELDS, zone_rows, 128), F32),
            pltpu.VMEM((3 * FIELDS, size, 128), F32),
            pltpu.VMEM((128, 128), F32),
            pltpu.VMEM((3 * FIELDS, 16, 128), F32),
            pltpu.VMEM((len(BANDS), 16, 128), F32),
            pltpu.VMEM((128, 128), F32),
            pltpu.VMEM((2, planes, 128, 128), F32),
            pltpu.VMEM((2, planes, 128, 256), F32),
            pltpu.VMEM((2, planes, 128, 128), F32),
            pltpu.VMEM((2, planes, 128, 256), F32),
            pltpu.VMEM((128, 128), F32),
        ],
        compiler_params=pltpu.CompilerParams(vmem_limit_bytes=40 * 1024 * 1024),
        name="zone",
    )(corners, zone_all_u, zone_all_w)
    updated = pl.pallas_call(
        functools.partial(gather_kernel, counts, brick, margins),
        out_shape=jax.ShapeDtypeStruct(brick, F32),
        in_specs=[whole, whole],
        out_specs=whole,
        scratch_shapes=[
            pltpu.VMEM((span[0], span[1], bz), F32),
            pltpu.VMEM((peers, span[0], span[1], bz), F32),
            pltpu.VMEM((2, margins[0], by, bz), F32),
            pltpu.VMEM((2, bx, margins[1], bz), F32),
            pltpu.VMEM((4, margins[0], margins[1], bz), F32),
            dma((len(AROUND),)),
            dma((len(AROUND),)),
            dma((peers,)),
            dma((peers,)),
        ],
        compiler_params=pltpu.CompilerParams(
            collective_id=1, has_side_effects=True, vmem_limit_bytes=40 * 1024 * 1024
        ),
        name="gather",
    )(added, modulus)
    return (field, updated)


def solution(mesh):
    placed = (
        P(None, "gx", "gy", "gz"),
        P(None, "gx", "gy", "gz"),
        P("gx", "gy", "gz"),
        P(("gx", "gy", "gz"), None),
    )
    return jax.shard_map(
        body,
        mesh=mesh,
        in_specs=placed,
        out_specs=(P(None, "gx", "gy", "gz"), P("gx", "gy", "gz")),
        check_vma=False,
    )
```

```python
import functools
import math

import jax
import jax.numpy as jnp
from jax import lax
from jax.experimental import pallas as pl
from jax.experimental.pallas import tpu as pltpu
from jax.sharding import PartitionSpec as P

PC = 10
HALO = 6
FSWEEPS = 4


MASS_TERM = 0.5
DAMPING = 0.1
EPSILON = 1e-06
HIGHEST = lax.Precision.HIGHEST
F32 = jnp.float32


def dot(a, b, contract):
    return lax.dot_general(
        a, b, ((contract[:1], contract[1:]), ((), ())), precision=HIGHEST, preferred_element_type=F32
    )


def roll(values, shift, axis):
    return pltpu.roll(values, shift % values.shape[axis], axis)


def iota(shape, axis):
    return lax.broadcasted_iota(jnp.int32, shape, axis)


MESH_ID = pl.DeviceIdType.MESH
AXES = ("gx", "gy", "gz")
AROUND = tuple((dx, dy) for dx in (-1, 0, 1) for dy in (-1, 0, 1) if (dx, dy) != (0, 0))
FACES = ((-1, 0, 0), (1, 0, 0), (0, -1, 0), (0, 1, 0), (0, 0, -1), (0, 0, 1))


class Place:
    def __init__(self, counts):
        self.counts = counts
        self.here = [lax.axis_index(name) for name in AXES]

    def exists(self, step):
        inside = None
        for at, count, move in zip(self.here, self.counts, step):
            if move:
                test = at + move < count if move > 0 else at + move >= 0
                inside = test if inside is None else inside & test
        return inside

    def device(self, step):
        return tuple(at + move for at, move in zip(self.here, step))

    def peer(self, turn):
        return self.here[:2] + [lax.rem(self.here[2] + turn, self.counts[2])]

    def call(self):
        barrier = pltpu.get_barrier_semaphore()
        total = self.counts[2] - 1
        for dx, dy in AROUND:
            step = (dx, dy, 0)

            @pl.when(self.exists(step))
            def _():
                pl.semaphore_signal(
                    barrier, inc=1, device_id=self.device(step), device_id_type=MESH_ID
                )

            total = total + self.exists(step).astype(jnp.int32)
        for turn in range(1, self.counts[2]):
            pl.semaphore_signal(
                barrier, inc=1, device_id=tuple(self.peer(turn)), device_id_type=MESH_ID
            )
        return barrier, total


def opposite(step):
    return tuple(-move for move in step)


class Message:
    def __init__(self, place, step, source, target, send, recv):
        self.place, self.step = place, step
        self.copy = pltpu.make_async_remote_copy(
            src_ref=source,
            dst_ref=target,
            send_sem=send,
            recv_sem=recv,
            device_id=place.device(step),
            device_id_type=MESH_ID,
        )

    def start(self):
        pl.when(self.place.exists(self.step))(self.copy.start)

    def sent(self):
        pl.when(self.place.exists(self.step))(self.copy.wait_send)

    def arrived(self):
        pl.when(self.place.exists(opposite(self.step)))(self.copy.wait_recv)


def edge_span(move, size, margin, reach=None):
    reach = margin if reach is None else reach
    if move > 0:
        return slice(margin + size - reach, margin + size), slice(margin - reach, margin)
    if move < 0:
        far = margin + size
        return slice(margin, margin + reach), slice(far, far + reach)
    return slice(margin, margin + size), slice(margin, margin + size)


def regions(brick, margins, reach):
    found = []
    for dx, dy in AROUND:
        from_x, to_x = edge_span(dx, brick[0], margins[0], reach)
        from_y, to_y = edge_span(dy, brick[1], margins[1], reach)
        found.append(((dx, dy, 0), (from_x, from_y), (to_x, to_y)))
    return sorted(found, key=lambda entry: (entry[0][1] == 0, entry[0][0] != 0))


def spread_messages(place, brick, margins, ref, lanes, send, recv, reach):
    return [
        Message(
            place,
            step,
            ref.at[:, source[0], source[1], lanes],
            ref.at[:, target[0], target[1], lanes],
            send.at[n],
            recv.at[n],
        )
        for n, (step, source, target) in enumerate(regions(brick, margins, reach))
    ]


class Relay:
    def __init__(self, place, step, ref, lanes, span, send, recv):
        self.place, self.step = place, step
        view = ref.at[:, span[0], span[1], lanes]
        self.copies = [
            pltpu.make_async_remote_copy(
                src_ref=view,
                dst_ref=view,
                send_sem=send.at[turn - 1],
                recv_sem=recv.at[turn - 1],
                device_id=tuple(place.peer(turn)),
                device_id_type=MESH_ID,
            )
            for turn in range(1, place.counts[2])
        ]

    def when(self, action):
        test = self.place.exists(self.step) if any(self.step) else None
        action() if test is None else pl.when(test)(action)

    def start(self):
        self.when(lambda: [copy.start() for copy in self.copies] and None)

    def wait(self):
        self.when(lambda: [copy.wait() for copy in self.copies] and None)


def clear_outside(place, brick, margins, refs, lanes):
    for dx, dy in AROUND:
        _, to_x = edge_span(-dx, brick[0], margins[0])
        _, to_y = edge_span(-dy, brick[1], margins[1])

        @pl.when(jnp.logical_not(place.exists((dx, dy, 0))))
        def _():
            for ref in refs:
                for k in range(ref.shape[0]):
                    shape = (to_x.stop - to_x.start, to_y.stop - to_y.start, lanes.size)
                    ref[k, to_x, to_y, lanes] = jnp.zeros(shape, F32)


def sweep_kernel(counts, brick, margins, forcing, start, modulus, zone_u, zone_w, *scratch):
    fields, rows_in, rows_out, sides = scratch[0:4], scratch[4], scratch[5], scratch[6:10]
    coupling, inverse = scratch[10:12]
    face_send, face_recv, bulk_send, bulk_recv, peer_send, peer_recv, load = scratch[12:]
    place = Place(counts)
    bx, by, bz = brick
    hx, hy = margins
    lanes = pl.ds(pl.multiple_of(place.here[2] * bz, bz), bz)
    every = pl.ds(0, counts[2] * bz)
    row = iota((by, bz), 0)
    lane = iota((by, bz), 1)
    own = (slice(hx, hx + bx), slice(hy, hy + by))
    loads = [
        pltpu.make_async_copy(start, fields[0].at[:3, 1 : bx + 1], load.at[0]),
        pltpu.make_async_copy(modulus, fields[0].at[3, 1 : bx + 1], load.at[1]),
        pltpu.make_async_copy(modulus, zone_w.at[3, own[0], own[1], lanes], load.at[2]),
        pltpu.make_async_copy(forcing, zone_w.at[:3, own[0], own[1], lanes], load.at[3]),
    ]
    for copy in loads:
        copy.start()
    barrier, greetings = place.call()

    clear_outside(place, brick, margins, (zone_u, zone_w), every)
    for n, (dx, dy, dz) in enumerate(FACES):

        @pl.when(jnp.logical_not(place.exists((dx, dy, dz))))
        def _():
            for sweep in range(FSWEEPS):
                if dx:
                    plane = 0 if dx < 0 else bx + 1
                    for k in range(fields[sweep].shape[0]):
                        fields[sweep][k, plane] = jnp.zeros((by, bz), F32)
                elif dy:
                    for k in range(4):
                        rows_in[sweep, 0 if dy < 0 else 1, k] = jnp.zeros((bx, bz), F32)
                else:
                    for k in range(sides[sweep].shape[1]):
                        blank = jnp.zeros((bx, by, bz), F32)
                        sides[sweep][0 if dz < 0 else 1, k] = blank

    loads[0].wait()
    loads[1].wait()

    def stage(x, _):
        for k in range(4):
            u = fields[0][k, x + 1]
            rows_out[0, 0, k, pl.ds(x, 1), :] = u[:1]
            rows_out[0, 1, k, pl.ds(x, 1), :] = u[by - 1 :]
        return 0

    lax.fori_loop(0, bx, stage, 0)

    def faces(sweep):
        channels = 4 if sweep == 0 else 3
        field = fields[sweep]
        messages = []
        for n, step in enumerate(FACES):
            dx, dy, dz = step
            if dx:
                source = field.at[:, bx if dx > 0 else 1]
                target = field.at[:, 0 if dx > 0 else bx + 1]
            elif dy:
                source = rows_out.at[sweep, 1 if dy > 0 else 0, :channels]
                target = rows_in.at[sweep, 0 if dy > 0 else 1, :channels]
            else:
                source = field.at[:, 1 : bx + 1]
                target = sides[sweep].at[0 if dz > 0 else 1]
            at = (sweep, n)
            messages.append(
                Message(place, step, source, target, face_send.at[at], face_recv.at[at])
            )
        return messages

    def relays(first, last, slot, ref, reach):
        view = ref.at[first:last]
        entries = [((0, 0, 0), own)]
        entries += [(opposite(step), target) for step, _, target in regions(brick, margins, reach)]
        return [
            Relay(place, step, view, lanes, span, peer_send.at[slot, n], peer_recv.at[slot, n])
            for n, (step, span) in enumerate(entries)
        ]

    pl.semaphore_wait(barrier, greetings)
    messages = faces(0)
    pending = list(messages)
    for message in messages:
        message.start()
    loads[2].wait()
    loads[3].wait()
    bulk, forward = [], []
    for slot, (first, last, reach) in enumerate(((3, 4, HALO), (0, 1, HALO - 1), (1, 2, HALO - 1), (2, 3, HALO - 1))):
        bulk.append(
            spread_messages(
                place,
                brick,
                margins,
                zone_w.at[first:last],
                lanes,
                bulk_send.at[slot],
                bulk_recv.at[slot],
                reach,
            )
        )
        forward.append(relays(first, last, slot, zone_w, reach))

    def around(sweep, k, x, u):
        low, high = rows_in[sweep, 0, k, pl.ds(x, 1), :], rows_in[sweep, 1, k, pl.ds(x, 1), :]
        y_up = jnp.where(row == by - 1, jnp.broadcast_to(high, u.shape), roll(u, -1, 0))
        y_down = jnp.where(row == 0, jnp.broadcast_to(low, u.shape), roll(u, 1, 0))
        below, above = sides[sweep][0, k, x], sides[sweep][1, k, x]
        z_up = jnp.where(lane == bz - 1, roll(above, -1, 1), roll(u, -1, 1))
        z_down = jnp.where(lane == 0, roll(below, 1, 1), roll(u, 1, 1))
        field = fields[sweep]
        return field[k, x + 2], field[k, x], y_up, y_down, z_up, z_down

    def couple(x, _):
        m = fields[0][3, x + 1]
        below = MASS_TERM
        for n, other in enumerate(around(0, 3, x, m)):
            face = 0.5 * (m + other)
            coupling[n, x] = face
            below = below + face
        inverse[x] = 1.0 / below
        return 0

    for sweep in range(FSWEEPS):
        for message in bulk[sweep]:
            message.start()
        forward[sweep][0].start()
        for message in messages:
            message.arrived()
        if sweep == 0:
            lax.fori_loop(0, bx, couple, 0)

        def relax(x, _, sweep=sweep):
            weights = [coupling[n, x] for n in range(6)]
            scale = inverse[x]
            for k in range(3):
                u = fields[sweep][k, x + 1]
                total = zone_w[k, hx + x, hy : hy + by, lanes]
                for weight, other in zip(weights, around(sweep, k, x, u)):
                    total = total + weight * other
                total = total * scale
                if sweep < FSWEEPS - 1:
                    fields[sweep + 1][k, x + 1] = total
                    rows_out[sweep + 1, 0, k, pl.ds(x, 1), :] = total[:1]
                    rows_out[sweep + 1, 1, k, pl.ds(x, 1), :] = total[by - 1 :]
                else:
                    zone_u[k, hx + x, hy : hy + by, lanes] = total
            return 0

        lax.fori_loop(0, bx, relax, 0)
        if sweep < FSWEEPS - 1:
            messages = faces(sweep + 1)
            pending += messages
            for message in messages:
                message.start()
    final = spread_messages(
        place, brick, margins, zone_u, lanes, bulk_send.at[4], bulk_recv.at[4], HALO
    )
    for message in final:
        message.start()
    forward.append(relays(0, 3, 4, zone_u, HALO))
    forward[4][0].start()
    bulk.append(final)
    for group, onward in zip(bulk, forward):
        for message, relay in zip(group, onward[1:]):
            message.arrived()
            relay.start()
    for message in pending + sum(bulk, []):
        message.sent()
    for relay in sum(forward, []):
        relay.wait()


def gather_kernel(counts, brick, margins, added, modulus, out, total, from_peer, *scratch):
    from_x, from_y, from_xy, send, recv, peer_send, peer_recv = scratch
    place = Place(counts)
    bx, by, bz = brick
    hx, hy = margins

    def part(turn):
        at = lax.rem(place.here[2] + turn, counts[2])
        return pl.ds(pl.multiple_of(at * bz, bz), bz)

    targets = {}
    for n, (dx, dy) in enumerate(AROUND):
        if dy == 0:
            targets[n] = from_x.at[(dx + 1) // 2]
        elif dx == 0:
            targets[n] = from_y.at[(dy + 1) // 2]
        else:
            targets[n] = from_xy.at[dx + 1 + (dy + 1) // 2]

    barrier, greetings = place.call()
    for n, (dx, dy) in enumerate(AROUND):

        @pl.when(jnp.logical_not(place.exists((-dx, -dy, 0))))
        def _():
            targets[n][...] = jnp.zeros(targets[n].shape, F32)

    pl.semaphore_wait(barrier, greetings)
    copies = [
        pltpu.make_async_remote_copy(
            src_ref=added.at[:, :, part(turn)],
            dst_ref=from_peer.at[turn - 1],
            send_sem=peer_send.at[turn - 1],
            recv_sem=peer_recv.at[turn - 1],
            device_id=tuple(place.peer(turn)),
            device_id_type=MESH_ID,
        )
        for turn in range(1, counts[2])
    ]
    for copy in copies:
        copy.start()
    for copy in copies:
        copy.wait_recv()

    def collect(x, _):
        value = added[x, :, part(0)]
        for turn in range(1, counts[2]):
            value = value + from_peer[turn - 1, x]
        total[x] = value
        return 0

    lax.fori_loop(0, total.shape[0], collect, 0)
    messages = []
    for n, (dx, dy) in enumerate(AROUND):
        _, at_x = edge_span(-dx, bx, hx, HALO - 1)
        _, at_y = edge_span(-dy, by, hy, HALO - 1)
        messages.append(
            Message(place, (dx, dy, 0), total.at[at_x, at_y], targets[n], send.at[n], recv.at[n])
        )
    for message in messages:
        message.start()

    def centre(x, _):
        out[x] = modulus[x] + total[hx + x, hy : hy + by, :]
        return 0

    lax.fori_loop(0, bx, centre, 0)
    for message in messages:
        message.arrived()
    for n, (dx, dy) in enumerate(AROUND):
        to_x, _ = edge_span(-dx, bx, hx, HALO - 1)
        to_y, _ = edge_span(-dy, by, hy, HALO - 1)
        out[to_x.start - hx : to_x.stop - hx, to_y.start - hy : to_y.stop - hy, :] += targets[n][...]
    for message in messages:
        message.sent()
    for copy in copies:
        copy.wait_send()


FIELDS = 8


def coarse_fields(zone_u, zone_f, zone_m, temp, fields):
    rows = zone_m.shape[1]
    first_y = iota((rows, 128), 0) % 2 == 1
    first_z = iota((rows, 128), 1) % 2 == 1
    rank = iota((PC, 128), 0)
    lane = iota((PC, 128), 1)
    for x in range(PC):
        for k in range(3):
            sums = [None] * FIELDS

            def put(number, value):
                sums[number] = value if sums[number] is None else sums[number] + value

            for a in range(2):
                at = 2 * x + 1 + a
                u, m = zone_u[k, at], zone_m[at]
                applied = MASS_TERM * u
                laplace = jnp.zeros_like(u)
                for number, (axis, step) in enumerate(
                    ((0, 1), (0, -1), (1, 1), (1, -1), (2, 1), (2, -1))
                ):
                    if axis == 0:
                        u_next, m_next = zone_u[k, at + step], zone_m[at + step]
                    else:
                        u_next, m_next = roll(u, -step, axis - 1), roll(m, -step, axis - 1)
                    change = u - u_next
                    applied = applied + 0.5 * (m + m_next) * change
                    laplace = laplace + change
                    flow = -0.5 * m_next * change
                    if axis == 0:
                        same = (a == 0) == (step == 1)
                        put(0 if same else 1 + number, flow)
                    else:
                        first = first_y if axis == 1 else first_z
                        near = first if step == 1 else ~first
                        put(0, jnp.where(near, flow, 0.0))
                        put(1 + number, jnp.where(near, 0.0, flow))
                put(0, -0.5 * m * laplace)
                put(7, zone_f[k, at] - applied)
            for number in range(FIELDS):
                slot = temp.at[k * FIELDS + number]
                slot[...] = sums[number]
                pair = slot[pl.ds(1, PC, stride=2), :] + slot[pl.ds(2, PC, stride=2), :]
                pair = pair + roll(pair, -1, 1)
                keep = (lane % 2 == 1) & (lane < 2 * PC)
                if number == 1 and x == PC - 1 or number == 2 and x == 0:
                    keep = jnp.zeros_like(keep)
                if number == 3:
                    keep = keep & (rank < PC - 1)
                if number == 4:
                    keep = keep & (rank > 0)
                if number == 5:
                    keep = keep & (lane < 2 * PC - 2)
                if number == 6:
                    keep = keep & (lane > 1)
                fields[k * FIELDS + number, x * PC : (x + 1) * PC, :] = jnp.where(keep, pair, 0.0)


PAIRS = ((0, 0, 0), (1, 0, 0), (-1, 0, 0), (0, 1, 0), (0, -1, 0), (0, 0, 1), (0, 0, -1))
BANDS = tuple(
    sorted({tuple(b - a for a, b in zip(one, two)) for one in PAIRS for two in PAIRS})
)
PER_GROUP = 12


def transpose_fields(fields, packed, flat):
    size = fields.shape[1]
    flat[...] = jnp.zeros_like(flat)
    for group in range(2):
        total = None
        for j in range(PER_GROUP):
            shift = 2 * PC * (j // 2) - 1 + j % 2
            part = fields[group * PER_GROUP + j]
            part = roll(part, shift, 1) if shift else part
            total = part if total is None else total + part
        packed[:size, :] = total
        packed[size:, :] = jnp.zeros((128 - size, 128), F32)
        packed[...] = packed[...].T
        for j in range(PER_GROUP):
            first = 2 * PC * (j // 2) + j % 2
            flat[group * PER_GROUP + j, :PC, :] = packed[pl.ds(first, PC, stride=2), :]


def band_sums(flat, packed, bands, slopes):
    columns = [[flat[k * FIELDS + n] for k in range(3)] for n in range(FIELDS)]

    def product(a, b):
        return sum(columns[a][k] * columns[b][k] for k in range(3))

    def moved(value, step):
        x, y, z = step
        value = roll(value, PC * x + y, 1) if x or y else value
        return roll(value, z, 0) if z else value

    totals = {}
    trace = None
    for a in range(len(PAIRS)):
        for b in range(a, len(PAIRS)):
            value = product(a, b)
            if a == b:
                trace = value if trace is None else trace + value
            for one, two in {(a, b), (b, a)}:
                key = tuple(q - p for p, q in zip(PAIRS[one], PAIRS[two]))
                part = moved(value, PAIRS[two])
                totals[key] = part if key not in totals else totals[key] + part
    trace = jnp.sum(jnp.sum(trace, axis=0, keepdims=True), axis=1, keepdims=True)
    ridge = DAMPING * trace / PC**3 + EPSILON
    totals[0, 0, 0] = totals[0, 0, 0] + ridge
    for n, key in enumerate(BANDS):
        bands[n] = totals[key]
    slope = None
    for a in range(len(PAIRS)):
        part = moved(product(a, FIELDS - 1), PAIRS[a])
        slope = part if slope is None else slope + part
    packed[...] = jnp.zeros_like(packed)
    packed[: slope.shape[0], :] = slope
    slopes[...] = packed[...].T


def fill(c, t, z, bands, slopes, mat, side, reach):
    params = PC * PC
    lane = iota((8, 128), 1)
    gap = lane - iota((8, 128), 0)
    column = pltpu.roll(slopes[...], params - z, 1)
    ahead = 1 if c == 0 else -1

    def rows_of(depth):
        found = []
        for n, (x, y, dz) in enumerate(BANDS):
            if dz == depth * ahead:
                row = bands[n, pl.ds(z + depth * ahead, 1), :]
                found.append((PC * x + y, jnp.broadcast_to(row, (8, 128))))
        return found

    parts = [rows_of(depth) for depth in range(reach + 1)]
    for q in range(-(-params // 8)):
        here = slice(8 * q, 8 * q + 8)
        inside = lane < params

        def block(entries):
            value = jnp.zeros((8, 128), F32)
            for offset, row in entries:
                value = jnp.where(gap == 8 * q + offset, row, value)
            return jnp.where(inside, value, 0.0)

        mat[c, t, here, :] = block(parts[0])
        first = block(parts[1]) if reach > 0 else jnp.zeros((8, 128), F32)
        side[c, t, here, 0:128] = jnp.where(lane == params, column[here], first)
        if reach > 1:
            side[c, t, here, 128:256] = block(parts[2])


def assemble(bands, slopes, mat, side):
    meet = PC // 2 - 1
    mat[...] = jnp.zeros_like(mat)
    side[...] = jnp.zeros_like(side)

    def both(t, _):
        fill(0, t, t, bands, slopes, mat, side, 2)
        fill(1, t, PC - 1 - t, bands, slopes, mat, side, 2)
        return 0

    lax.fori_loop(0, meet, both, 0)
    fill(0, meet, meet, bands, slopes, mat, side, 1)
    fill(0, meet + 1, meet + 1, bands, slopes, mat, side, 0)


def factored(blocks, count):
    lane = iota((8, 128), 1)
    sub = iota((8, 128), 0)
    tiles = -(-count // 8)

    def over_lanes(value, at):
        return jnp.broadcast_to(value[:, at : at + 1], value.shape)

    def over_rows(value, at):
        return jnp.broadcast_to(value[at : at + 1, :], value.shape)

    grids = [[block[8 * q : 8 * q + 8] for q in range(tiles)] for block in blocks]
    lower = [[] for _ in blocks]
    scaled = [[] for _ in blocks]
    for p in range(tiles):
        pivots = range(8 * p, min(8 * p + 8, count))
        within = (lane >= pivots[0]) & (lane <= pivots[-1])
        keep = (lane <= pivots[-1]) & (sub < len(pivots))
        for grid, low, high in zip(grids, lower, scaled):
            panel = grid[p]
            unit = jnp.where(lane - 8 * p == sub, 1.0, 0.0)
            low.append(jnp.where(keep, jnp.where(within, unit, panel), 0.0))
            columns = [over_lanes(panel, j) for j in pivots]
            for i, j in enumerate(pivots):
                column = columns[i]
                pivot = 1.0 / over_rows(column, i)
                row = jnp.where(lane == j, pivot, over_rows(panel, i) * pivot)
                for n in range(i + 1, len(pivots)):
                    crossing = over_rows(columns[n], i) * pivot
                    columns[n] = jnp.where(sub == i, crossing, columns[n] - column * crossing)
                cleared = jnp.where(lane == j, 0.0, panel)
                panel = jnp.where(sub == i, row, cleared - column * row)
            high.append(jnp.where(keep, panel, 0.0))
            rows = [over_rows(panel, i) for i in range(len(pivots))]
            for q in range(p + 1, tiles):
                old = grid[q]
                terms = [over_lanes(old, j) * row for j, row in zip(pivots, rows)]
                while len(terms) > 1:
                    pairs = [terms[n] + terms[n + 1] for n in range(0, len(terms) - 1, 2)]
                    terms = pairs + terms[len(terms) - len(terms) % 2 :]
                grid[q] = jnp.where(within, 0.0, old) - terms[0]
    return [
        (jnp.concatenate(low, axis=0), jnp.concatenate(high, axis=0))
        for low, high in zip(lower, scaled)
    ]


def eliminate(t, chains, size, mat, side, lowers, solved, more=True):
    params = PC * PC
    mark = iota((128, 128), 1) == params
    blocks = [mat[c, t, :size, :] for c in chains]
    for c, (low, high) in zip(chains, factored(blocks, params)):
        lowers[c, t, :size, :] = low
        right = side[c, t, :size, :]
        z = dot(high[:, :size], right, (1, 0))
        solved[c, t, :size, :] = z
        if not more:
            continue
        y = dot(low[:, :size], right, (1, 0))
        schur = dot(y, z, (0, 0))
        near, far = schur[:128], schur[128:]
        mat[c, t + 1] -= near[:, :128]
        side[c, t + 1, :, 0:128] -= jnp.where(mark, near[:, :128], near[:, 128:])
        mat[c, t + 2] -= far[:, 128:]
        side[c, t + 2, :, 0:128] -= jnp.where(mark, far[:, :128], 0.0)


def solve_zone(size, mat, side, lowers, solved, spread):
    params = PC * PC
    meet = PC // 2 - 1
    mark = iota((128, 128), 1) == params
    lowers[...] = jnp.zeros_like(lowers)
    solved[...] = jnp.zeros_like(solved)

    def both(t, _):
        eliminate(t, (0, 1), size, mat, side, lowers, solved)
        return 0

    lax.fori_loop(0, meet, both, 0)
    mat[0, meet] += mat[1, meet + 1]
    mat[0, meet + 1] += mat[1, meet]
    turned = side[1, meet, :, 0:128].T
    side[0, meet, :, 0:128] += jnp.where(mark, side[1, meet + 1, :, 0:128], turned)
    side[0, meet + 1, :, 0:128] += jnp.where(mark, side[1, meet, :, 0:128], 0.0)
    eliminate(meet, (0,), size, mat, side, lowers, solved)
    eliminate(meet + 1, (0,), size, mat, side, lowers, solved, more=False)

    flag = iota((8, 128), 1) == params

    def back(c, t, near, far):
        row = jnp.concatenate([jnp.where(flag, -1.0, near), far], axis=1)
        value = dot(row, solved[c, t], (1, 1))
        return -dot(value, lowers[c, t], (1, 0))

    blank = jnp.zeros((8, 128), F32)
    rows = [blank] * PC
    rows[meet + 1] = back(0, meet + 1, blank, blank)
    rows[meet] = back(0, meet, rows[meet + 1], blank)
    for t in range(meet - 1, -1, -1):
        rows[t] = back(0, t, rows[t + 1], rows[t + 2])
        z = PC - 1 - t
        rows[z] = back(1, t, rows[z - 1], rows[z - 2])
    spread[...] = jnp.zeros_like(spread)
    for z in range(PC):
        spread[2 * z + 1 : 2 * z + 3, :] = -rows[z][:2]
    spread[...] = spread[...].T


def place_zone(begin, zone_m, spread, temp, added):
    rows = zone_m.shape[1]
    span = 2 * PC

    def ramp(position):
        value = jnp.sin(math.pi * (position.astype(F32) - 0.5) / span)
        return jnp.where((position >= 1) & (position <= span), value, 0.0)

    weight = ramp(iota((rows, 128), 0)) * ramp(iota((rows, 128), 1))
    temp[0] = jnp.zeros_like(weight)
    shift = lax.rem(begin[2] + added.shape[2], added.shape[2])
    for x in range(PC):
        part = spread[x * PC : (x + 1) * PC, :]
        temp[0, pl.ds(1, PC, stride=2), :] = part
        temp[0, pl.ds(2, PC, stride=2), :] = part
        value = weight * temp[0]
        for a in range(2):
            at = 2 * x + 1 + a
            plane = value * math.sin(math.pi * (at - 0.5) / span) * zone_m[at]
            plane = jnp.pad(plane, ((0, added.shape[1] - rows), (0, 0)))
            plane = pltpu.roll(plane, begin[1], 0)
            plane = jnp.pad(plane, ((0, 0), (0, added.shape[2] - 128)))
            added[begin[0] + at] += pltpu.roll(plane, shift, 1)


def cut_zone(begin, depth, zone_all_u, zone_all_w, zone_u, zone_f, zone_m):
    count, rows = zone_m.shape[:2]
    whole_rows, whole_lanes = zone_all_u.shape[-2:]
    shift = lax.rem(whole_lanes - begin[2], whole_lanes)
    shift_y = lax.rem(whole_rows - begin[1], whole_rows)
    z = begin[2] + iota((rows, 128), 1)
    inside = (z >= 0) & (z < depth) & (iota((rows, 128), 0) < count)

    def cut(x, _):
        def take(ref, k):
            plane = pltpu.roll(ref[k, begin[0] + x], shift, 1)[:, :128]
            return jnp.where(inside, pltpu.roll(plane, shift_y, 0)[:rows], 0.0)

        for k in range(3):
            zone_u[k, x] = take(zone_all_u, k)
            zone_f[k, x] = take(zone_all_w, k)
        zone_m[x] = take(zone_all_w, 3)
        return 0

    lax.fori_loop(0, count, cut, 0)


def zone_kernel(counts, brick, margins, where, zone_all_u, zone_all_w, field_out, added, *scratch):
    scratch, (corners, ready) = scratch[:-2], scratch[-2:]
    zone_u, zone_f, zone_m = scratch[:3]
    temp, fields, packed, flat, bands, slopes, mat, side, lowers, solved, spread = scratch[3:]
    bx, by, bz = brick
    hx, hy = margins
    here = [lax.axis_index(name) for name in AXES]
    lanes = pl.ds(pl.multiple_of(here[2] * bz, bz), bz)
    fetch = pltpu.make_async_copy(where, corners, ready.at[0])
    fetch.start()
    inner = zone_all_u.at[:, hx : hx + bx, hy : hy + by, lanes]
    store = pltpu.make_async_copy(inner, field_out, ready.at[1])
    store.start()
    added[...] = jnp.zeros_like(added)
    fetch.wait()
    for number in range(corners.shape[0]):
        begin = [
            corners[number, 0] - here[0] * bx + hx - 1,
            corners[number, 1] - here[1] * by + hy - 1,
            corners[number, 2] - 1,
        ]
        cut_zone(begin, counts[2] * bz, zone_all_u, zone_all_w, zone_u, zone_f, zone_m)
        fields[...] = jnp.zeros_like(fields)
        coarse_fields(zone_u, zone_f, zone_m, temp, fields)
        transpose_fields(fields, packed, flat)
        band_sums(flat, packed, bands, slopes)
        assemble(bands, slopes, mat, side)
        solve_zone(fields.shape[1], mat, side, lowers, solved, spread)
        place_zone(begin, zone_m, spread, temp, added)
    store.wait()


def body(forcing, start_field, modulus, corners):
    brick = modulus.shape
    bx, by, bz = brick
    counts = [lax.axis_size(name) for name in AXES]
    margins = (HALO, -(-HALO // 8) * 8)
    span = [size + 2 * margin for size, margin in zip(brick, margins)] + [counts[2] * bz]
    whole = pl.BlockSpec(memory_space=pltpu.VMEM)
    dma = pltpu.SemaphoreType.DMA
    peers = max(counts[2] - 1, 1)
    zone_all_u, zone_all_w = pl.pallas_call(
        functools.partial(sweep_kernel, counts, brick, margins),
        out_shape=(
            jax.ShapeDtypeStruct((3, *span), F32),
            jax.ShapeDtypeStruct((4, *span), F32),
        ),
        in_specs=[pl.BlockSpec(memory_space=pltpu.HBM)] * 3,
        out_specs=(whole, whole),
        scratch_shapes=[
            pltpu.VMEM((4, bx + 2, by, bz), F32),
            *[pltpu.VMEM((3, bx + 2, by, bz), F32)] * (FSWEEPS - 1),
            pltpu.VMEM((FSWEEPS, 2, 4, bx, bz), F32),
            pltpu.VMEM((FSWEEPS, 2, 4, bx, bz), F32),
            pltpu.VMEM((2, 4, bx, by, bz), F32),
            *[pltpu.VMEM((2, 3, bx, by, bz), F32)] * (FSWEEPS - 1),
            pltpu.VMEM((6, bx, by, bz), F32),
            pltpu.VMEM((bx, by, bz), F32),
            dma((FSWEEPS, len(FACES))),
            dma((FSWEEPS, len(FACES))),
            dma((5, len(AROUND))),
            dma((5, len(AROUND))),
            dma((5, len(AROUND) + 1, peers)),
            dma((5, len(AROUND) + 1, peers)),
            dma((4,)),
        ],
        compiler_params=pltpu.CompilerParams(
            collective_id=0, has_side_effects=True, vmem_limit_bytes=40 * 1024 * 1024
        ),
        name="sweeps",
    )(*[pltpu.with_memory_space_constraint(each, pltpu.HBM) for each in (forcing, start_field, modulus)])
    zone_span = 2 * PC + 2
    zone_rows = -(-zone_span // 8) * 8
    size = -(-PC * PC // 8) * 8
    planes = PC // 2 + 3
    field, added = pl.pallas_call(
        functools.partial(zone_kernel, counts, brick, margins),
        out_shape=(
            jax.ShapeDtypeStruct(forcing.shape, F32),
            jax.ShapeDtypeStruct(tuple(span), F32),
        ),
        in_specs=[pl.BlockSpec(memory_space=pltpu.HBM), whole, whole],
        out_specs=(pl.BlockSpec(memory_space=pl.ANY), whole),
        scratch_shapes=[
            pltpu.VMEM((3, zone_span, zone_rows, 128), F32),
            pltpu.VMEM((3, zone_span, zone_rows, 128), F32),
            pltpu.VMEM((zone_span, zone_rows, 128), F32),
            pltpu.VMEM((3 * FIELDS, zone_rows, 128), F32),
            pltpu.VMEM((3 * FIELDS, size, 128), F32),
            pltpu.VMEM((128, 128), F32),
            pltpu.VMEM((3 * FIELDS, 16, 128), F32),
            pltpu.VMEM((len(BANDS), 16, 128), F32),
            pltpu.VMEM((128, 128), F32),
            pltpu.VMEM((2, planes, 128, 128), F32),
            pltpu.VMEM((2, planes, 128, 256), F32),
            pltpu.VMEM((2, planes, 128, 128), F32),
            pltpu.VMEM((2, planes, 128, 256), F32),
            pltpu.VMEM((128, 128), F32),
            pltpu.SMEM(corners.shape, jnp.int32),
            dma((2,)),
        ],
        compiler_params=pltpu.CompilerParams(vmem_limit_bytes=40 * 1024 * 1024),
        name="zone",
    )(pltpu.with_memory_space_constraint(corners, pltpu.HBM), zone_all_u, zone_all_w)
    updated = pl.pallas_call(
        functools.partial(gather_kernel, counts, brick, margins),
        out_shape=jax.ShapeDtypeStruct(brick, F32),
        in_specs=[whole, whole],
        out_specs=whole,
        scratch_shapes=[
            pltpu.VMEM((span[0], span[1], bz), F32),
            pltpu.VMEM((peers, span[0], span[1], bz), F32),
            pltpu.VMEM((2, HALO - 1, by, bz), F32),
            pltpu.VMEM((2, bx, HALO - 1, bz), F32),
            pltpu.VMEM((4, HALO - 1, HALO - 1, bz), F32),
            dma((len(AROUND),)),
            dma((len(AROUND),)),
            dma((peers,)),
            dma((peers,)),
        ],
        compiler_params=pltpu.CompilerParams(
            collective_id=1, has_side_effects=True, vmem_limit_bytes=40 * 1024 * 1024
        ),
        name="gather",
    )(added, modulus)
    return (field, updated)


def solution(mesh):
    placed = (
        P(None, "gx", "gy", "gz"),
        P(None, "gx", "gy", "gz"),
        P("gx", "gy", "gz"),
        P(("gx", "gy", "gz"), None),
    )
    return jax.shard_map(
        body,
        mesh=mesh,
        in_specs=placed,
        out_specs=(P(None, "gx", "gy", "gz"), P("gx", "gy", "gz")),
        check_vma=False,
    )
```

```python
import functools
import math

import jax
import jax.numpy as jnp
from jax import lax
from jax.experimental import pallas as pl
from jax.experimental.pallas import tpu as pltpu
from jax.sharding import PartitionSpec as P

PC = 10
HALO = 6
FSWEEPS = 4


MASS_TERM = 0.5
DAMPING = 0.1
EPSILON = 1e-06
HIGHEST = lax.Precision.HIGHEST
F32 = jnp.float32


def dot(a, b, contract, precision=lax.Precision.HIGH):
    return lax.dot_general(
        a, b, ((contract[:1], contract[1:]), ((), ())), precision=precision, preferred_element_type=F32
    )


def roll(values, shift, axis):
    return pltpu.roll(values, shift % values.shape[axis], axis)


def iota(shape, axis):
    return lax.broadcasted_iota(jnp.int32, shape, axis)


MESH_ID = pl.DeviceIdType.MESH
AXES = ("gx", "gy", "gz")
AROUND = tuple((dx, dy) for dx in (-1, 0, 1) for dy in (-1, 0, 1) if (dx, dy) != (0, 0))
FACES = ((-1, 0, 0), (1, 0, 0), (0, -1, 0), (0, 1, 0), (0, 0, -1), (0, 0, 1))


class Place:
    def __init__(self, counts):
        self.counts = counts
        self.here = [lax.axis_index(name) for name in AXES]

    def exists(self, step):
        inside = None
        for at, count, move in zip(self.here, self.counts, step):
            if move:
                test = at + move < count if move > 0 else at + move >= 0
                inside = test if inside is None else inside & test
        return inside

    def device(self, step):
        return tuple(at + move for at, move in zip(self.here, step))

    def peer(self, turn):
        return self.here[:2] + [lax.rem(self.here[2] + turn, self.counts[2])]

    def call(self):
        barrier = pltpu.get_barrier_semaphore()
        total = self.counts[2] - 1
        for dx, dy in AROUND:
            step = (dx, dy, 0)

            @pl.when(self.exists(step))
            def _():
                pl.semaphore_signal(
                    barrier, inc=1, device_id=self.device(step), device_id_type=MESH_ID
                )

            total = total + self.exists(step).astype(jnp.int32)
        for turn in range(1, self.counts[2]):
            pl.semaphore_signal(
                barrier, inc=1, device_id=tuple(self.peer(turn)), device_id_type=MESH_ID
            )
        return barrier, total


def opposite(step):
    return tuple(-move for move in step)


class Message:
    def __init__(self, place, step, source, target, send, recv):
        self.place, self.step = place, step
        self.copy = pltpu.make_async_remote_copy(
            src_ref=source,
            dst_ref=target,
            send_sem=send,
            recv_sem=recv,
            device_id=place.device(step),
            device_id_type=MESH_ID,
        )

    def start(self):
        pl.when(self.place.exists(self.step))(self.copy.start)

    def sent(self):
        pl.when(self.place.exists(self.step))(self.copy.wait_send)

    def arrived(self):
        pl.when(self.place.exists(opposite(self.step)))(self.copy.wait_recv)


def edge_span(move, size, margin, reach=None):
    reach = margin if reach is None else reach
    if move > 0:
        return slice(margin + size - reach, margin + size), slice(margin - reach, margin)
    if move < 0:
        far = margin + size
        return slice(margin, margin + reach), slice(far, far + reach)
    return slice(margin, margin + size), slice(margin, margin + size)


def regions(brick, margins, reach):
    found = []
    for dx, dy in AROUND:
        from_x, to_x = edge_span(dx, brick[0], margins[0], reach)
        from_y, to_y = edge_span(dy, brick[1], margins[1], reach)
        found.append(((dx, dy, 0), (from_x, from_y), (to_x, to_y)))
    return sorted(found, key=lambda entry: (entry[0][1] == 0, entry[0][0] != 0))


def spread_messages(place, brick, margins, ref, lanes, send, recv, reach):
    return [
        Message(
            place,
            step,
            ref.at[:, source[0], source[1], lanes],
            ref.at[:, target[0], target[1], lanes],
            send.at[n],
            recv.at[n],
        )
        for n, (step, source, target) in enumerate(regions(brick, margins, reach))
    ]


class Relay:
    def __init__(self, place, step, ref, lanes, span, send, recv):
        self.place, self.step = place, step
        view = ref.at[:, span[0], span[1], lanes]
        self.copies = [
            pltpu.make_async_remote_copy(
                src_ref=view,
                dst_ref=view,
                send_sem=send.at[turn - 1],
                recv_sem=recv.at[turn - 1],
                device_id=tuple(place.peer(turn)),
                device_id_type=MESH_ID,
            )
            for turn in range(1, place.counts[2])
        ]

    def when(self, action):
        test = self.place.exists(self.step) if any(self.step) else None
        action() if test is None else pl.when(test)(action)

    def start(self):
        self.when(lambda: [copy.start() for copy in self.copies] and None)

    def wait(self):
        self.when(lambda: [copy.wait() for copy in self.copies] and None)


def clear_outside(place, brick, margins, refs, lanes):
    for dx, dy in AROUND:
        _, to_x = edge_span(-dx, brick[0], margins[0])
        _, to_y = edge_span(-dy, brick[1], margins[1])

        @pl.when(jnp.logical_not(place.exists((dx, dy, 0))))
        def _():
            for ref in refs:
                for k in range(ref.shape[0]):
                    shape = (to_x.stop - to_x.start, to_y.stop - to_y.start, lanes.size)
                    ref[k, to_x, to_y, lanes] = jnp.zeros(shape, F32)


def sweep_kernel(counts, brick, margins, forcing, start, modulus, zone_u, zone_w, *scratch):
    fields, rows_in, rows_out, sides = scratch[0:4], scratch[4], scratch[5], scratch[6:10]
    coupling, inverse = scratch[10:12]
    face_send, face_recv, bulk_send, bulk_recv, peer_send, peer_recv, load = scratch[12:]
    place = Place(counts)
    bx, by, bz = brick
    hx, hy = margins
    lanes = pl.ds(pl.multiple_of(place.here[2] * bz, bz), bz)
    every = pl.ds(0, counts[2] * bz)
    row = iota((by, bz), 0)
    lane = iota((by, bz), 1)
    own = (slice(hx, hx + bx), slice(hy, hy + by))
    loads = [
        pltpu.make_async_copy(start, fields[0].at[:3, 1 : bx + 1], load.at[0]),
        pltpu.make_async_copy(modulus, fields[0].at[3, 1 : bx + 1], load.at[1]),
        pltpu.make_async_copy(modulus, zone_w.at[3, own[0], own[1], lanes], load.at[2]),
        pltpu.make_async_copy(forcing, zone_w.at[:3, own[0], own[1], lanes], load.at[3]),
    ]
    for copy in loads:
        copy.start()
    barrier, greetings = place.call()

    clear_outside(place, brick, margins, (zone_u, zone_w), every)
    for n, (dx, dy, dz) in enumerate(FACES):

        @pl.when(jnp.logical_not(place.exists((dx, dy, dz))))
        def _():
            for sweep in range(FSWEEPS):
                if dx:
                    plane = 0 if dx < 0 else bx + 1
                    for k in range(fields[sweep].shape[0]):
                        fields[sweep][k, plane] = jnp.zeros((by, bz), F32)
                elif dy:
                    for k in range(4):
                        rows_in[sweep, 0 if dy < 0 else 1, k] = jnp.zeros((bx, bz), F32)
                else:
                    for k in range(sides[sweep].shape[1]):
                        blank = jnp.zeros((bx, by, bz), F32)
                        sides[sweep][0 if dz < 0 else 1, k] = blank

    loads[0].wait()
    loads[1].wait()

    def stage(x, _):
        for k in range(4):
            u = fields[0][k, x + 1]
            rows_out[0, 0, k, pl.ds(x, 1), :] = u[:1]
            rows_out[0, 1, k, pl.ds(x, 1), :] = u[by - 1 :]
        return 0

    lax.fori_loop(0, bx, stage, 0)

    def faces(sweep, k):
        field = fields[sweep]
        messages = []
        for n, step in enumerate(FACES):
            dx, dy, dz = step
            if dx:
                source = field.at[k, bx if dx > 0 else 1]
                target = field.at[k, 0 if dx > 0 else bx + 1]
            elif dy:
                source = rows_out.at[sweep, 1 if dy > 0 else 0, k]
                target = rows_in.at[sweep, 0 if dy > 0 else 1, k]
            else:
                source = field.at[k, 1 : bx + 1]
                target = sides[sweep].at[0 if dz > 0 else 1, k]
            at = (sweep, k, n)
            messages.append(
                Message(place, step, source, target, face_send.at[at], face_recv.at[at])
            )
        return messages

    def relays(first, last, slot, ref, reach):
        view = ref.at[first:last]
        entries = [((0, 0, 0), own)]
        entries += [(opposite(step), target) for step, _, target in regions(brick, margins, reach)]
        return [
            Relay(place, step, view, lanes, span, peer_send.at[slot, n], peer_recv.at[slot, n])
            for n, (step, span) in enumerate(entries)
        ]

    pl.semaphore_wait(barrier, greetings)
    waiting = {(0, k): faces(0, k) for k in (3, 0, 1, 2)}
    pending = sum(waiting.values(), [])
    for message in pending:
        message.start()
    loads[2].wait()
    loads[3].wait()
    bulk, forward = [], []
    for slot, (first, last, reach) in enumerate(((3, 4, HALO), (0, 1, HALO - 1), (1, 2, HALO - 1), (2, 3, HALO - 1))):
        bulk.append(
            spread_messages(
                place,
                brick,
                margins,
                zone_w.at[first:last],
                lanes,
                bulk_send.at[slot],
                bulk_recv.at[slot],
                reach,
            )
        )
        forward.append(relays(first, last, slot, zone_w, reach))

    def around(sweep, k, x, u):
        low, high = rows_in[sweep, 0, k, pl.ds(x, 1), :], rows_in[sweep, 1, k, pl.ds(x, 1), :]
        y_up = jnp.where(row == by - 1, jnp.broadcast_to(high, u.shape), roll(u, -1, 0))
        y_down = jnp.where(row == 0, jnp.broadcast_to(low, u.shape), roll(u, 1, 0))
        below, above = sides[sweep][0, k, x], sides[sweep][1, k, x]
        z_up = jnp.where(lane == bz - 1, roll(above, -1, 1), roll(u, -1, 1))
        z_down = jnp.where(lane == 0, roll(below, 1, 1), roll(u, 1, 1))
        field = fields[sweep]
        return field[k, x + 2], field[k, x], y_up, y_down, z_up, z_down

    def couple(x, _):
        m = fields[0][3, x + 1]
        below = MASS_TERM
        for n, other in enumerate(around(0, 3, x, m)):
            face = 0.5 * (m + other)
            coupling[n, x] = face
            below = below + face
        inverse[x] = 1.0 / below
        return 0

    for sweep in range(FSWEEPS):
        for message in bulk[sweep]:
            message.start()
        forward[sweep][0].start()
        if sweep == 0:
            for message in waiting[0, 3]:
                message.arrived()
            lax.fori_loop(0, bx, couple, 0)
        for k in range(3):
            for message in waiting[sweep, k]:
                message.arrived()

            def relax(x, _, sweep=sweep, k=k):
                u = fields[sweep][k, x + 1]
                total = zone_w[k, hx + x, hy : hy + by, lanes]
                for n, other in enumerate(around(sweep, k, x, u)):
                    total = total + coupling[n, x] * other
                total = total * inverse[x]
                if sweep < FSWEEPS - 1:
                    fields[sweep + 1][k, x + 1] = total
                    rows_out[sweep + 1, 0, k, pl.ds(x, 1), :] = total[:1]
                    rows_out[sweep + 1, 1, k, pl.ds(x, 1), :] = total[by - 1 :]
                else:
                    zone_u[k, hx + x, hy : hy + by, lanes] = total
                return 0

            lax.fori_loop(0, bx, relax, 0)
            if sweep < FSWEEPS - 1:
                waiting[sweep + 1, k] = faces(sweep + 1, k)
                pending += waiting[sweep + 1, k]
                for message in waiting[sweep + 1, k]:
                    message.start()
            else:
                slot = FSWEEPS + k
                final = spread_messages(
                    place,
                    brick,
                    margins,
                    zone_u.at[k : k + 1],
                    lanes,
                    bulk_send.at[slot],
                    bulk_recv.at[slot],
                    HALO,
                )
                for message in final:
                    message.start()
                bulk.append(final)
                forward.append(relays(k, k + 1, slot, zone_u, HALO))
                forward[slot][0].start()
    for group, onward in zip(bulk, forward):
        for message, relay in zip(group, onward[1:]):
            message.arrived()
            relay.start()
    for message in pending + sum(bulk, []):
        message.sent()
    for relay in sum(forward, []):
        relay.wait()


def gather_kernel(counts, brick, margins, added, modulus, out, total, from_peer, *scratch):
    from_x, from_y, from_xy, send, recv, peer_send, peer_recv = scratch
    place = Place(counts)
    bx, by, bz = brick
    hx, hy = margins

    def part(turn):
        at = lax.rem(place.here[2] + turn, counts[2])
        return pl.ds(pl.multiple_of(at * bz, bz), bz)

    targets = {}
    for n, (dx, dy) in enumerate(AROUND):
        if dy == 0:
            targets[n] = from_x.at[(dx + 1) // 2]
        elif dx == 0:
            targets[n] = from_y.at[(dy + 1) // 2]
        else:
            targets[n] = from_xy.at[dx + 1 + (dy + 1) // 2]

    barrier, greetings = place.call()
    for n, (dx, dy) in enumerate(AROUND):

        @pl.when(jnp.logical_not(place.exists((-dx, -dy, 0))))
        def _():
            targets[n][...] = jnp.zeros(targets[n].shape, F32)

    pl.semaphore_wait(barrier, greetings)
    copies = [
        pltpu.make_async_remote_copy(
            src_ref=added.at[:, :, part(turn)],
            dst_ref=from_peer.at[turn - 1],
            send_sem=peer_send.at[turn - 1],
            recv_sem=peer_recv.at[turn - 1],
            device_id=tuple(place.peer(turn)),
            device_id_type=MESH_ID,
        )
        for turn in range(1, counts[2])
    ]
    for copy in copies:
        copy.start()
    for copy in copies:
        copy.wait_recv()

    def collect(x, _):
        value = added[x, :, part(0)]
        for turn in range(1, counts[2]):
            value = value + from_peer[turn - 1, x]
        total[x] = value
        return 0

    lax.fori_loop(0, total.shape[0], collect, 0)
    messages = []
    for n, (dx, dy) in enumerate(AROUND):
        _, at_x = edge_span(-dx, bx, hx, HALO - 1)
        _, at_y = edge_span(-dy, by, hy, HALO - 1)
        messages.append(
            Message(place, (dx, dy, 0), total.at[at_x, at_y], targets[n], send.at[n], recv.at[n])
        )
    for message in messages:
        message.start()

    def centre(x, _):
        out[x] = modulus[x] + total[hx + x, hy : hy + by, :]
        return 0

    lax.fori_loop(0, bx, centre, 0)
    for message in messages:
        message.arrived()
    for n, (dx, dy) in enumerate(AROUND):
        to_x, _ = edge_span(-dx, bx, hx, HALO - 1)
        to_y, _ = edge_span(-dy, by, hy, HALO - 1)
        out[to_x.start - hx : to_x.stop - hx, to_y.start - hy : to_y.stop - hy, :] += targets[n][...]
    for message in messages:
        message.sent()
    for copy in copies:
        copy.wait_send()


FIELDS = 8


def coarse_fields(zone_u, zone_f, zone_m, temp, fields):
    rows = zone_m.shape[1]
    first_y = iota((rows, 128), 0) % 2 == 1
    first_z = iota((rows, 128), 1) % 2 == 1
    rank = iota((PC, 128), 0)
    lane = iota((PC, 128), 1)
    for x in range(PC):
        for k in range(3):
            sums = [None] * FIELDS

            def put(number, value):
                sums[number] = value if sums[number] is None else sums[number] + value

            for a in range(2):
                at = 2 * x + 1 + a
                u, m = zone_u[k, at], zone_m[at]
                applied = MASS_TERM * u
                laplace = jnp.zeros_like(u)
                for number, (axis, step) in enumerate(
                    ((0, 1), (0, -1), (1, 1), (1, -1), (2, 1), (2, -1))
                ):
                    if axis == 0:
                        u_next, m_next = zone_u[k, at + step], zone_m[at + step]
                    else:
                        u_next, m_next = roll(u, -step, axis - 1), roll(m, -step, axis - 1)
                    change = u - u_next
                    applied = applied + 0.5 * (m + m_next) * change
                    laplace = laplace + change
                    flow = -0.5 * m_next * change
                    if axis == 0:
                        same = (a == 0) == (step == 1)
                        put(0 if same else 1 + number, flow)
                    else:
                        first = first_y if axis == 1 else first_z
                        near = first if step == 1 else ~first
                        put(0, jnp.where(near, flow, 0.0))
                        put(1 + number, jnp.where(near, 0.0, flow))
                put(0, -0.5 * m * laplace)
                put(7, zone_f[k, at] - applied)
            for number in range(FIELDS):
                slot = temp.at[k * FIELDS + number]
                slot[...] = sums[number]
                pair = slot[pl.ds(1, PC, stride=2), :] + slot[pl.ds(2, PC, stride=2), :]
                pair = pair + roll(pair, -1, 1)
                keep = (lane % 2 == 1) & (lane < 2 * PC)
                if number == 1 and x == PC - 1 or number == 2 and x == 0:
                    keep = jnp.zeros_like(keep)
                if number == 3:
                    keep = keep & (rank < PC - 1)
                if number == 4:
                    keep = keep & (rank > 0)
                if number == 5:
                    keep = keep & (lane < 2 * PC - 2)
                if number == 6:
                    keep = keep & (lane > 1)
                fields[k * FIELDS + number, x * PC : (x + 1) * PC, :] = jnp.where(keep, pair, 0.0)


PAIRS = ((0, 0, 0), (1, 0, 0), (-1, 0, 0), (0, 1, 0), (0, -1, 0), (0, 0, 1), (0, 0, -1))
BANDS = tuple(
    sorted({tuple(b - a for a, b in zip(one, two)) for one in PAIRS for two in PAIRS})
)
PER_GROUP = 12


def transpose_fields(fields, packed, flat):
    size = fields.shape[1]
    flat[...] = jnp.zeros_like(flat)
    for group in range(2):
        total = None
        for j in range(PER_GROUP):
            shift = 2 * PC * (j // 2) - 1 + j % 2
            part = fields[group * PER_GROUP + j]
            part = roll(part, shift, 1) if shift else part
            total = part if total is None else total + part
        packed[:size, :] = total
        packed[size:, :] = jnp.zeros((128 - size, 128), F32)
        packed[...] = packed[...].T
        for j in range(PER_GROUP):
            first = 2 * PC * (j // 2) + j % 2
            flat[group * PER_GROUP + j, :PC, :] = packed[pl.ds(first, PC, stride=2), :]


def band_sums(flat, packed, bands, slopes):
    columns = [[flat[k * FIELDS + n] for k in range(3)] for n in range(FIELDS)]

    def product(a, b):
        return sum(columns[a][k] * columns[b][k] for k in range(3))

    def moved(value, step):
        x, y, z = step
        value = roll(value, PC * x + y, 1) if x or y else value
        return roll(value, z, 0) if z else value

    totals = {}
    trace = None
    for a in range(len(PAIRS)):
        for b in range(a, len(PAIRS)):
            value = product(a, b)
            if a == b:
                trace = value if trace is None else trace + value
            for one, two in {(a, b), (b, a)}:
                key = tuple(q - p for p, q in zip(PAIRS[one], PAIRS[two]))
                part = moved(value, PAIRS[two])
                totals[key] = part if key not in totals else totals[key] + part
    trace = jnp.sum(jnp.sum(trace, axis=0, keepdims=True), axis=1, keepdims=True)
    ridge = DAMPING * trace / PC**3 + EPSILON
    totals[0, 0, 0] = totals[0, 0, 0] + ridge
    for n, key in enumerate(BANDS):
        bands[n] = totals[key]
    slope = None
    for a in range(len(PAIRS)):
        part = moved(product(a, FIELDS - 1), PAIRS[a])
        slope = part if slope is None else slope + part
    packed[...] = jnp.zeros_like(packed)
    packed[: slope.shape[0], :] = slope
    slopes[...] = packed[...].T


def fill(c, t, z, bands, slopes, mat, side, reach):
    params = PC * PC
    lane = iota((8, 128), 1)
    gap = lane - iota((8, 128), 0)
    column = pltpu.roll(slopes[...], params - z, 1)
    ahead = 1 if c == 0 else -1

    def rows_of(depth):
        found = []
        for n, (x, y, dz) in enumerate(BANDS):
            if dz == depth * ahead:
                row = bands[n, pl.ds(z + depth * ahead, 1), :]
                found.append((PC * x + y, jnp.broadcast_to(row, (8, 128))))
        return found

    parts = [rows_of(depth) for depth in range(reach + 1)]
    for q in range(-(-params // 8)):
        here = slice(8 * q, 8 * q + 8)
        inside = lane < params

        def block(entries):
            value = jnp.zeros((8, 128), F32)
            for offset, row in entries:
                value = jnp.where(gap == 8 * q + offset, row, value)
            return jnp.where(inside, value, 0.0)

        mat[c, t, here, :] = block(parts[0])
        first = block(parts[1]) if reach > 0 else jnp.zeros((8, 128), F32)
        side[c, t, here, 0:128] = jnp.where(lane == params, column[here], first)
        if reach > 1:
            side[c, t, here, 128:256] = block(parts[2])


def assemble(bands, slopes, mat, side):
    meet = PC // 2 - 1
    mat[...] = jnp.zeros_like(mat)
    side[...] = jnp.zeros_like(side)

    def both(t, _):
        fill(0, t, t, bands, slopes, mat, side, 2)
        fill(1, t, PC - 1 - t, bands, slopes, mat, side, 2)
        return 0

    lax.fori_loop(0, meet, both, 0)
    fill(0, meet, meet, bands, slopes, mat, side, 1)
    fill(0, meet + 1, meet + 1, bands, slopes, mat, side, 0)


GROUPS = 5


def factored(blocks, count):
    lane = iota((8, 128), 1)
    sub = iota((8, 128), 0)
    tiles = -(-count // 8)
    chains = range(len(blocks))

    def over_lanes(value, at):
        return jnp.broadcast_to(value[:, at : at + 1], value.shape)

    def over_rows(value, at):
        return jnp.broadcast_to(value[at : at + 1, :], value.shape)

    grids = [[block[8 * q : 8 * q + 8] for q in range(tiles)] for block in blocks]
    lower = [[] for _ in blocks]
    scaled = [[] for _ in blocks]
    first = 0
    while first < tiles:
        last = min(first + GROUPS, tiles)
        for p in range(first, last):
            width = min(8, count - 8 * p)
            within = (lane >= 8 * p) & (lane < 8 * p + width)
            unit = jnp.where(lane - 8 * p == sub, 1.0, 0.0)
            for c in chains:
                grid = grids[c]
                panel = grid[p]
                columns = [over_lanes(panel, 8 * p + n) for n in range(width)]
                panel = jnp.where(within, unit, panel)
                lower[c].append(panel)
                rows = [over_rows(panel, n) for n in range(width)]
                for i in range(width):
                    j = 8 * p + i
                    column = columns[i]
                    pivot = 1.0 / over_rows(column, i)
                    row = over_rows(panel, i) * pivot
                    for n in range(i + 1, width):
                        crossing = over_rows(columns[n], i) * pivot
                        columns[n] = jnp.where(sub == i, crossing, columns[n] - column * crossing)
                    panel = jnp.where(sub == i, row, panel - column * row)
                rows = [over_rows(panel, n) for n in range(width)]
                panel = rows[0]
                for n in range(1, width):
                    panel = jnp.where(sub == n, rows[n], panel)
                scaled[c].append(panel)
                for q in range(p + 1, last):
                    old = grid[q]
                    terms = [over_lanes(old, 8 * p + n) * row for n, row in enumerate(rows)]
                    while len(terms) > 1:
                        pairs = [terms[n] + terms[n + 1] for n in range(0, len(terms) - 1, 2)]
                        terms = pairs + terms[len(terms) - len(terms) % 2 :]
                    grid[q] = jnp.where(within, 0.0, old) - terms[0]
        if last < tiles:
            within = (lane >= 8 * first) & (lane < 8 * last)
            for c in chains:
                low = jnp.concatenate(lower[c][first:last], axis=0)
                high = jnp.concatenate(
                    [
                        jnp.where((lane < 8 * p + 8) | (lane >= 8 * last), scaled[c][p], 0.0)
                        for p in range(first, last)
                    ],
                    axis=0,
                )
                change = dot(low, high, (0, 0))
                for q in range(last, tiles):
                    old = jnp.where(within, 0.0, grids[c][q])
                    grids[c][q] = old - change[8 * q : 8 * q + 8]
        first = last

    def trimmed(parts):
        kept = []
        for p, part in enumerate(parts):
            limit = min(8 * p + 8, count)
            kept.append(jnp.where((lane < limit) & (sub < limit - 8 * p), part, 0.0))
        return jnp.concatenate(kept, axis=0)

    return [(trimmed(lower[c]), trimmed(scaled[c])) for c in chains]


def eliminate(t, chains, size, mat, side, lowers, solved, more=True):
    params = PC * PC
    mark = iota((128, 128), 1) == params
    blocks = [mat[c, t, :size, :] for c in chains]
    for c, (low, high) in zip(chains, factored(blocks, params)):
        lowers[c, t, :size, :] = low
        right = side[c, t, :size, :]
        z = dot(high[:, :size], right, (1, 0))
        solved[c, t, :size, :] = z
        if not more:
            continue
        y = dot(low[:, :size], right, (1, 0))
        schur = dot(y, z, (0, 0))
        near, far = schur[:128], schur[128:]
        mat[c, t + 1] -= near[:, :128]
        side[c, t + 1, :, 0:128] -= jnp.where(mark, near[:, :128], near[:, 128:])
        mat[c, t + 2] -= far[:, 128:]
        side[c, t + 2, :, 0:128] -= jnp.where(mark, far[:, :128], 0.0)


def solve_zone(size, mat, side, lowers, solved, spread):
    params = PC * PC
    meet = PC // 2 - 1
    mark = iota((128, 128), 1) == params
    for ref in (lowers, solved):
        ref[:, :, size:, :] = jnp.zeros((*ref.shape[:2], ref.shape[2] - size, ref.shape[3]), F32)

    def both(t, _):
        eliminate(t, (0, 1), size, mat, side, lowers, solved)
        return 0

    lax.fori_loop(0, meet, both, 0)
    mat[0, meet] += mat[1, meet + 1]
    mat[0, meet + 1] += mat[1, meet]
    turned = side[1, meet, :, 0:128].T
    side[0, meet, :, 0:128] += jnp.where(mark, side[1, meet + 1, :, 0:128], turned)
    side[0, meet + 1, :, 0:128] += jnp.where(mark, side[1, meet, :, 0:128], 0.0)
    eliminate(meet, (0,), size, mat, side, lowers, solved)
    eliminate(meet + 1, (0,), size, mat, side, lowers, solved, more=False)

    flag = iota((8, 128), 1) == params

    def back(c, t, near, far):
        row = jnp.concatenate([jnp.where(flag, -1.0, near), far], axis=1)
        value = dot(row, solved[c, t], (1, 1))
        return -dot(value, lowers[c, t], (1, 0))

    blank = jnp.zeros((8, 128), F32)
    rows = [blank] * PC
    rows[meet + 1] = back(0, meet + 1, blank, blank)
    rows[meet] = back(0, meet, rows[meet + 1], blank)
    for t in range(meet - 1, -1, -1):
        rows[t] = back(0, t, rows[t + 1], rows[t + 2])
        z = PC - 1 - t
        rows[z] = back(1, t, rows[z - 1], rows[z - 2])
    spread[...] = jnp.zeros_like(spread)
    for z in range(PC):
        spread[2 * z + 1 : 2 * z + 3, :] = -rows[z][:2]
    spread[...] = spread[...].T


def place_zone(begin, zone_m, spread, temp, added):
    rows = zone_m.shape[1]
    span = 2 * PC

    def ramp(position):
        value = jnp.sin(math.pi * (position.astype(F32) - 0.5) / span)
        return jnp.where((position >= 1) & (position <= span), value, 0.0)

    weight = ramp(iota((rows, 128), 0)) * ramp(iota((rows, 128), 1))
    temp[0] = jnp.zeros_like(weight)
    shift = lax.rem(begin[2] + added.shape[2], added.shape[2])
    for x in range(PC):
        part = spread[x * PC : (x + 1) * PC, :]
        temp[0, pl.ds(1, PC, stride=2), :] = part
        temp[0, pl.ds(2, PC, stride=2), :] = part
        value = weight * temp[0]
        for a in range(2):
            at = 2 * x + 1 + a
            plane = value * math.sin(math.pi * (at - 0.5) / span) * zone_m[at]
            plane = jnp.pad(plane, ((0, added.shape[1] - rows), (0, 0)))
            plane = pltpu.roll(plane, begin[1], 0)
            plane = jnp.pad(plane, ((0, 0), (0, added.shape[2] - 128)))
            added[begin[0] + at] += pltpu.roll(plane, shift, 1)


def cut_zone(begin, depth, zone_all_u, zone_all_w, zone_u, zone_f, zone_m):
    count, rows = zone_m.shape[:2]
    whole_rows, whole_lanes = zone_all_u.shape[-2:]
    shift = lax.rem(whole_lanes - begin[2], whole_lanes)
    shift_y = lax.rem(whole_rows - begin[1], whole_rows)
    z = begin[2] + iota((rows, 128), 1)
    inside = (z >= 0) & (z < depth) & (iota((rows, 128), 0) < count)

    def cut(x, _):
        def take(ref, k):
            plane = pltpu.roll(ref[k, begin[0] + x], shift, 1)[:, :128]
            return jnp.where(inside, pltpu.roll(plane, shift_y, 0)[:rows], 0.0)

        for k in range(3):
            zone_u[k, x] = take(zone_all_u, k)
            zone_f[k, x] = take(zone_all_w, k)
        zone_m[x] = take(zone_all_w, 3)
        return 0

    lax.fori_loop(0, count, cut, 0)


def zone_kernel(counts, brick, margins, where, zone_all_u, zone_all_w, field_out, added, *scratch):
    scratch, (corners, ready) = scratch[:-2], scratch[-2:]
    zone_u, zone_f, zone_m = scratch[:3]
    temp, fields, packed, flat, bands, slopes, mat, side, lowers, solved, spread = scratch[3:]
    bx, by, bz = brick
    hx, hy = margins
    here = [lax.axis_index(name) for name in AXES]
    lanes = pl.ds(pl.multiple_of(here[2] * bz, bz), bz)
    fetch = pltpu.make_async_copy(where, corners, ready.at[0])
    fetch.start()
    inner = zone_all_u.at[:, hx : hx + bx, hy : hy + by, lanes]
    store = pltpu.make_async_copy(inner, field_out, ready.at[1])
    store.start()
    added[...] = jnp.zeros_like(added)
    fetch.wait()
    for number in range(corners.shape[0]):
        begin = [
            corners[number, 0] - here[0] * bx + hx - 1,
            corners[number, 1] - here[1] * by + hy - 1,
            corners[number, 2] - 1,
        ]
        cut_zone(begin, counts[2] * bz, zone_all_u, zone_all_w, zone_u, zone_f, zone_m)
        fields[...] = jnp.zeros_like(fields)
        coarse_fields(zone_u, zone_f, zone_m, temp, fields)
        transpose_fields(fields, packed, flat)
        band_sums(flat, packed, bands, slopes)
        assemble(bands, slopes, mat, side)
        solve_zone(fields.shape[1], mat, side, lowers, solved, spread)
        place_zone(begin, zone_m, spread, temp, added)
    store.wait()


def body(forcing, start_field, modulus, corners):
    brick = modulus.shape
    bx, by, bz = brick
    counts = [lax.axis_size(name) for name in AXES]
    margins = (HALO, -(-HALO // 8) * 8)
    span = [size + 2 * margin for size, margin in zip(brick, margins)] + [counts[2] * bz]
    whole = pl.BlockSpec(memory_space=pltpu.VMEM)
    dma = pltpu.SemaphoreType.DMA
    peers = max(counts[2] - 1, 1)
    zone_all_u, zone_all_w = pl.pallas_call(
        functools.partial(sweep_kernel, counts, brick, margins),
        out_shape=(
            jax.ShapeDtypeStruct((3, *span), F32),
            jax.ShapeDtypeStruct((4, *span), F32),
        ),
        in_specs=[pl.BlockSpec(memory_space=pltpu.HBM)] * 3,
        out_specs=(whole, whole),
        scratch_shapes=[
            pltpu.VMEM((4, bx + 2, by, bz), F32),
            *[pltpu.VMEM((3, bx + 2, by, bz), F32)] * (FSWEEPS - 1),
            pltpu.VMEM((FSWEEPS, 2, 4, bx, bz), F32),
            pltpu.VMEM((FSWEEPS, 2, 4, bx, bz), F32),
            pltpu.VMEM((2, 4, bx, by, bz), F32),
            *[pltpu.VMEM((2, 3, bx, by, bz), F32)] * (FSWEEPS - 1),
            pltpu.VMEM((6, bx, by, bz), F32),
            pltpu.VMEM((bx, by, bz), F32),
            dma((FSWEEPS, 4, len(FACES))),
            dma((FSWEEPS, 4, len(FACES))),
            dma((FSWEEPS + 3, len(AROUND))),
            dma((FSWEEPS + 3, len(AROUND))),
            dma((FSWEEPS + 3, len(AROUND) + 1, peers)),
            dma((FSWEEPS + 3, len(AROUND) + 1, peers)),
            dma((4,)),
        ],
        compiler_params=pltpu.CompilerParams(
            collective_id=0, has_side_effects=True, vmem_limit_bytes=40 * 1024 * 1024
        ),
        name="sweeps",
    )(*[pltpu.with_memory_space_constraint(each, pltpu.HBM) for each in (forcing, start_field, modulus)])
    zone_span = 2 * PC + 2
    zone_rows = -(-zone_span // 8) * 8
    size = -(-PC * PC // 8) * 8
    planes = PC // 2 + 3
    field, added = pl.pallas_call(
        functools.partial(zone_kernel, counts, brick, margins),
        out_shape=(
            jax.ShapeDtypeStruct(forcing.shape, F32),
            jax.ShapeDtypeStruct(tuple(span), F32),
        ),
        in_specs=[pl.BlockSpec(memory_space=pltpu.HBM), whole, whole],
        out_specs=(pl.BlockSpec(memory_space=pl.ANY), whole),
        scratch_shapes=[
            pltpu.VMEM((3, zone_span, zone_rows, 128), F32),
            pltpu.VMEM((3, zone_span, zone_rows, 128), F32),
            pltpu.VMEM((zone_span, zone_rows, 128), F32),
            pltpu.VMEM((3 * FIELDS, zone_rows, 128), F32),
            pltpu.VMEM((3 * FIELDS, size, 128), F32),
            pltpu.VMEM((128, 128), F32),
            pltpu.VMEM((3 * FIELDS, 16, 128), F32),
            pltpu.VMEM((len(BANDS), 16, 128), F32),
            pltpu.VMEM((128, 128), F32),
            pltpu.VMEM((2, planes, 128, 128), F32),
            pltpu.VMEM((2, planes, 128, 256), F32),
            pltpu.VMEM((2, planes, 128, 128), F32),
            pltpu.VMEM((2, planes, 128, 256), F32),
            pltpu.VMEM((128, 128), F32),
            pltpu.SMEM(corners.shape, jnp.int32),
            dma((2,)),
        ],
        compiler_params=pltpu.CompilerParams(vmem_limit_bytes=40 * 1024 * 1024),
        name="zone",
    )(pltpu.with_memory_space_constraint(corners, pltpu.HBM), zone_all_u, zone_all_w)
    updated = pl.pallas_call(
        functools.partial(gather_kernel, counts, brick, margins),
        out_shape=jax.ShapeDtypeStruct(brick, F32),
        in_specs=[whole, whole],
        out_specs=whole,
        scratch_shapes=[
            pltpu.VMEM((span[0], span[1], bz), F32),
            pltpu.VMEM((peers, span[0], span[1], bz), F32),
            pltpu.VMEM((2, HALO - 1, by, bz), F32),
            pltpu.VMEM((2, bx, HALO - 1, bz), F32),
            pltpu.VMEM((4, HALO - 1, HALO - 1, bz), F32),
            dma((len(AROUND),)),
            dma((len(AROUND),)),
            dma((peers,)),
            dma((peers,)),
        ],
        compiler_params=pltpu.CompilerParams(
            collective_id=1, has_side_effects=True, vmem_limit_bytes=40 * 1024 * 1024
        ),
        name="gather",
    )(added, modulus)
    return (field, updated)


def solution(mesh):
    placed = (
        P(None, "gx", "gy", "gz"),
        P(None, "gx", "gy", "gz"),
        P("gx", "gy", "gz"),
        P(("gx", "gy", "gz"), None),
    )
    return jax.shard_map(
        body,
        mesh=mesh,
        in_specs=placed,
        out_specs=(P(None, "gx", "gy", "gz"), P("gx", "gy", "gz")),
        check_vma=False,
    )
```

```python
import functools
import math

import jax
import jax.numpy as jnp
from jax import lax
from jax.experimental import pallas as pl
from jax.experimental.pallas import tpu as pltpu
from jax.sharding import PartitionSpec as P

PC = 10
HALO = 6
FSWEEPS = 4


MASS_TERM = 0.5
DAMPING = 0.1
EPSILON = 1e-06
HIGHEST = lax.Precision.HIGHEST
F32 = jnp.float32


def dot(a, b, contract, precision=lax.Precision.HIGH):
    return lax.dot_general(
        a, b, ((contract[:1], contract[1:]), ((), ())), precision=precision, preferred_element_type=F32
    )


def roll(values, shift, axis):
    return pltpu.roll(values, shift % values.shape[axis], axis)


def iota(shape, axis):
    return lax.broadcasted_iota(jnp.int32, shape, axis)


MESH_ID = pl.DeviceIdType.MESH
AXES = ("gx", "gy", "gz")
AROUND = tuple((dx, dy) for dx in (-1, 0, 1) for dy in (-1, 0, 1) if (dx, dy) != (0, 0))
FACES = ((-1, 0, 0), (1, 0, 0), (0, -1, 0), (0, 1, 0), (0, 0, -1), (0, 0, 1))


class Place:
    def __init__(self, counts):
        self.counts = counts
        self.here = [lax.axis_index(name) for name in AXES]

    def exists(self, step):
        inside = None
        for at, count, move in zip(self.here, self.counts, step):
            if move:
                test = at + move < count if move > 0 else at + move >= 0
                inside = test if inside is None else inside & test
        return inside

    def device(self, step):
        return tuple(at + move for at, move in zip(self.here, step))

    def peer(self, turn):
        return self.here[:2] + [lax.rem(self.here[2] + turn, self.counts[2])]

    def call(self):
        barrier = pltpu.get_barrier_semaphore()
        total = self.counts[2] - 1
        for dx, dy in AROUND:
            step = (dx, dy, 0)

            @pl.when(self.exists(step))
            def _():
                pl.semaphore_signal(
                    barrier, inc=1, device_id=self.device(step), device_id_type=MESH_ID
                )

            total = total + self.exists(step).astype(jnp.int32)
        for turn in range(1, self.counts[2]):
            pl.semaphore_signal(
                barrier, inc=1, device_id=tuple(self.peer(turn)), device_id_type=MESH_ID
            )
        return barrier, total


def opposite(step):
    return tuple(-move for move in step)


class Message:
    def __init__(self, place, step, source, target, send, recv):
        self.place, self.step = place, step
        self.copy = pltpu.make_async_remote_copy(
            src_ref=source,
            dst_ref=target,
            send_sem=send,
            recv_sem=recv,
            device_id=place.device(step),
            device_id_type=MESH_ID,
        )

    def start(self):
        pl.when(self.place.exists(self.step))(self.copy.start)

    def sent(self):
        pl.when(self.place.exists(self.step))(self.copy.wait_send)

    def arrived(self):
        pl.when(self.place.exists(opposite(self.step)))(self.copy.wait_recv)


def edge_span(move, size, margin, reach=None):
    reach = margin if reach is None else reach
    if move > 0:
        return slice(margin + size - reach, margin + size), slice(margin - reach, margin)
    if move < 0:
        far = margin + size
        return slice(margin, margin + reach), slice(far, far + reach)
    return slice(margin, margin + size), slice(margin, margin + size)


def regions(brick, margins, reach):
    found = []
    for dx, dy in AROUND:
        from_x, to_x = edge_span(dx, brick[0], margins[0], reach)
        from_y, to_y = edge_span(dy, brick[1], margins[1], reach)
        found.append(((dx, dy, 0), (from_x, from_y), (to_x, to_y)))
    return sorted(found, key=lambda entry: (entry[0][1] == 0, entry[0][0] == 0))


def spread_messages(place, brick, margins, ref, lanes, send, recv, reach):
    return [
        Message(
            place,
            step,
            ref.at[:, source[0], source[1], lanes],
            ref.at[:, target[0], target[1], lanes],
            send.at[n],
            recv.at[n],
        )
        for n, (step, source, target) in enumerate(regions(brick, margins, reach))
    ]


class Relay:
    def __init__(self, place, step, ref, lanes, span, send, recv):
        self.place, self.step = place, step
        view = ref.at[:, span[0], span[1], lanes]
        self.copies = [
            pltpu.make_async_remote_copy(
                src_ref=view,
                dst_ref=view,
                send_sem=send.at[turn - 1],
                recv_sem=recv.at[turn - 1],
                device_id=tuple(place.peer(turn)),
                device_id_type=MESH_ID,
            )
            for turn in range(1, place.counts[2])
        ]

    def when(self, action):
        test = self.place.exists(self.step) if any(self.step) else None
        action() if test is None else pl.when(test)(action)

    def start(self):
        self.when(lambda: [copy.start() for copy in self.copies] and None)

    def wait(self):
        self.when(lambda: [copy.wait() for copy in self.copies] and None)


def clear_outside(place, brick, margins, refs, lanes):
    for dx, dy in AROUND:
        _, to_x = edge_span(-dx, brick[0], margins[0])
        _, to_y = edge_span(-dy, brick[1], margins[1])

        @pl.when(jnp.logical_not(place.exists((dx, dy, 0))))
        def _():
            for ref in refs:
                for k in range(ref.shape[0]):
                    shape = (to_x.stop - to_x.start, to_y.stop - to_y.start, lanes.size)
                    ref[k, to_x, to_y, lanes] = jnp.zeros(shape, F32)


def sweep_kernel(counts, brick, margins, forcing, start, modulus, zone_u, zone_w, *scratch):
    fields, rows_in, rows_out, sides = scratch[0:4], scratch[4], scratch[5], scratch[6:10]
    coupling, inverse = scratch[10:12]
    face_send, face_recv, bulk_send, bulk_recv, peer_send, peer_recv, load = scratch[12:]
    place = Place(counts)
    bx, by, bz = brick
    hx, hy = margins
    lanes = pl.ds(pl.multiple_of(place.here[2] * bz, bz), bz)
    every = pl.ds(0, counts[2] * bz)
    row = iota((by, bz), 0)
    lane = iota((by, bz), 1)
    own = (slice(hx, hx + bx), slice(hy, hy + by))
    loads = [
        pltpu.make_async_copy(start, fields[0].at[:3, 1 : bx + 1], load.at[0]),
        pltpu.make_async_copy(modulus, fields[0].at[3, 1 : bx + 1], load.at[1]),
        pltpu.make_async_copy(modulus, zone_w.at[3, own[0], own[1], lanes], load.at[2]),
        pltpu.make_async_copy(forcing, zone_w.at[:3, own[0], own[1], lanes], load.at[3]),
    ]
    for copy in loads:
        copy.start()
    barrier, greetings = place.call()

    for n, (dx, dy, dz) in enumerate(FACES):

        @pl.when(jnp.logical_not(place.exists((dx, dy, dz))))
        def _():
            for sweep in range(FSWEEPS):
                if dx:
                    plane = 0 if dx < 0 else bx + 1
                    for k in range(fields[sweep].shape[0]):
                        fields[sweep][k, plane] = jnp.zeros((by, bz), F32)
                elif dy:
                    for k in range(4):
                        rows_in[sweep, 0 if dy < 0 else 1, k] = jnp.zeros((bx, bz), F32)
                else:
                    for k in range(sides[sweep].shape[1]):
                        blank = jnp.zeros((bx, by, bz), F32)
                        sides[sweep][0 if dz < 0 else 1, k] = blank

    loads[0].wait()
    loads[1].wait()

    def stage(x, _):
        for k in range(4):
            u = fields[0][k, x + 1]
            rows_out[0, 0, k, pl.ds(x, 1), :] = u[:1]
            rows_out[0, 1, k, pl.ds(x, 1), :] = u[by - 1 :]
        return 0

    lax.fori_loop(0, bx, stage, 0)

    def faces(sweep, k):
        field = fields[sweep]
        messages = []
        for n, step in enumerate(FACES):
            dx, dy, dz = step
            if dx:
                source = field.at[k, bx if dx > 0 else 1]
                target = field.at[k, 0 if dx > 0 else bx + 1]
            elif dy:
                source = rows_out.at[sweep, 1 if dy > 0 else 0, k]
                target = rows_in.at[sweep, 0 if dy > 0 else 1, k]
            else:
                source = field.at[k, 1 : bx + 1]
                target = sides[sweep].at[0 if dz > 0 else 1, k]
            at = (sweep, k, n)
            messages.append(
                Message(place, step, source, target, face_send.at[at], face_recv.at[at])
            )
        return messages

    def relays(first, last, slot, ref, reach):
        view = ref.at[first:last]
        entries = [((0, 0, 0), own)]
        entries += [(opposite(step), target) for step, _, target in regions(brick, margins, reach)]
        return [
            Relay(place, step, view, lanes, span, peer_send.at[slot, n], peer_recv.at[slot, n])
            for n, (step, span) in enumerate(entries)
        ]

    pl.semaphore_wait(barrier, greetings)
    waiting = {(0, k): faces(0, k) for k in (3, 0, 1, 2)}
    pending = sum(waiting.values(), [])
    for message in pending:
        message.start()
    loads[2].wait()
    loads[3].wait()
    bulk, forward = [], []
    for slot, (first, last, reach) in enumerate(((3, 4, HALO), (0, 1, HALO - 1), (1, 2, HALO - 1), (2, 3, HALO - 1))):
        bulk.append(
            spread_messages(
                place,
                brick,
                margins,
                zone_w.at[first:last],
                lanes,
                bulk_send.at[slot],
                bulk_recv.at[slot],
                reach,
            )
        )
        forward.append(relays(first, last, slot, zone_w, reach))

    def around(sweep, k, x, u):
        low, high = rows_in[sweep, 0, k, pl.ds(x, 1), :], rows_in[sweep, 1, k, pl.ds(x, 1), :]
        y_up = jnp.where(row == by - 1, jnp.broadcast_to(high, u.shape), roll(u, -1, 0))
        y_down = jnp.where(row == 0, jnp.broadcast_to(low, u.shape), roll(u, 1, 0))
        below, above = sides[sweep][0, k, x], sides[sweep][1, k, x]
        z_up = jnp.where(lane == bz - 1, roll(above, -1, 1), roll(u, -1, 1))
        z_down = jnp.where(lane == 0, roll(below, 1, 1), roll(u, 1, 1))
        field = fields[sweep]
        return field[k, x + 2], field[k, x], y_up, y_down, z_up, z_down

    def couple(x, _):
        m = fields[0][3, x + 1]
        below = MASS_TERM
        for n, other in enumerate(around(0, 3, x, m)):
            face = 0.5 * (m + other)
            coupling[n, x] = face
            below = below + face
        inverse[x] = 1.0 / below
        return 0

    for sweep in range(FSWEEPS):
        for message in bulk[sweep]:
            message.start()
        forward[sweep][0].start()
        if sweep == 0:
            clear_outside(place, brick, margins, (zone_u, zone_w), every)
            for message in waiting[0, 3]:
                message.arrived()
            lax.fori_loop(0, bx, couple, 0)
        for k in range(3):
            for message in waiting[sweep, k]:
                message.arrived()

            def relax(x, _, sweep=sweep, k=k):
                u = fields[sweep][k, x + 1]
                total = zone_w[k, hx + x, hy : hy + by, lanes]
                for n, other in enumerate(around(sweep, k, x, u)):
                    total = total + coupling[n, x] * other
                total = total * inverse[x]
                if sweep < FSWEEPS - 1:
                    fields[sweep + 1][k, x + 1] = total
                    rows_out[sweep + 1, 0, k, pl.ds(x, 1), :] = total[:1]
                    rows_out[sweep + 1, 1, k, pl.ds(x, 1), :] = total[by - 1 :]
                else:
                    zone_u[k, hx + x, hy : hy + by, lanes] = total
                return 0

            lax.fori_loop(0, bx, relax, 0)
            if sweep < FSWEEPS - 1:
                waiting[sweep + 1, k] = faces(sweep + 1, k)
                pending += waiting[sweep + 1, k]
                for message in waiting[sweep + 1, k]:
                    message.start()
            else:
                slot = FSWEEPS + k
                final = spread_messages(
                    place,
                    brick,
                    margins,
                    zone_u.at[k : k + 1],
                    lanes,
                    bulk_send.at[slot],
                    bulk_recv.at[slot],
                    HALO,
                )
                for message in final:
                    message.start()
                bulk.append(final)
                forward.append(relays(k, k + 1, slot, zone_u, HALO))
                forward[slot][0].start()
    for group, onward in zip(bulk, forward):
        for message, relay in zip(group, onward[1:]):
            message.arrived()
            relay.start()
    for message in pending + sum(bulk, []):
        message.sent()
    for relay in sum(forward, []):
        relay.wait()


def gather_kernel(counts, brick, margins, added, modulus, out, total, from_peer, *scratch):
    from_x, from_y, from_xy, send, recv, peer_send, peer_recv = scratch
    place = Place(counts)
    bx, by, bz = brick
    hx, hy = margins

    def part(turn):
        at = lax.rem(place.here[2] + turn, counts[2])
        return pl.ds(pl.multiple_of(at * bz, bz), bz)

    targets = {}
    for n, (dx, dy) in enumerate(AROUND):
        if dy == 0:
            targets[n] = from_x.at[(dx + 1) // 2]
        elif dx == 0:
            targets[n] = from_y.at[(dy + 1) // 2]
        else:
            targets[n] = from_xy.at[dx + 1 + (dy + 1) // 2]

    barrier, greetings = place.call()
    for n, (dx, dy) in enumerate(AROUND):

        @pl.when(jnp.logical_not(place.exists((-dx, -dy, 0))))
        def _():
            targets[n][...] = jnp.zeros(targets[n].shape, F32)

    pl.semaphore_wait(barrier, greetings)
    copies = [
        pltpu.make_async_remote_copy(
            src_ref=added.at[:, :, part(turn)],
            dst_ref=from_peer.at[turn - 1],
            send_sem=peer_send.at[turn - 1],
            recv_sem=peer_recv.at[turn - 1],
            device_id=tuple(place.peer(turn)),
            device_id_type=MESH_ID,
        )
        for turn in range(1, counts[2])
    ]
    for copy in copies:
        copy.start()
    for copy in copies:
        copy.wait_recv()

    def collect(x, _):
        value = added[x, :, part(0)]
        for turn in range(1, counts[2]):
            value = value + from_peer[turn - 1, x]
        total[x] = value
        return 0

    lax.fori_loop(0, total.shape[0], collect, 0)
    messages = []
    for n, (dx, dy) in enumerate(AROUND):
        _, at_x = edge_span(-dx, bx, hx, HALO - 1)
        _, at_y = edge_span(-dy, by, hy, HALO - 1)
        messages.append(
            Message(place, (dx, dy, 0), total.at[at_x, at_y], targets[n], send.at[n], recv.at[n])
        )
    for message in messages:
        message.start()

    def centre(x, _):
        out[x] = modulus[x] + total[hx + x, hy : hy + by, :]
        return 0

    lax.fori_loop(0, bx, centre, 0)
    for message in messages:
        message.arrived()
    for n, (dx, dy) in enumerate(AROUND):
        to_x, _ = edge_span(-dx, bx, hx, HALO - 1)
        to_y, _ = edge_span(-dy, by, hy, HALO - 1)
        out[to_x.start - hx : to_x.stop - hx, to_y.start - hy : to_y.stop - hy, :] += targets[n][...]
    for message in messages:
        message.sent()
    for copy in copies:
        copy.wait_send()


FIELDS = 8


def coarse_fields(zone_u, zone_f, zone_m, temp, fields):
    rows = zone_m.shape[1]
    first_y = iota((rows, 128), 0) % 2 == 1
    first_z = iota((rows, 128), 1) % 2 == 1
    rank = iota((PC, 128), 0)
    lane = iota((PC, 128), 1)
    steps = ((0, 1), (0, -1), (1, 1), (1, -1), (2, 1), (2, -1))
    for x in range(PC):
        middles, others = [], []
        for a in range(2):
            at = 2 * x + 1 + a
            m = zone_m[at]
            middles.append(m)
            others.append(
                [
                    zone_m[at + step] if axis == 0 else roll(m, -step, axis - 1)
                    for axis, step in steps
                ]
            )
        for k in range(3):
            sums = [None] * FIELDS

            def put(number, value):
                sums[number] = value if sums[number] is None else sums[number] + value

            for a in range(2):
                at = 2 * x + 1 + a
                u, m = zone_u[k, at], middles[a]
                applied = MASS_TERM * u
                laplace = jnp.zeros_like(u)
                for number, (axis, step) in enumerate(steps):
                    u_next = zone_u[k, at + step] if axis == 0 else roll(u, -step, axis - 1)
                    m_next = others[a][number]
                    change = u - u_next
                    applied = applied + 0.5 * (m + m_next) * change
                    laplace = laplace + change
                    flow = -0.5 * m_next * change
                    if axis == 0:
                        same = (a == 0) == (step == 1)
                        put(0 if same else 1 + number, flow)
                    else:
                        first = first_y if axis == 1 else first_z
                        near = first if step == 1 else ~first
                        put(0, jnp.where(near, flow, 0.0))
                        put(1 + number, jnp.where(near, 0.0, flow))
                put(0, -0.5 * m * laplace)
                put(7, zone_f[k, at] - applied)
            for number in range(FIELDS):
                slot = temp.at[k * FIELDS + number]
                slot[...] = sums[number]
                pair = slot[pl.ds(1, PC, stride=2), :] + slot[pl.ds(2, PC, stride=2), :]
                pair = pair + roll(pair, -1, 1)
                keep = (lane % 2 == 1) & (lane < 2 * PC)
                if number == 1 and x == PC - 1 or number == 2 and x == 0:
                    keep = jnp.zeros_like(keep)
                if number == 3:
                    keep = keep & (rank < PC - 1)
                if number == 4:
                    keep = keep & (rank > 0)
                if number == 5:
                    keep = keep & (lane < 2 * PC - 2)
                if number == 6:
                    keep = keep & (lane > 1)
                fields[k * FIELDS + number, x * PC : (x + 1) * PC, :] = jnp.where(keep, pair, 0.0)


PAIRS = ((0, 0, 0), (1, 0, 0), (-1, 0, 0), (0, 1, 0), (0, -1, 0), (0, 0, 1), (0, 0, -1))
BANDS = tuple(
    sorted({tuple(b - a for a, b in zip(one, two)) for one in PAIRS for two in PAIRS})
)
PER_GROUP = 12


def transpose_fields(fields, packed, flat):
    size = fields.shape[1]
    flat[...] = jnp.zeros_like(flat)
    for group in range(2):
        total = None
        for j in range(PER_GROUP):
            shift = 2 * PC * (j // 2) - 1 + j % 2
            part = fields[group * PER_GROUP + j]
            part = roll(part, shift, 1) if shift else part
            total = part if total is None else total + part
        packed[:size, :] = total
        packed[size:, :] = jnp.zeros((128 - size, 128), F32)
        packed[...] = packed[...].T
        for j in range(PER_GROUP):
            first = 2 * PC * (j // 2) + j % 2
            flat[group * PER_GROUP + j, :PC, :] = packed[pl.ds(first, PC, stride=2), :]


def band_sums(flat, packed, bands, slopes):
    columns = [[flat[k * FIELDS + n] for k in range(3)] for n in range(FIELDS)]

    def product(a, b):
        return sum(columns[a][k] * columns[b][k] for k in range(3))

    def moved(value, step):
        x, y, z = step
        value = roll(value, PC * x + y, 1) if x or y else value
        return roll(value, z, 0) if z else value

    totals = {}
    trace = None
    for a in range(len(PAIRS)):
        for b in range(a, len(PAIRS)):
            value = product(a, b)
            if a == b:
                trace = value if trace is None else trace + value
            for one, two in {(a, b), (b, a)}:
                key = tuple(q - p for p, q in zip(PAIRS[one], PAIRS[two]))
                part = moved(value, PAIRS[two])
                totals[key] = part if key not in totals else totals[key] + part
    trace = jnp.sum(jnp.sum(trace, axis=0, keepdims=True), axis=1, keepdims=True)
    ridge = DAMPING * trace / PC**3 + EPSILON
    totals[0, 0, 0] = totals[0, 0, 0] + ridge
    for n, key in enumerate(BANDS):
        bands[n] = totals[key]
    slope = None
    for a in range(len(PAIRS)):
        part = moved(product(a, FIELDS - 1), PAIRS[a])
        slope = part if slope is None else slope + part
    packed[...] = jnp.zeros_like(packed)
    packed[: slope.shape[0], :] = slope
    slopes[...] = packed[...].T


def fill(c, t, z, bands, slopes, mat, side, reach):
    params = PC * PC
    lane = iota((8, 128), 1)
    gap = lane - iota((8, 128), 0)
    column = pltpu.roll(slopes[...], params - z, 1)
    ahead = 1 if c == 0 else -1

    def rows_of(depth):
        found = []
        for n, (x, y, dz) in enumerate(BANDS):
            if dz == depth * ahead:
                row = bands[n, pl.ds(z + depth * ahead, 1), :]
                found.append((PC * x + y, jnp.broadcast_to(row, (8, 128))))
        return found

    parts = [rows_of(depth) for depth in range(reach + 1)]
    for q in range(-(-params // 8)):
        here = slice(8 * q, 8 * q + 8)
        inside = lane < params

        def block(entries):
            value = jnp.zeros((8, 128), F32)
            for offset, row in entries:
                value = jnp.where(gap == 8 * q + offset, row, value)
            return jnp.where(inside, value, 0.0)

        mat[c, t, here, :] = block(parts[0])
        first = block(parts[1]) if reach > 0 else jnp.zeros((8, 128), F32)
        side[c, t, here, 0:128] = jnp.where(lane == params, column[here], first)
        if reach > 1:
            side[c, t, here, 128:256] = block(parts[2])


def assemble(bands, slopes, mat, side):
    meet = PC // 2 - 1
    for at in (meet, meet + 1):
        mat[1, at] = jnp.zeros(mat.shape[2:], F32)
        for c in range(2):
            side[c, at] = jnp.zeros(side.shape[2:], F32)

    def both(t, _):
        fill(0, t, t, bands, slopes, mat, side, 2)
        fill(1, t, PC - 1 - t, bands, slopes, mat, side, 2)
        return 0

    lax.fori_loop(0, meet, both, 0)
    fill(0, meet, meet, bands, slopes, mat, side, 1)
    fill(0, meet + 1, meet + 1, bands, slopes, mat, side, 0)


GROUPS = 5


def factored(blocks, count):
    lane = iota((8, 128), 1)
    sub = iota((8, 128), 0)
    tiles = -(-count // 8)
    chains = range(len(blocks))

    def over_lanes(value, at):
        return jnp.broadcast_to(value[:, at : at + 1], value.shape)

    def over_rows(value, at):
        return jnp.broadcast_to(value[at : at + 1, :], value.shape)

    grids = [[block[8 * q : 8 * q + 8] for q in range(tiles)] for block in blocks]
    lower = [[] for _ in blocks]
    scaled = [[] for _ in blocks]
    first = 0
    while first < tiles:
        last = min(first + GROUPS, tiles)
        for p in range(first, last):
            width = min(8, count - 8 * p)
            within = (lane >= 8 * p) & (lane < 8 * p + width)
            unit = jnp.where(lane - 8 * p == sub, 1.0, 0.0)
            for c in chains:
                grid = grids[c]
                panel = grid[p]
                columns = [over_lanes(panel, 8 * p + n) for n in range(width)]
                panel = jnp.where(within, unit, panel)
                lower[c].append(panel)
                rows = [over_rows(panel, n) for n in range(width)]
                for i in range(width):
                    j = 8 * p + i
                    column = columns[i]
                    pivot = 1.0 / over_rows(column, i)
                    row = over_rows(panel, i) * pivot
                    for n in range(i + 1, width):
                        crossing = over_rows(columns[n], i) * pivot
                        columns[n] = jnp.where(sub == i, crossing, columns[n] - column * crossing)
                    panel = jnp.where(sub == i, row, panel - column * row)
                rows = [over_rows(panel, n) for n in range(width)]
                panel = rows[0]
                for n in range(1, width):
                    panel = jnp.where(sub == n, rows[n], panel)
                scaled[c].append(panel)
                for q in range(p + 1, last):
                    old = grid[q]
                    terms = [over_lanes(old, 8 * p + n) * row for n, row in enumerate(rows)]
                    while len(terms) > 1:
                        pairs = [terms[n] + terms[n + 1] for n in range(0, len(terms) - 1, 2)]
                        terms = pairs + terms[len(terms) - len(terms) % 2 :]
                    grid[q] = jnp.where(within, 0.0, old) - terms[0]
        if last < tiles:
            within = (lane >= 8 * first) & (lane < 8 * last)
            for c in chains:
                low = jnp.concatenate(lower[c][first:last], axis=0)
                high = jnp.concatenate(
                    [
                        jnp.where((lane < 8 * p + 8) | (lane >= 8 * last), scaled[c][p], 0.0)
                        for p in range(first, last)
                    ],
                    axis=0,
                )
                change = dot(low, high, (0, 0))
                for q in range(last, tiles):
                    old = jnp.where(within, 0.0, grids[c][q])
                    grids[c][q] = old - change[8 * q : 8 * q + 8]
        first = last

    def trimmed(parts):
        kept = []
        for p, part in enumerate(parts):
            limit = min(8 * p + 8, count)
            kept.append(jnp.where((lane < limit) & (sub < limit - 8 * p), part, 0.0))
        return jnp.concatenate(kept, axis=0)

    return [(trimmed(lower[c]), trimmed(scaled[c])) for c in chains]


def eliminate(t, chains, size, mat, side, lowers, solved, more=True):
    params = PC * PC
    mark = iota((128, 128), 1) == params
    blocks = [mat[c, t, :size, :] for c in chains]
    for c, (low, high) in zip(chains, factored(blocks, params)):
        lowers[c, t, :size, :] = low
        right = side[c, t, :size, :]
        z = dot(high[:, :size], right, (1, 0))
        solved[c, t, :size, :] = z
        if not more:
            continue
        y = dot(low[:, :size], right, (1, 0))
        schur = dot(y, z, (0, 0))
        near, far = schur[:128], schur[128:]
        mat[c, t + 1] -= near[:, :128]
        side[c, t + 1, :, 0:128] -= jnp.where(mark, near[:, :128], near[:, 128:])
        mat[c, t + 2] -= far[:, 128:]
        side[c, t + 2, :, 0:128] -= jnp.where(mark, far[:, :128], 0.0)


def solve_zone(size, mat, side, lowers, solved, spread):
    params = PC * PC
    meet = PC // 2 - 1
    mark = iota((128, 128), 1) == params
    for ref in (lowers, solved):
        ref[:, :, size:, :] = jnp.zeros((*ref.shape[:2], ref.shape[2] - size, ref.shape[3]), F32)

    def both(t, _):
        eliminate(t, (0, 1), size, mat, side, lowers, solved)
        return 0

    lax.fori_loop(0, meet, both, 0)
    mat[0, meet] += mat[1, meet + 1]
    mat[0, meet + 1] += mat[1, meet]
    turned = side[1, meet, :, 0:128].T
    side[0, meet, :, 0:128] += jnp.where(mark, side[1, meet + 1, :, 0:128], turned)
    side[0, meet + 1, :, 0:128] += jnp.where(mark, side[1, meet, :, 0:128], 0.0)
    eliminate(meet, (0,), size, mat, side, lowers, solved)
    eliminate(meet + 1, (0,), size, mat, side, lowers, solved, more=False)

    flag = iota((8, 128), 1) == params

    def back(c, t, near, far):
        row = jnp.concatenate([jnp.where(flag, -1.0, near), far], axis=1)
        value = dot(row, solved[c, t], (1, 1))
        return -dot(value, lowers[c, t], (1, 0))

    blank = jnp.zeros((8, 128), F32)
    rows = [blank] * PC
    rows[meet + 1] = back(0, meet + 1, blank, blank)
    rows[meet] = back(0, meet, rows[meet + 1], blank)
    for t in range(meet - 1, -1, -1):
        rows[t] = back(0, t, rows[t + 1], rows[t + 2])
        z = PC - 1 - t
        rows[z] = back(1, t, rows[z - 1], rows[z - 2])
    spread[...] = jnp.zeros_like(spread)
    for z in range(PC):
        spread[2 * z + 1 : 2 * z + 3, :] = -rows[z][:2]
    spread[...] = spread[...].T


def place_zone(begin, zone_m, spread, temp, added):
    rows = zone_m.shape[1]
    span = 2 * PC

    def ramp(position):
        value = jnp.sin(math.pi * (position.astype(F32) - 0.5) / span)
        return jnp.where((position >= 1) & (position <= span), value, 0.0)

    weight = ramp(iota((rows, 128), 0)) * ramp(iota((rows, 128), 1))
    temp[0] = jnp.zeros_like(weight)
    shift = lax.rem(begin[2] + added.shape[2], added.shape[2])
    for x in range(PC):
        part = spread[x * PC : (x + 1) * PC, :]
        temp[0, pl.ds(1, PC, stride=2), :] = part
        temp[0, pl.ds(2, PC, stride=2), :] = part
        value = weight * temp[0]
        for a in range(2):
            at = 2 * x + 1 + a
            plane = value * math.sin(math.pi * (at - 0.5) / span) * zone_m[at]
            plane = jnp.pad(plane, ((0, added.shape[1] - rows), (0, 0)))
            plane = pltpu.roll(plane, begin[1], 0)
            plane = jnp.pad(plane, ((0, 0), (0, added.shape[2] - 128)))
            added[begin[0] + at] += pltpu.roll(plane, shift, 1)


def cut_zone(begin, depth, zone_all_u, zone_all_w, zone_u, zone_f, zone_m):
    count, rows = zone_m.shape[:2]
    whole_rows, whole_lanes = zone_all_u.shape[-2:]
    shift_y = lax.rem(whole_rows - begin[1], whole_rows)
    shift = lax.rem(whole_lanes - begin[2], whole_lanes)
    z = begin[2] + iota((rows, 128), 1)
    inside = (z >= 0) & (z < depth) & (iota((rows, 128), 0) < count)

    def cut(x, _):
        def take(ref, k):
            plane = pltpu.roll(ref[k, begin[0] + x], shift, 1)[:, :128]
            return jnp.where(inside, pltpu.roll(plane, shift_y, 0)[:rows], 0.0)

        for k in range(3):
            zone_u[k, x] = take(zone_all_u, k)
            zone_f[k, x] = take(zone_all_w, k)
        zone_m[x] = take(zone_all_w, 3)
        return 0

    lax.fori_loop(0, count, cut, 0)


def zone_kernel(counts, brick, margins, where, zone_all_u, zone_all_w, field_out, added, *scratch):
    scratch, (corners, ready) = scratch[:-2], scratch[-2:]
    zone_u, zone_f, zone_m = scratch[:3]
    temp, fields, packed, flat, bands, slopes, mat, side, lowers, solved, spread = scratch[3:]
    bx, by, bz = brick
    hx, hy = margins
    here = [lax.axis_index(name) for name in AXES]
    lanes = pl.ds(pl.multiple_of(here[2] * bz, bz), bz)
    fetch = pltpu.make_async_copy(where, corners, ready.at[0])
    fetch.start()
    inner = zone_all_u.at[:, hx : hx + bx, hy : hy + by, lanes]
    store = pltpu.make_async_copy(inner, field_out, ready.at[1])
    store.start()
    added[...] = jnp.zeros_like(added)
    fetch.wait()
    for number in range(corners.shape[0]):
        begin = [
            corners[number, 0] - here[0] * bx + hx - 1,
            corners[number, 1] - here[1] * by + hy - 1,
            corners[number, 2] - 1,
        ]
        cut_zone(begin, counts[2] * bz, zone_all_u, zone_all_w, zone_u, zone_f, zone_m)
        rest = fields.shape[1] - PC * PC
        fields[:, PC * PC :, :] = jnp.zeros((fields.shape[0], rest, 128), F32)
        coarse_fields(zone_u, zone_f, zone_m, temp, fields)
        transpose_fields(fields, packed, flat)
        band_sums(flat, packed, bands, slopes)
        assemble(bands, slopes, mat, side)
        solve_zone(fields.shape[1], mat, side, lowers, solved, spread)
        place_zone(begin, zone_m, spread, temp, added)
    store.wait()


def body(forcing, start_field, modulus, corners):
    brick = modulus.shape
    bx, by, bz = brick
    counts = [lax.axis_size(name) for name in AXES]
    margins = (HALO, -(-HALO // 8) * 8)
    span = [size + 2 * margin for size, margin in zip(brick, margins)] + [counts[2] * bz]
    whole = pl.BlockSpec(memory_space=pltpu.VMEM)
    dma = pltpu.SemaphoreType.DMA
    peers = max(counts[2] - 1, 1)
    zone_all_u, zone_all_w = pl.pallas_call(
        functools.partial(sweep_kernel, counts, brick, margins),
        out_shape=(
            jax.ShapeDtypeStruct((3, *span), F32),
            jax.ShapeDtypeStruct((4, *span), F32),
        ),
        in_specs=[pl.BlockSpec(memory_space=pltpu.HBM)] * 3,
        out_specs=(whole, whole),
        scratch_shapes=[
            pltpu.VMEM((4, bx + 2, by, bz), F32),
            *[pltpu.VMEM((3, bx + 2, by, bz), F32)] * (FSWEEPS - 1),
            pltpu.VMEM((FSWEEPS, 2, 4, bx, bz), F32),
            pltpu.VMEM((FSWEEPS, 2, 4, bx, bz), F32),
            pltpu.VMEM((2, 4, bx, by, bz), F32),
            *[pltpu.VMEM((2, 3, bx, by, bz), F32)] * (FSWEEPS - 1),
            pltpu.VMEM((6, bx, by, bz), F32),
            pltpu.VMEM((bx, by, bz), F32),
            dma((FSWEEPS, 4, len(FACES))),
            dma((FSWEEPS, 4, len(FACES))),
            dma((FSWEEPS + 3, len(AROUND))),
            dma((FSWEEPS + 3, len(AROUND))),
            dma((FSWEEPS + 3, len(AROUND) + 1, peers)),
            dma((FSWEEPS + 3, len(AROUND) + 1, peers)),
            dma((4,)),
        ],
        compiler_params=pltpu.CompilerParams(
            collective_id=0, has_side_effects=True, vmem_limit_bytes=40 * 1024 * 1024
        ),
        name="sweeps",
    )(*[pltpu.with_memory_space_constraint(each, pltpu.HBM) for each in (forcing, start_field, modulus)])
    zone_span = 2 * PC + 2
    zone_rows = -(-zone_span // 8) * 8
    size = -(-PC * PC // 8) * 8
    planes = PC // 2 + 3
    field, added = pl.pallas_call(
        functools.partial(zone_kernel, counts, brick, margins),
        out_shape=(
            jax.ShapeDtypeStruct(forcing.shape, F32),
            jax.ShapeDtypeStruct(tuple(span), F32),
        ),
        in_specs=[pl.BlockSpec(memory_space=pltpu.HBM), whole, whole],
        out_specs=(pl.BlockSpec(memory_space=pl.ANY), whole),
        scratch_shapes=[
            pltpu.VMEM((3, zone_span, zone_rows, 128), F32),
            pltpu.VMEM((3, zone_span, zone_rows, 128), F32),
            pltpu.VMEM((zone_span, zone_rows, 128), F32),
            pltpu.VMEM((3 * FIELDS, zone_rows, 128), F32),
            pltpu.VMEM((3 * FIELDS, size, 128), F32),
            pltpu.VMEM((128, 128), F32),
            pltpu.VMEM((3 * FIELDS, 16, 128), F32),
            pltpu.VMEM((len(BANDS), 16, 128), F32),
            pltpu.VMEM((128, 128), F32),
            pltpu.VMEM((2, planes, 128, 128), F32),
            pltpu.VMEM((2, planes, 128, 256), F32),
            pltpu.VMEM((2, planes, 128, 128), F32),
            pltpu.VMEM((2, planes, 128, 256), F32),
            pltpu.VMEM((128, 128), F32),
            pltpu.SMEM(corners.shape, jnp.int32),
            dma((2,)),
        ],
        compiler_params=pltpu.CompilerParams(vmem_limit_bytes=40 * 1024 * 1024),
        name="zone",
    )(pltpu.with_memory_space_constraint(corners, pltpu.HBM), zone_all_u, zone_all_w)
    updated = pl.pallas_call(
        functools.partial(gather_kernel, counts, brick, margins),
        out_shape=jax.ShapeDtypeStruct(brick, F32),
        in_specs=[whole, whole],
        out_specs=whole,
        scratch_shapes=[
            pltpu.VMEM((span[0], span[1], bz), F32),
            pltpu.VMEM((peers, span[0], span[1], bz), F32),
            pltpu.VMEM((2, HALO - 1, by, bz), F32),
            pltpu.VMEM((2, bx, HALO - 1, bz), F32),
            pltpu.VMEM((4, HALO - 1, HALO - 1, bz), F32),
            dma((len(AROUND),)),
            dma((len(AROUND),)),
            dma((peers,)),
            dma((peers,)),
        ],
        compiler_params=pltpu.CompilerParams(
            collective_id=1, has_side_effects=True, vmem_limit_bytes=40 * 1024 * 1024
        ),
        name="gather",
    )(added, modulus)
    return (field, updated)


def solution(mesh):
    placed = (
        P(None, "gx", "gy", "gz"),
        P(None, "gx", "gy", "gz"),
        P("gx", "gy", "gz"),
        P(("gx", "gy", "gz"), None),
    )
    return jax.shard_map(
        body,
        mesh=mesh,
        in_specs=placed,
        out_specs=(P(None, "gx", "gy", "gz"), P("gx", "gy", "gz")),
        check_vma=False,
    )
```

```python
import functools
import math

import jax
import jax.numpy as jnp
from jax import lax
from jax.experimental import pallas as pl
from jax.experimental.pallas import tpu as pltpu
from jax.sharding import PartitionSpec as P

PC = 10
HALO = 6
FSWEEPS = 4


MASS_TERM = 0.5
DAMPING = 0.1
EPSILON = 1e-06
HIGHEST = lax.Precision.HIGHEST
F32 = jnp.float32


def dot(a, b, contract, precision=lax.Precision.HIGH):
    return lax.dot_general(
        a, b, ((contract[:1], contract[1:]), ((), ())), precision=precision, preferred_element_type=F32
    )


def roll(values, shift, axis):
    return pltpu.roll(values, shift % values.shape[axis], axis)


def iota(shape, axis):
    return lax.broadcasted_iota(jnp.int32, shape, axis)


MESH_ID = pl.DeviceIdType.MESH
AXES = ("gx", "gy", "gz")
AROUND = tuple((dx, dy) for dx in (-1, 0, 1) for dy in (-1, 0, 1) if (dx, dy) != (0, 0))
FACES = ((-1, 0, 0), (1, 0, 0), (0, -1, 0), (0, 1, 0), (0, 0, -1), (0, 0, 1))


def each(count, step, width):
    while count % width:
        width -= 1

    def several(n, _):
        for i in range(width):
            step(width * n + i, 0)
        return 0

    lax.fori_loop(0, count // width, several, 0)


class Place:
    def __init__(self, counts):
        self.counts = counts
        self.here = [lax.axis_index(name) for name in AXES]

    def exists(self, step):
        inside = None
        for at, count, move in zip(self.here, self.counts, step):
            if move:
                test = at + move < count if move > 0 else at + move >= 0
                inside = test if inside is None else inside & test
        return inside

    def device(self, step):
        return tuple(at + move for at, move in zip(self.here, step))

    def peer(self, turn):
        return self.here[:2] + [lax.rem(self.here[2] + turn, self.counts[2])]

    def call(self):
        barrier = pltpu.get_barrier_semaphore()
        total = self.counts[2] - 1
        for dx, dy in AROUND:
            step = (dx, dy, 0)

            @pl.when(self.exists(step))
            def _():
                pl.semaphore_signal(
                    barrier, inc=1, device_id=self.device(step), device_id_type=MESH_ID
                )

            total = total + self.exists(step).astype(jnp.int32)
        for turn in range(1, self.counts[2]):
            pl.semaphore_signal(
                barrier, inc=1, device_id=tuple(self.peer(turn)), device_id_type=MESH_ID
            )
        return barrier, total


def opposite(step):
    return tuple(-move for move in step)


class Message:
    def __init__(self, place, step, source, target, send, recv):
        self.place, self.step = place, step
        self.copy = pltpu.make_async_remote_copy(
            src_ref=source,
            dst_ref=target,
            send_sem=send,
            recv_sem=recv,
            device_id=place.device(step),
            device_id_type=MESH_ID,
        )

    def start(self):
        pl.when(self.place.exists(self.step))(self.copy.start)

    def sent(self):
        pl.when(self.place.exists(self.step))(self.copy.wait_send)

    def arrived(self):
        pl.when(self.place.exists(opposite(self.step)))(self.copy.wait_recv)


def edge_span(move, size, margin, reach=None):
    reach = margin if reach is None else reach
    if move > 0:
        return slice(margin + size - reach, margin + size), slice(margin - reach, margin)
    if move < 0:
        far = margin + size
        return slice(margin, margin + reach), slice(far, far + reach)
    return slice(margin, margin + size), slice(margin, margin + size)


def regions(brick, margins, reach):
    found = []
    for dx, dy in AROUND:
        from_x, to_x = edge_span(dx, brick[0], margins[0], reach)
        from_y, to_y = edge_span(dy, brick[1], margins[1], reach)
        found.append(((dx, dy, 0), (from_x, from_y), (to_x, to_y)))
    return sorted(found, key=lambda entry: (entry[0][1] == 0, entry[0][0] == 0))


def spread_messages(place, brick, margins, ref, lanes, send, recv, reach):
    return [
        Message(
            place,
            step,
            ref.at[:, source[0], source[1], lanes],
            ref.at[:, target[0], target[1], lanes],
            send.at[n],
            recv.at[n],
        )
        for n, (step, source, target) in enumerate(regions(brick, margins, reach))
    ]


class Relay:
    def __init__(self, place, step, ref, lanes, span, send, recv):
        self.place, self.step = place, step
        view = ref.at[:, span[0], span[1], lanes]
        self.copies = [
            pltpu.make_async_remote_copy(
                src_ref=view,
                dst_ref=view,
                send_sem=send.at[turn - 1],
                recv_sem=recv.at[turn - 1],
                device_id=tuple(place.peer(turn)),
                device_id_type=MESH_ID,
            )
            for turn in range(1, place.counts[2])
        ]

    def when(self, action):
        test = self.place.exists(self.step) if any(self.step) else None
        action() if test is None else pl.when(test)(action)

    def start(self):
        self.when(lambda: [copy.start() for copy in self.copies] and None)

    def wait(self):
        self.when(lambda: [copy.wait() for copy in self.copies] and None)


def clear_outside(place, brick, margins, refs, lanes):
    for dx, dy in AROUND:
        _, to_x = edge_span(-dx, brick[0], margins[0])
        _, to_y = edge_span(-dy, brick[1], margins[1])

        @pl.when(jnp.logical_not(place.exists((dx, dy, 0))))
        def _():
            for ref in refs:
                for k in range(ref.shape[0]):
                    shape = (to_x.stop - to_x.start, to_y.stop - to_y.start, lanes.size)
                    ref[k, to_x, to_y, lanes] = jnp.zeros(shape, F32)


def sweep_kernel(counts, brick, margins, forcing, start, modulus, zone_u, zone_w, *scratch):
    fields, rows_in, rows_out, sides = scratch[0:4], scratch[4], scratch[5], scratch[6:10]
    coupling, inverse = scratch[10:12]
    face_send, face_recv, bulk_send, bulk_recv, peer_send, peer_recv, load = scratch[12:]
    place = Place(counts)
    bx, by, bz = brick
    hx, hy = margins
    lanes = pl.ds(pl.multiple_of(place.here[2] * bz, bz), bz)
    every = pl.ds(0, counts[2] * bz)
    row = iota((by, bz), 0)
    lane = iota((by, bz), 1)
    own = (slice(hx, hx + bx), slice(hy, hy + by))
    loads = [
        pltpu.make_async_copy(start, fields[0].at[:3, 1 : bx + 1], load.at[0]),
        pltpu.make_async_copy(modulus, fields[0].at[3, 1 : bx + 1], load.at[1]),
        pltpu.make_async_copy(modulus, zone_w.at[3, own[0], own[1], lanes], load.at[2]),
        pltpu.make_async_copy(forcing, zone_w.at[:3, own[0], own[1], lanes], load.at[3]),
    ]
    for copy in loads:
        copy.start()
    barrier, greetings = place.call()

    for n, (dx, dy, dz) in enumerate(FACES):

        @pl.when(jnp.logical_not(place.exists((dx, dy, dz))))
        def _():
            for sweep in range(FSWEEPS):
                if dx:
                    plane = 0 if dx < 0 else bx + 1
                    for k in range(fields[sweep].shape[0]):
                        fields[sweep][k, plane] = jnp.zeros((by, bz), F32)
                elif dy:
                    for k in range(4):
                        rows_in[sweep, 0 if dy < 0 else 1, k] = jnp.zeros((bx, bz), F32)
                else:
                    for k in range(sides[sweep].shape[1]):
                        blank = jnp.zeros((bx, by, bz), F32)
                        sides[sweep][0 if dz < 0 else 1, k] = blank

    loads[0].wait()
    loads[1].wait()

    def stage(x, _):
        for k in range(4):
            u = fields[0][k, x + 1]
            rows_out[0, 0, k, pl.ds(x, 1), :] = u[:1]
            rows_out[0, 1, k, pl.ds(x, 1), :] = u[by - 1 :]
        return 0

    each(bx, stage, 4)

    def faces(sweep, k):
        field = fields[sweep]
        messages = []
        for n, step in enumerate(FACES):
            dx, dy, dz = step
            if dx:
                source = field.at[k, bx if dx > 0 else 1]
                target = field.at[k, 0 if dx > 0 else bx + 1]
            elif dy:
                source = rows_out.at[sweep, 1 if dy > 0 else 0, k]
                target = rows_in.at[sweep, 0 if dy > 0 else 1, k]
            else:
                source = field.at[k, 1 : bx + 1]
                target = sides[sweep].at[0 if dz > 0 else 1, k]
            at = (sweep, k, n)
            messages.append(
                Message(place, step, source, target, face_send.at[at], face_recv.at[at])
            )
        return messages

    def relays(first, last, slot, ref, reach):
        view = ref.at[first:last]
        entries = [((0, 0, 0), own)]
        entries += [(opposite(step), target) for step, _, target in regions(brick, margins, reach)]
        return [
            Relay(place, step, view, lanes, span, peer_send.at[slot, n], peer_recv.at[slot, n])
            for n, (step, span) in enumerate(entries)
        ]

    pl.semaphore_wait(barrier, greetings)
    waiting = {(0, k): faces(0, k) for k in (3, 0, 1, 2)}
    pending = sum(waiting.values(), [])
    for message in pending:
        message.start()
    loads[2].wait()
    loads[3].wait()
    bulk, forward = [], []
    for slot, (first, last, reach) in enumerate(((3, 4, HALO), (0, 1, HALO - 1), (1, 2, HALO - 1), (2, 3, HALO - 1))):
        bulk.append(
            spread_messages(
                place,
                brick,
                margins,
                zone_w.at[first:last],
                lanes,
                bulk_send.at[slot],
                bulk_recv.at[slot],
                reach,
            )
        )
        forward.append(relays(first, last, slot, zone_w, reach))

    def around(sweep, k, x, u):
        low, high = rows_in[sweep, 0, k, pl.ds(x, 1), :], rows_in[sweep, 1, k, pl.ds(x, 1), :]
        y_up = jnp.where(row == by - 1, jnp.broadcast_to(high, u.shape), roll(u, -1, 0))
        y_down = jnp.where(row == 0, jnp.broadcast_to(low, u.shape), roll(u, 1, 0))
        below, above = sides[sweep][0, k, x], sides[sweep][1, k, x]
        z_up = jnp.where(lane == bz - 1, roll(above, -1, 1), roll(u, -1, 1))
        z_down = jnp.where(lane == 0, roll(below, 1, 1), roll(u, 1, 1))
        field = fields[sweep]
        return field[k, x + 2], field[k, x], y_up, y_down, z_up, z_down

    def couple(x, _):
        m = fields[0][3, x + 1]
        below = MASS_TERM
        for n, other in enumerate(around(0, 3, x, m)):
            face = 0.5 * (m + other)
            coupling[n, x] = face
            below = below + face
        inverse[x] = 1.0 / below
        return 0

    for sweep in range(FSWEEPS):
        for message in bulk[sweep]:
            message.start()
        forward[sweep][0].start()
        if sweep == 0:
            clear_outside(place, brick, margins, (zone_u, zone_w), every)
            for message in waiting[0, 3]:
                message.arrived()
            each(bx, couple, 2)
        for k in range(3):
            for message in waiting[sweep, k]:
                message.arrived()

            def relax(x, _, sweep=sweep, k=k):
                u = fields[sweep][k, x + 1]
                total = zone_w[k, hx + x, hy : hy + by, lanes]
                for n, other in enumerate(around(sweep, k, x, u)):
                    total = total + coupling[n, x] * other
                total = total * inverse[x]
                if sweep < FSWEEPS - 1:
                    fields[sweep + 1][k, x + 1] = total
                    rows_out[sweep + 1, 0, k, pl.ds(x, 1), :] = total[:1]
                    rows_out[sweep + 1, 1, k, pl.ds(x, 1), :] = total[by - 1 :]
                else:
                    zone_u[k, hx + x, hy : hy + by, lanes] = total
                return 0

            each(bx, relax, 4)
            if sweep < FSWEEPS - 1:
                waiting[sweep + 1, k] = faces(sweep + 1, k)
                pending += waiting[sweep + 1, k]
                for message in waiting[sweep + 1, k]:
                    message.start()
            else:
                slot = FSWEEPS + k
                final = spread_messages(
                    place,
                    brick,
                    margins,
                    zone_u.at[k : k + 1],
                    lanes,
                    bulk_send.at[slot],
                    bulk_recv.at[slot],
                    HALO,
                )
                for message in final:
                    message.start()
                bulk.append(final)
                forward.append(relays(k, k + 1, slot, zone_u, HALO))
                forward[slot][0].start()
    for group, onward in zip(bulk, forward):
        for message, relay in zip(group, onward[1:]):
            message.arrived()
            relay.start()
    for message in pending + sum(bulk, []):
        message.sent()
    for relay in sum(forward, []):
        relay.wait()


def gather_kernel(counts, brick, margins, added, modulus, out, total, from_peer, *scratch):
    from_x, from_y, from_xy, send, recv, peer_send, peer_recv = scratch
    place = Place(counts)
    bx, by, bz = brick
    hx, hy = margins

    def part(turn):
        at = lax.rem(place.here[2] + turn, counts[2])
        return pl.ds(pl.multiple_of(at * bz, bz), bz)

    targets = {}
    for n, (dx, dy) in enumerate(AROUND):
        if dy == 0:
            targets[n] = from_x.at[(dx + 1) // 2]
        elif dx == 0:
            targets[n] = from_y.at[(dy + 1) // 2]
        else:
            targets[n] = from_xy.at[dx + 1 + (dy + 1) // 2]

    barrier, greetings = place.call()
    for n, (dx, dy) in enumerate(AROUND):

        @pl.when(jnp.logical_not(place.exists((-dx, -dy, 0))))
        def _():
            targets[n][...] = jnp.zeros(targets[n].shape, F32)

    pl.semaphore_wait(barrier, greetings)
    copies = [
        pltpu.make_async_remote_copy(
            src_ref=added.at[:, :, part(turn)],
            dst_ref=from_peer.at[turn - 1],
            send_sem=peer_send.at[turn - 1],
            recv_sem=peer_recv.at[turn - 1],
            device_id=tuple(place.peer(turn)),
            device_id_type=MESH_ID,
        )
        for turn in range(1, counts[2])
    ]
    for copy in copies:
        copy.start()
    for copy in copies:
        copy.wait_recv()

    def collect(x, _):
        value = added[x, :, part(0)]
        for turn in range(1, counts[2]):
            value = value + from_peer[turn - 1, x]
        total[x] = value
        return 0

    lax.fori_loop(0, total.shape[0], collect, 0)
    messages = []
    for n, (dx, dy) in enumerate(AROUND):
        _, at_x = edge_span(-dx, bx, hx, HALO - 1)
        _, at_y = edge_span(-dy, by, hy, HALO - 1)
        messages.append(
            Message(place, (dx, dy, 0), total.at[at_x, at_y], targets[n], send.at[n], recv.at[n])
        )
    for message in messages:
        message.start()

    def centre(x, _):
        out[x] = modulus[x] + total[hx + x, hy : hy + by, :]
        return 0

    lax.fori_loop(0, bx, centre, 0)
    for message in messages:
        message.arrived()
    for n, (dx, dy) in enumerate(AROUND):
        to_x, _ = edge_span(-dx, bx, hx, HALO - 1)
        to_y, _ = edge_span(-dy, by, hy, HALO - 1)
        out[to_x.start - hx : to_x.stop - hx, to_y.start - hy : to_y.stop - hy, :] += targets[n][...]
    for message in messages:
        message.sent()
    for copy in copies:
        copy.wait_send()


FIELDS = 8


def coarse_fields(zone_u, zone_f, zone_m, temp, fields):
    rows = zone_m.shape[1]
    first_y = iota((rows, 128), 0) % 2 == 1
    first_z = iota((rows, 128), 1) % 2 == 1
    rank = iota((PC, 128), 0)
    lane = iota((PC, 128), 1)
    steps = ((0, 1), (0, -1), (1, 1), (1, -1), (2, 1), (2, -1))
    for x in range(PC):
        middles, others = [], []
        for a in range(2):
            at = 2 * x + 1 + a
            m = zone_m[at]
            middles.append(m)
            others.append(
                [
                    zone_m[at + step] if axis == 0 else roll(m, -step, axis - 1)
                    for axis, step in steps
                ]
            )
        for k in range(3):
            sums = [None] * FIELDS

            def put(number, value):
                sums[number] = value if sums[number] is None else sums[number] + value

            for a in range(2):
                at = 2 * x + 1 + a
                u, m = zone_u[k, at], middles[a]
                applied = MASS_TERM * u
                laplace = jnp.zeros_like(u)
                for number, (axis, step) in enumerate(steps):
                    u_next = zone_u[k, at + step] if axis == 0 else roll(u, -step, axis - 1)
                    m_next = others[a][number]
                    change = u - u_next
                    applied = applied + 0.5 * (m + m_next) * change
                    laplace = laplace + change
                    flow = -0.5 * m_next * change
                    if axis == 0:
                        same = (a == 0) == (step == 1)
                        put(0 if same else 1 + number, flow)
                    else:
                        first = first_y if axis == 1 else first_z
                        near = first if step == 1 else ~first
                        put(0, jnp.where(near, flow, 0.0))
                        put(1 + number, jnp.where(near, 0.0, flow))
                put(0, -0.5 * m * laplace)
                put(7, zone_f[k, at] - applied)
            for number in range(FIELDS):
                slot = temp.at[k * FIELDS + number]
                slot[...] = sums[number]
                pair = slot[pl.ds(1, PC, stride=2), :] + slot[pl.ds(2, PC, stride=2), :]
                pair = pair + roll(pair, -1, 1)
                keep = (lane % 2 == 1) & (lane < 2 * PC)
                if number == 1 and x == PC - 1 or number == 2 and x == 0:
                    keep = jnp.zeros_like(keep)
                if number == 3:
                    keep = keep & (rank < PC - 1)
                if number == 4:
                    keep = keep & (rank > 0)
                if number == 5:
                    keep = keep & (lane < 2 * PC - 2)
                if number == 6:
                    keep = keep & (lane > 1)
                fields[k * FIELDS + number, x * PC : (x + 1) * PC, :] = jnp.where(keep, pair, 0.0)


PAIRS = ((0, 0, 0), (1, 0, 0), (-1, 0, 0), (0, 1, 0), (0, -1, 0), (0, 0, 1), (0, 0, -1))
BANDS = tuple(
    sorted({tuple(b - a for a, b in zip(one, two)) for one in PAIRS for two in PAIRS})
)
PER_GROUP = 12


def transpose_fields(fields, packed, flat):
    size = fields.shape[1]
    flat[...] = jnp.zeros_like(flat)
    for group in range(2):
        total = None
        for j in range(PER_GROUP):
            shift = 2 * PC * (j // 2) - 1 + j % 2
            part = fields[group * PER_GROUP + j]
            part = roll(part, shift, 1) if shift else part
            total = part if total is None else total + part
        packed[:size, :] = total
        packed[size:, :] = jnp.zeros((128 - size, 128), F32)
        packed[...] = packed[...].T
        for j in range(PER_GROUP):
            first = 2 * PC * (j // 2) + j % 2
            flat[group * PER_GROUP + j, :PC, :] = packed[pl.ds(first, PC, stride=2), :]


def band_sums(flat, packed, bands, slopes):
    columns = [[flat[k * FIELDS + n] for k in range(3)] for n in range(FIELDS)]

    def product(a, b):
        return sum(columns[a][k] * columns[b][k] for k in range(3))

    def moved(value, step):
        x, y, z = step
        value = roll(value, PC * x + y, 1) if x or y else value
        return roll(value, z, 0) if z else value

    totals = {}
    trace = None
    for a in range(len(PAIRS)):
        for b in range(a, len(PAIRS)):
            value = product(a, b)
            if a == b:
                trace = value if trace is None else trace + value
            for one, two in {(a, b), (b, a)}:
                key = tuple(q - p for p, q in zip(PAIRS[one], PAIRS[two]))
                part = moved(value, PAIRS[two])
                totals[key] = part if key not in totals else totals[key] + part
    trace = jnp.sum(jnp.sum(trace, axis=0, keepdims=True), axis=1, keepdims=True)
    ridge = DAMPING * trace / PC**3 + EPSILON
    totals[0, 0, 0] = totals[0, 0, 0] + ridge
    for n, key in enumerate(BANDS):
        bands[n] = totals[key]
    slope = None
    for a in range(len(PAIRS)):
        part = moved(product(a, FIELDS - 1), PAIRS[a])
        slope = part if slope is None else slope + part
    packed[...] = jnp.zeros_like(packed)
    packed[: slope.shape[0], :] = slope
    slopes[...] = packed[...].T


def fill(c, t, z, bands, slopes, mat, side, reach):
    params = PC * PC
    lane = iota((8, 128), 1)
    gap = lane - iota((8, 128), 0)
    column = pltpu.roll(slopes[...], params - z, 1)
    ahead = 1 if c == 0 else -1

    def rows_of(depth):
        found = []
        for n, (x, y, dz) in enumerate(BANDS):
            if dz == depth * ahead:
                row = bands[n, pl.ds(z + depth * ahead, 1), :]
                found.append((PC * x + y, jnp.broadcast_to(row, (8, 128))))
        return found

    parts = [rows_of(depth) for depth in range(reach + 1)]
    for q in range(-(-params // 8)):
        here = slice(8 * q, 8 * q + 8)
        inside = lane < params

        def block(entries):
            value = jnp.zeros((8, 128), F32)
            for offset, row in entries:
                value = jnp.where(gap == 8 * q + offset, row, value)
            return jnp.where(inside, value, 0.0)

        mat[c, t, here, :] = block(parts[0])
        first = block(parts[1]) if reach > 0 else jnp.zeros((8, 128), F32)
        side[c, t, here, 0:128] = jnp.where(lane == params, column[here], first)
        if reach > 1:
            side[c, t, here, 128:256] = block(parts[2])


def assemble(bands, slopes, mat, side):
    meet = PC // 2 - 1
    for at in (meet, meet + 1):
        mat[1, at] = jnp.zeros(mat.shape[2:], F32)
        for c in range(2):
            side[c, at] = jnp.zeros(side.shape[2:], F32)

    def both(t, _):
        fill(0, t, t, bands, slopes, mat, side, 2)
        fill(1, t, PC - 1 - t, bands, slopes, mat, side, 2)
        return 0

    lax.fori_loop(0, meet, both, 0)
    fill(0, meet, meet, bands, slopes, mat, side, 1)
    fill(0, meet + 1, meet + 1, bands, slopes, mat, side, 0)


GROUPS = 5


def factored(blocks, count):
    lane = iota((8, 128), 1)
    sub = iota((8, 128), 0)
    tiles = -(-count // 8)
    chains = range(len(blocks))

    def over_lanes(value, at):
        return jnp.broadcast_to(value[:, at : at + 1], value.shape)

    def over_rows(value, at):
        return jnp.broadcast_to(value[at : at + 1, :], value.shape)

    grids = [[block[8 * q : 8 * q + 8] for q in range(tiles)] for block in blocks]
    lower = [[] for _ in blocks]
    scaled = [[] for _ in blocks]
    first = 0
    while first < tiles:
        last = min(first + GROUPS, tiles)
        for p in range(first, last):
            width = min(8, count - 8 * p)
            within = (lane >= 8 * p) & (lane < 8 * p + width)
            unit = jnp.where(lane - 8 * p == sub, 1.0, 0.0)
            for c in chains:
                grid = grids[c]
                panel = grid[p]
                columns = [over_lanes(panel, 8 * p + n) for n in range(width)]
                panel = jnp.where(within, unit, panel)
                lower[c].append(panel)
                rows = [over_rows(panel, n) for n in range(width)]
                for i in range(width):
                    j = 8 * p + i
                    column = columns[i]
                    pivot = 1.0 / over_rows(column, i)
                    row = over_rows(panel, i) * pivot
                    for n in range(i + 1, width):
                        crossing = over_rows(columns[n], i) * pivot
                        columns[n] = jnp.where(sub == i, crossing, columns[n] - column * crossing)
                    panel = jnp.where(sub == i, row, panel - column * row)
                rows = [over_rows(panel, n) for n in range(width)]
                panel = rows[0]
                for n in range(1, width):
                    panel = jnp.where(sub == n, rows[n], panel)
                scaled[c].append(panel)
                for q in range(p + 1, last):
                    old = grid[q]
                    terms = [over_lanes(old, 8 * p + n) * row for n, row in enumerate(rows)]
                    while len(terms) > 1:
                        pairs = [terms[n] + terms[n + 1] for n in range(0, len(terms) - 1, 2)]
                        terms = pairs + terms[len(terms) - len(terms) % 2 :]
                    grid[q] = jnp.where(within, 0.0, old) - terms[0]
        if last < tiles:
            within = (lane >= 8 * first) & (lane < 8 * last)
            for c in chains:
                low = jnp.concatenate(lower[c][first:last], axis=0)
                high = jnp.concatenate(
                    [
                        jnp.where((lane < 8 * p + 8) | (lane >= 8 * last), scaled[c][p], 0.0)
                        for p in range(first, last)
                    ],
                    axis=0,
                )
                change = dot(low, high, (0, 0))
                for q in range(last, tiles):
                    old = jnp.where(within, 0.0, grids[c][q])
                    grids[c][q] = old - change[8 * q : 8 * q + 8]
        first = last

    def trimmed(parts):
        kept = []
        for p, part in enumerate(parts):
            limit = min(8 * p + 8, count)
            kept.append(jnp.where((lane < limit) & (sub < limit - 8 * p), part, 0.0))
        return jnp.concatenate(kept, axis=0)

    return [(trimmed(lower[c]), trimmed(scaled[c])) for c in chains]


def eliminate(t, chains, size, mat, side, lowers, solved, more=True):
    params = PC * PC
    mark = iota((128, 128), 1) == params
    blocks = [mat[c, t, :size, :] for c in chains]
    for c, (low, high) in zip(chains, factored(blocks, params)):
        lowers[c, t, :size, :] = low
        right = side[c, t, :size, :]
        z = dot(high[:, :size], right, (1, 0))
        solved[c, t, :size, :] = z
        if not more:
            continue
        y = dot(low[:, :size], right, (1, 0))
        schur = dot(y, z, (0, 0))
        near, far = schur[:128], schur[128:]
        mat[c, t + 1] -= near[:, :128]
        side[c, t + 1, :, 0:128] -= jnp.where(mark, near[:, :128], near[:, 128:])
        mat[c, t + 2] -= far[:, 128:]
        side[c, t + 2, :, 0:128] -= jnp.where(mark, far[:, :128], 0.0)


def solve_zone(size, mat, side, lowers, solved, spread):
    params = PC * PC
    meet = PC // 2 - 1
    mark = iota((128, 128), 1) == params
    for ref in (lowers, solved):
        ref[:, :, size:, :] = jnp.zeros((*ref.shape[:2], ref.shape[2] - size, ref.shape[3]), F32)

    def both(t, _):
        eliminate(t, (0, 1), size, mat, side, lowers, solved)
        return 0

    lax.fori_loop(0, meet, both, 0)
    mat[0, meet] += mat[1, meet + 1]
    mat[0, meet + 1] += mat[1, meet]
    turned = side[1, meet, :, 0:128].T
    side[0, meet, :, 0:128] += jnp.where(mark, side[1, meet + 1, :, 0:128], turned)
    side[0, meet + 1, :, 0:128] += jnp.where(mark, side[1, meet, :, 0:128], 0.0)
    eliminate(meet, (0,), size, mat, side, lowers, solved)
    eliminate(meet + 1, (0,), size, mat, side, lowers, solved, more=False)

    flag = iota((8, 128), 1) == params

    def back(c, t, near, far):
        row = jnp.concatenate([jnp.where(flag, -1.0, near), far], axis=1)
        value = dot(row, solved[c, t], (1, 1))
        return -dot(value, lowers[c, t], (1, 0))

    blank = jnp.zeros((8, 128), F32)
    rows = [blank] * PC
    rows[meet + 1] = back(0, meet + 1, blank, blank)
    rows[meet] = back(0, meet, rows[meet + 1], blank)
    for t in range(meet - 1, -1, -1):
        rows[t] = back(0, t, rows[t + 1], rows[t + 2])
        z = PC - 1 - t
        rows[z] = back(1, t, rows[z - 1], rows[z - 2])
    spread[...] = jnp.zeros_like(spread)
    for z in range(PC):
        spread[2 * z + 1 : 2 * z + 3, :] = -rows[z][:2]
    spread[...] = spread[...].T


def place_zone(begin, zone_m, spread, temp, added):
    rows = zone_m.shape[1]
    span = 2 * PC

    def ramp(position):
        value = jnp.sin(math.pi * (position.astype(F32) - 0.5) / span)
        return jnp.where((position >= 1) & (position <= span), value, 0.0)

    weight = ramp(iota((rows, 128), 0)) * ramp(iota((rows, 128), 1))
    temp[0] = jnp.zeros_like(weight)
    shift = lax.rem(begin[2] + added.shape[2], added.shape[2])
    for x in range(PC):
        part = spread[x * PC : (x + 1) * PC, :]
        temp[0, pl.ds(1, PC, stride=2), :] = part
        temp[0, pl.ds(2, PC, stride=2), :] = part
        value = weight * temp[0]
        for a in range(2):
            at = 2 * x + 1 + a
            plane = value * math.sin(math.pi * (at - 0.5) / span) * zone_m[at]
            plane = jnp.pad(plane, ((0, added.shape[1] - rows), (0, 0)))
            plane = pltpu.roll(plane, begin[1], 0)
            plane = jnp.pad(plane, ((0, 0), (0, added.shape[2] - 128)))
            added[begin[0] + at] += pltpu.roll(plane, shift, 1)


def cut_zone(begin, depth, zone_all_u, zone_all_w, zone_u, zone_f, zone_m):
    count, rows = zone_m.shape[:2]
    whole_rows, whole_lanes = zone_all_u.shape[-2:]
    shift_y = lax.rem(whole_rows - begin[1], whole_rows)
    shift = lax.rem(whole_lanes - begin[2], whole_lanes)
    z = begin[2] + iota((rows, 128), 1)
    inside = (z >= 0) & (z < depth) & (iota((rows, 128), 0) < count)

    def cut(x, _):
        def take(ref, k):
            plane = pltpu.roll(ref[k, begin[0] + x], shift, 1)[:, :128]
            return jnp.where(inside, pltpu.roll(plane, shift_y, 0)[:rows], 0.0)

        for k in range(3):
            zone_u[k, x] = take(zone_all_u, k)
            zone_f[k, x] = take(zone_all_w, k)
        zone_m[x] = take(zone_all_w, 3)
        return 0

    each(count, cut, 2)


def zone_kernel(counts, brick, margins, where, zone_all_u, zone_all_w, field_out, added, *scratch):
    scratch, (corners, ready) = scratch[:-2], scratch[-2:]
    zone_u, zone_f, zone_m = scratch[:3]
    temp, fields, packed, flat, bands, slopes, mat, side, lowers, solved, spread = scratch[3:]
    bx, by, bz = brick
    hx, hy = margins
    here = [lax.axis_index(name) for name in AXES]
    lanes = pl.ds(pl.multiple_of(here[2] * bz, bz), bz)
    fetch = pltpu.make_async_copy(where, corners, ready.at[0])
    fetch.start()
    inner = zone_all_u.at[:, hx : hx + bx, hy : hy + by, lanes]
    store = pltpu.make_async_copy(inner, field_out, ready.at[1])
    store.start()
    added[...] = jnp.zeros_like(added)
    fetch.wait()
    for number in range(corners.shape[0]):
        begin = [
            corners[number, 0] - here[0] * bx + hx - 1,
            corners[number, 1] - here[1] * by + hy - 1,
            corners[number, 2] - 1,
        ]
        cut_zone(begin, counts[2] * bz, zone_all_u, zone_all_w, zone_u, zone_f, zone_m)
        rest = fields.shape[1] - PC * PC
        fields[:, PC * PC :, :] = jnp.zeros((fields.shape[0], rest, 128), F32)
        coarse_fields(zone_u, zone_f, zone_m, temp, fields)
        transpose_fields(fields, packed, flat)
        band_sums(flat, packed, bands, slopes)
        assemble(bands, slopes, mat, side)
        solve_zone(fields.shape[1], mat, side, lowers, solved, spread)
        place_zone(begin, zone_m, spread, temp, added)
    store.wait()


def body(forcing, start_field, modulus, corners):
    brick = modulus.shape
    bx, by, bz = brick
    counts = [lax.axis_size(name) for name in AXES]
    margins = (HALO, -(-HALO // 8) * 8)
    span = [size + 2 * margin for size, margin in zip(brick, margins)] + [counts[2] * bz]
    whole = pl.BlockSpec(memory_space=pltpu.VMEM)
    dma = pltpu.SemaphoreType.DMA
    peers = max(counts[2] - 1, 1)
    zone_all_u, zone_all_w = pl.pallas_call(
        functools.partial(sweep_kernel, counts, brick, margins),
        out_shape=(
            jax.ShapeDtypeStruct((3, *span), F32),
            jax.ShapeDtypeStruct((4, *span), F32),
        ),
        in_specs=[pl.BlockSpec(memory_space=pltpu.HBM)] * 3,
        out_specs=(whole, whole),
        scratch_shapes=[
            pltpu.VMEM((4, bx + 2, by, bz), F32),
            *[pltpu.VMEM((3, bx + 2, by, bz), F32)] * (FSWEEPS - 1),
            pltpu.VMEM((FSWEEPS, 2, 4, bx, bz), F32),
            pltpu.VMEM((FSWEEPS, 2, 4, bx, bz), F32),
            pltpu.VMEM((2, 4, bx, by, bz), F32),
            *[pltpu.VMEM((2, 3, bx, by, bz), F32)] * (FSWEEPS - 1),
            pltpu.VMEM((6, bx, by, bz), F32),
            pltpu.VMEM((bx, by, bz), F32),
            dma((FSWEEPS, 4, len(FACES))),
            dma((FSWEEPS, 4, len(FACES))),
            dma((FSWEEPS + 3, len(AROUND))),
            dma((FSWEEPS + 3, len(AROUND))),
            dma((FSWEEPS + 3, len(AROUND) + 1, peers)),
            dma((FSWEEPS + 3, len(AROUND) + 1, peers)),
            dma((4,)),
        ],
        compiler_params=pltpu.CompilerParams(
            collective_id=0, has_side_effects=True, vmem_limit_bytes=40 * 1024 * 1024
        ),
        name="sweeps",
    )(*[pltpu.with_memory_space_constraint(each, pltpu.HBM) for each in (forcing, start_field, modulus)])
    zone_span = 2 * PC + 2
    zone_rows = -(-zone_span // 8) * 8
    size = -(-PC * PC // 8) * 8
    planes = PC // 2 + 3
    field, added = pl.pallas_call(
        functools.partial(zone_kernel, counts, brick, margins),
        out_shape=(
            jax.ShapeDtypeStruct(forcing.shape, F32),
            jax.ShapeDtypeStruct(tuple(span), F32),
        ),
        in_specs=[pl.BlockSpec(memory_space=pltpu.HBM), whole, whole],
        out_specs=(pl.BlockSpec(memory_space=pl.ANY), whole),
        scratch_shapes=[
            pltpu.VMEM((3, zone_span, zone_rows, 128), F32),
            pltpu.VMEM((3, zone_span, zone_rows, 128), F32),
            pltpu.VMEM((zone_span, zone_rows, 128), F32),
            pltpu.VMEM((3 * FIELDS, zone_rows, 128), F32),
            pltpu.VMEM((3 * FIELDS, size, 128), F32),
            pltpu.VMEM((128, 128), F32),
            pltpu.VMEM((3 * FIELDS, 16, 128), F32),
            pltpu.VMEM((len(BANDS), 16, 128), F32),
            pltpu.VMEM((128, 128), F32),
            pltpu.VMEM((2, planes, 128, 128), F32),
            pltpu.VMEM((2, planes, 128, 256), F32),
            pltpu.VMEM((2, planes, 128, 128), F32),
            pltpu.VMEM((2, planes, 128, 256), F32),
            pltpu.VMEM((128, 128), F32),
            pltpu.SMEM(corners.shape, jnp.int32),
            dma((2,)),
        ],
        compiler_params=pltpu.CompilerParams(vmem_limit_bytes=40 * 1024 * 1024),
        name="zone",
    )(pltpu.with_memory_space_constraint(corners, pltpu.HBM), zone_all_u, zone_all_w)
    updated = pl.pallas_call(
        functools.partial(gather_kernel, counts, brick, margins),
        out_shape=jax.ShapeDtypeStruct(brick, F32),
        in_specs=[whole, whole],
        out_specs=whole,
        scratch_shapes=[
            pltpu.VMEM((span[0], span[1], bz), F32),
            pltpu.VMEM((peers, span[0], span[1], bz), F32),
            pltpu.VMEM((2, HALO - 1, by, bz), F32),
            pltpu.VMEM((2, bx, HALO - 1, bz), F32),
            pltpu.VMEM((4, HALO - 1, HALO - 1, bz), F32),
            dma((len(AROUND),)),
            dma((len(AROUND),)),
            dma((peers,)),
            dma((peers,)),
        ],
        compiler_params=pltpu.CompilerParams(
            collective_id=1, has_side_effects=True, vmem_limit_bytes=40 * 1024 * 1024
        ),
        name="gather",
    )(added, modulus)
    return (field, updated)


def solution(mesh):
    placed = (
        P(None, "gx", "gy", "gz"),
        P(None, "gx", "gy", "gz"),
        P("gx", "gy", "gz"),
        P(("gx", "gy", "gz"), None),
    )
    return jax.shard_map(
        body,
        mesh=mesh,
        in_specs=placed,
        out_specs=(P(None, "gx", "gy", "gz"), P("gx", "gy", "gz")),
        check_vma=False,
    )
```
